32 devices in a mesh: groups: 2 (over y), ctx: 4 (over x, core), head: 4 (over z).
Axes of the slice: x: 2, y: 2, z: 4, core: 2. Of those that a mesh axis runs over, the one named last changes fastest.
Arguments:
- queries: bfloat16 [1536, 8, 5, 128], P(('groups', 'ctx'), 'head'), parts along dimension 0, may hold values from -6 to 6
- keys_values: bfloat16 [1536, 8, 2, 128], P(('groups', 'ctx'), 'head'), parts along dimension 0, may hold values from -6 to 6
- prior_state: bfloat16 [16, 8256, 128], P(('groups', 'head'), 'ctx'), parts along dimension 0, may hold values from -224 to 224
- counts: int32 [2], P('groups'), parts along dimension 0, may hold values from 384 to 1535
- continuation: int32 [64], P('groups'), parts along dimension 0, may hold values from 0 to 75967
- query_table: bfloat16 [75968, 8, 5, 128], P('ctx', 'head'), may hold values from -6 to 6
- pair_table: bfloat16 [75968, 8, 2, 128], P('ctx', 'head'), may hold values from -6 to 6
Outputs:
- readout: bfloat16 [1536, 8, 5, 128], P(('groups', 'ctx'), 'head'), parts along dimension 0
- decode_out: bfloat16 [64, 8, 5, 128], P(('groups', 'ctx'), 'head'), parts along dimension 0
- decode_state: float32 [16, 8256, 128], P(('groups', 'head'), 'ctx'), parts along dimension 0
The draws below stay inside these ranges and needn't reach their ends.
There are 2 independent parts, one for each index of `groups`. The reference program is written for one: setup_inputs(seed, part) draws one part's arguments, and reference() takes and returns one part's arrays. A program takes and returns all parts, laid end to end along the dimension named above; an argument that names none is the same for every part. Nothing has to cross between parts.
All inputs are finite; a program needn't handle non-finite values.
Results may differ from the reference program's by a relative error of at most 0.0048.
The reference program's roundings to bfloat16 on the way count: a program that leaves them out, or rounds other values in their place, can miss the bound.
Values may be sent and summed in bfloat16 or wider, within the bound.
A program may use at most 256 MiB of HBM per device.

```python
import math
import jax
import jax.numpy as jnp
import numpy as np
from jax import lax

HD = 128
KV = 8
G = 5
DX = 8256
TOK_DEV = 192
TOKENS = 768
STEPS = 32
VOCAB = 75968


def with_ends(values, key, smallest, high):
    dims = values.shape
    spot = [jax.random.randint(jax.random.fold_in(key, axis), (), 0, dims[axis]) for axis in range(len(dims))]
    values = values.at[tuple(spot)].set(smallest)
    longest = dims.index(max(dims))
    spot[longest] = (spot[longest] + 1) % dims[longest]
    return values.at[tuple(spot)].set(high)


def block_scale(rng, shape, cuts, smallest, largest):
    level, own = 1.0, jax.random.fold_in(rng, 6)
    for axis_at, shards_of in cuts:
        draws = jnp.exp(jax.random.uniform(jax.random.fold_in(own, axis_at), (shards_of,), jnp.float32, smallest / len(cuts), largest / len(cuts)))
        level = level * jnp.repeat(draws, shape[axis_at] // shards_of).reshape([-1 if axis == axis_at else 1 for axis in range(len(shape))])
    return level


def ranked_wide(own_key, shape, count, skew):
    loads = [min(1 << octave, count + 1 - (1 << octave)) * (1 << 20) // math.isqrt((1 << octave) ** skew) + 1 for octave in range((count + 1).bit_length()) if 1 << octave <= count]
    spread = 1 + sum(loads) // (1 << 30)
    grid = np.cumsum(np.array([max(1, weight // spread) for weight in loads]))
    pick = jax.random.randint(jax.random.fold_in(own_key, 1), shape, 0, int(grid[len(loads) - 1]))
    start = jnp.left_shift(1, jnp.searchsorted(jnp.asarray(grid, jnp.int32), pick, side="right").astype(jnp.int32))
    rank = start - 1 + jax.random.randint(jax.random.fold_in(own_key, 4), shape, 0, 1 << 30) % jnp.minimum(start, count + 1 - start)
    return jax.random.permutation(jax.random.fold_in(own_key, 2), count)[rank].astype(jnp.int32)


def centred(key, shape, scale, bound, shards=(), held_as=jnp.bfloat16):
    result = jax.random.normal(key, shape, jnp.float32) * scale
    if len(shards) > 0:
        result = block_scale(key, shape, shards, -0.22, 0.18) * result
    return jnp.clip(result, min=-bound, max=bound).astype(held_as)


def setup_inputs(seed: int = 0, part: int = 0) -> dict:
    keys = jax.random.split(jax.random.key(seed), 8)
    part_splits = jax.random.split(jax.random.fold_in(keys[7], part), 8)
    queries = centred(part_splits[0], (TOKENS, KV, G, HD), 1.0, 6.0, ((0, 4), (1, 4)))
    keys_values = centred(part_splits[1], (TOKENS, KV, 2, HD), 1.0, 6.0, ((0, 4), (1, 4)))
    prior_state = centred(part_splits[2], (KV, DX, HD), ((2 * TOKENS) ** 0.5), 224.0, ((0, 4), (1, 4)))
    counts = jax.random.randint(part_splits[3], (1,), TOKENS // 2, 2 * TOKENS).astype(jnp.int32)
    continuation = with_ends(ranked_wide(part_splits[4], (STEPS,), VOCAB, 2), jax.random.fold_in(part_splits[4], 3), 0, VOCAB - 1).astype(jnp.int32)
    query_table = centred(keys[5], (VOCAB, KV, G, HD), 1.0, 6.0, ((0, 4), (1, 4)))
    pair_table = centred(keys[6], (VOCAB, KV, 2, HD), 1.0, 6.0, ((0, 4), (1, 4)))
    return {"queries": queries, "keys_values": keys_values, "prior_state": prior_state, "counts": counts, "continuation": continuation, "query_table": query_table, "pair_table": pair_table}


ROOT_TWO = 2.0 ** 0.5
NUM_BLOCKS = 8

def expand_range(values, first_offset, how_many):
    width = values.shape[-1]
    doubled = jnp.concatenate([values, values], axis=-1)
    scaled = doubled * ROOT_TWO
    pieces = []
    for offset in range(first_offset, first_offset + how_many):
        partner = doubled if offset == 0 else scaled
        pieces.append(values * partner[..., offset:offset + width])
    return jnp.concatenate(pieces, axis=-1)

def expand_tail(values):
    half_width = values.shape[-1] // 2
    return values[..., :half_width] * (values[..., half_width:] * ROOT_TWO)

def feature_piece(values, number):
    head_size = values.shape[-1]
    if number == NUM_BLOCKS:
        return expand_tail(values)
    per_block = head_size // 2 // NUM_BLOCKS
    return expand_range(values, number * per_block, per_block)

def expand_all(values):
    return jnp.concatenate([feature_piece(values, number) for number in range(NUM_BLOCKS + 1)], axis=-1)

def causal_sum(query_rows, key_rows, value_rows):
    scores = jnp.einsum('tgd,sd->gts', query_rows.astype(jnp.float32), key_rows.astype(jnp.float32))
    allowed = jnp.arange(query_rows.shape[0], dtype=jnp.int32)[:, None] >= jnp.arange(key_rows.shape[0], dtype=jnp.int32)[None, :]
    weights = jnp.where(allowed[None], scores * scores / HD, 0.0).astype(jnp.bfloat16)
    return jnp.einsum('gts,sd->tgd', weights.astype(jnp.float32), value_rows.astype(jnp.float32))

def head_window(packed, start_count):
    head_queries, head_pairs, head_prior, step_queries, step_pairs = packed
    block_queries_all = head_queries.reshape(-1, TOK_DEV, G, HD)
    block_pairs_all = head_pairs.reshape(-1, TOK_DEV, 2, HD)
    block_count = block_queries_all.shape[0]

    def advance(running, block):
        block_queries, block_pairs, block_number = block
        phi_keys = expand_all(block_pairs[:, 0].astype(jnp.float32)).astype(jnp.bfloat16)
        phi_queries = expand_all(block_queries.astype(jnp.float32)).astype(jnp.bfloat16)
        carried = jnp.dot(phi_queries.reshape(-1, DX), running.astype(jnp.bfloat16), preferred_element_type=jnp.float32).reshape(TOK_DEV, G, HD)
        own_sum = causal_sum(block_queries, block_pairs[:, 0], block_pairs[:, 1])
        positions = start_count + block_number * TOK_DEV + jnp.arange(TOK_DEV, dtype=jnp.int32) + 1
        output = ((carried / HD + own_sum) / jnp.sqrt(positions.astype(jnp.float32))[:, None, None]).astype(jnp.bfloat16)
        running = running + jnp.dot(phi_keys.T, block_pairs[:, 1], preferred_element_type=jnp.float32)
        return (running, output)
    final_state, outputs = lax.scan(advance, head_prior.astype(jnp.float32), (block_queries_all, block_pairs_all, jnp.arange(block_count, dtype=jnp.int32)))
    readout = outputs.reshape(TOKENS, G, HD)
    step_phi_queries = expand_all(step_queries.astype(jnp.float32)).astype(jnp.bfloat16)
    step_carried = jnp.dot(step_phi_queries.reshape(-1, DX), final_state.astype(jnp.bfloat16), preferred_element_type=jnp.float32).reshape(STEPS, G, HD)
    step_own = causal_sum(step_queries, step_pairs[:, 0], step_pairs[:, 1])
    step_positions = start_count + TOKENS + jnp.arange(STEPS, dtype=jnp.int32) + 1
    decode_out = ((step_carried / HD + step_own) / jnp.sqrt(step_positions.astype(jnp.float32))[:, None, None]).astype(jnp.bfloat16)
    step_phi_keys = expand_all(step_pairs[:, 0].astype(jnp.float32)).astype(jnp.bfloat16)
    decode_state = final_state + jnp.dot(step_phi_keys.T, step_pairs[:, 1], preferred_element_type=jnp.float32)
    return (readout, decode_out, decode_state)

def reference(queries, keys_values, prior_state, counts, continuation, query_table, pair_table):
    step_queries = jnp.take(query_table, continuation, axis=0)
    step_pairs = jnp.take(pair_table, continuation, axis=0)
    start_count = counts[0]

    def per_head(packed):
        return head_window(packed, start_count)
    readout, decode_out, decode_state = lax.map(per_head, (jnp.swapaxes(queries, 0, 1), jnp.swapaxes(keys_values, 0, 1), prior_state, jnp.swapaxes(step_queries, 0, 1), jnp.swapaxes(step_pairs, 0, 1)))
    return (jnp.swapaxes(readout, 0, 1), jnp.swapaxes(decode_out, 0, 1), decode_state)
```

```python
import functools

import jax
import jax.numpy as jnp
from jax import lax
from jax.experimental import pallas as pl
from jax.experimental.pallas import tpu as pltpu
from jax.sharding import PartitionSpec as P


ROOT_TWO = 2.0**0.5
MESH = pl.DeviceIdType.MESH
TILE = 256
LANES = 128
CONTRACT_LAST = (((1,), (1,)), ((), ()))


def round_up(number, multiple):
    return (number + multiple - 1) // multiple * multiple


def pick_kernel(ids_ref, query_table, pair_table, query_out, pair_out, query_sem, pair_sem):
    vocab_rows = query_table.shape[0]
    first_row = lax.axis_index("ctx") * vocab_rows
    query_out[...] = jnp.zeros_like(query_out)
    pair_out[...] = jnp.zeros_like(pair_out)

    def each(step, act):
        row = ids_ref[step] - first_row

        @pl.when(jnp.logical_and(row >= 0, row < vocab_rows))
        def _():
            act(pltpu.make_async_copy(query_table.at[row], query_out.at[step], query_sem.at[step]))
            act(pltpu.make_async_copy(pair_table.at[row], pair_out.at[step], pair_sem.at[step]))

    for step in range(query_out.shape[0]):
        each(step, lambda copy: copy.start())
    for step in range(query_out.shape[0]):
        each(step, lambda copy: copy.wait())


def pick_rows(ids, query_table, pair_table):
    steps = ids.shape[0]
    return pl.pallas_call(
        pick_kernel,
        out_shape=(
            jax.ShapeDtypeStruct((steps,) + query_table.shape[1:], query_table.dtype),
            jax.ShapeDtypeStruct((steps,) + pair_table.shape[1:], pair_table.dtype),
        ),
        in_specs=[
            pl.BlockSpec(memory_space=pltpu.SMEM),
            pl.BlockSpec(memory_space=pl.ANY),
            pl.BlockSpec(memory_space=pl.ANY),
        ],
        out_specs=(
            pl.BlockSpec(memory_space=pltpu.VMEM),
            pl.BlockSpec(memory_space=pltpu.VMEM),
        ),
        scratch_shapes=[pltpu.SemaphoreType.DMA((steps,)), pltpu.SemaphoreType.DMA((steps,))],
        name="pick_rows",
    )(ids, query_table, pair_table)


def main_kernel(
    sizes,
    counts,
    queries,
    blob,
    prior,
    window_out,
    step_out,
    state_out,
    out,
    state,
    land_blob,
    land_prior,
    query_rows,
    query_plain,
    query_scaled,
    prior_turned,
    total_turned,
    step_rows,
    key_rows,
    value_rows,
    turned,
    blob_send,
    blob_recv,
    prior_send,
    prior_recv,
    local_sem,
):
    n, heads, group, tok_rows, step_count, rows_valid = sizes
    chips = n // 2
    per_shard = step_count // n
    window_rows = tok_rows * group
    window = n * tok_rows
    prior_rows = prior.shape[1]
    shifted = prior_rows == rows_valid
    state_rows = state.shape[1]
    blocks = land_prior.shape[2] // LANES
    row_tiles = out.shape[1] // TILE
    padded_keys = key_rows.shape[1]
    me = lax.axis_index("ctx")
    core = lax.rem(me, 2)
    partner = me + 1 - 2 * core

    def across(step):
        return lax.rem(me + 2 * step, n)

    def twin(index):
        return index + 1 - 2 * lax.rem(index, 2)

    barrier = pltpu.get_barrier_semaphore()
    pl.semaphore_signal(barrier, inc=1, device_id={"ctx": partner}, device_id_type=MESH)
    for step in range(1, chips):
        pl.semaphore_signal(barrier, inc=1, device_id={"ctx": across(step)}, device_id_type=MESH)
    pl.semaphore_wait(barrier, chips)

    def blob_copy(src, source, slot, target):
        return pltpu.make_async_remote_copy(
            src_ref=src,
            dst_ref=land_blob.at[source],
            send_sem=blob_send.at[slot],
            recv_sem=blob_recv.at[source],
            device_id={"ctx": target},
            device_id_type=MESH,
        )

    def landing(source):
        first = pl.multiple_of(lax.rem(source * rows_valid, LANES), 16) if shifted else 0
        return pl.ds(first, prior_rows)

    def prior_copy(src, source, head, slot, target):
        return pltpu.make_async_remote_copy(
            src_ref=src,
            dst_ref=land_prior.at[source, head, landing(source)],
            send_sem=prior_send.at[slot, head],
            recv_sem=prior_recv.at[source, head],
            device_id={"ctx": target},
            device_id_type=MESH,
        )

    def blob_own(slot):
        return blob_copy(blob, me, slot, partner if slot == 0 else across(slot))

    def blob_forward(step):
        source = across(step)
        return blob_copy(land_blob.at[source], source, chips - 1 + step, partner)

    def prior_own(slot, head):
        target = partner if slot == 0 else across(slot)
        return prior_copy(prior.at[head], me, head, slot, target)

    def prior_forward(step, head):
        source = across(step)
        return prior_copy(
            land_prior.at[source, head, landing(source)],
            source,
            head,
            chips - 1 + step,
            partner,
        )

    for slot in list(range(1, chips)) + [0]:
        blob_own(slot).start()
    for head in range(heads):
        for slot in list(range(1, chips)) + [0]:
            prior_own(slot, head).start()
    own_blob = pltpu.make_async_copy(blob, land_blob.at[me], local_sem.at[0])
    own_prior = pltpu.make_async_copy(
        prior, land_prior.at[me, :, landing(me)], local_sem.at[1]
    )
    own_blob.start()
    own_prior.start()

    if shifted:
        for source in range(n):
            lead_rows = source * rows_valid % LANES
            for first, last in (
                (0, lead_rows),
                (lead_rows + prior_rows, blocks * LANES),
            ):
                if last > first:
                    for head in range(heads):
                        land_prior[source, head, pl.ds(first, last - first), :] = jnp.zeros(
                            (last - first, LANES), jnp.bfloat16
                        )
    total_turned[...] = jnp.zeros_like(total_turned)
    for head in range(heads):
        query_rows[head, pl.ds(0, window_rows), :] = queries[head]
        query_rows[head, pl.ds(window_rows, out.shape[1] - window_rows), :] = jnp.zeros(
            (out.shape[1] - window_rows, LANES), jnp.bfloat16
        )
        spare = padded_keys - window - step_count
        if spare > 0:
            key_rows[head, pl.ds(window + step_count, spare), :] = jnp.zeros(
                (spare, LANES), jnp.bfloat16
            )
            value_rows[head, pl.ds(window + step_count, spare), :] = jnp.zeros(
                (spare, LANES), jnp.bfloat16
            )

    def place(source):
        first = source * rows_valid
        return lax.div(first, LANES), lax.rem(first, LANES)

    identity = (
        lax.broadcasted_iota(jnp.int32, (LANES, LANES), 0)
        == lax.broadcasted_iota(jnp.int32, (LANES, LANES), 1)
    ).astype(jnp.bfloat16)
    contract_last = (((1,), (1,)), ((), ()))

    def transposed(rows):
        return lax.dot_general(identity, rows, contract_last, preferred_element_type=jnp.float32)

    chunks_per_tile = TILE // LANES

    def turn_queries(head, first_tile, last_tile):
        for chunk in range(first_tile * chunks_per_tile, last_tile * chunks_per_tile):
            piece = transposed(query_rows[head, pl.ds(chunk * LANES, LANES), :])
            scaled = piece * ROOT_TWO
            query_plain[head, chunk] = piece
            query_scaled[head, chunk, pl.ds(0, LANES), :] = scaled
            query_scaled[head, chunk, pl.ds(LANES, LANES), :] = scaled

    def carry_tile(source, head, tile):
        first_offset, _ = place(source)
        columns = []
        for side in range(chunks_per_tile):
            chunk = tile * chunks_per_tile + side
            here = query_plain[head, chunk]
            pieces = []
            for block in range(blocks):
                row = lax.rem(first_offset + block, LANES)
                other = query_scaled[head, chunk, pl.ds(row, LANES), :]
                if block == 0:
                    other = jnp.where(first_offset == 0, here, other)
                pieces.append((here * other).astype(jnp.bfloat16))
            columns.append(jnp.concatenate(pieces, axis=0))
        features = jnp.concatenate(columns, axis=1)
        total_turned[head, tile] += jnp.dot(
            prior_turned[...], features, preferred_element_type=jnp.float32
        )

    def carry(source, head, first_tile, last_tile):
        prior_turned[...] = transposed(land_prior[source, head]).astype(jnp.bfloat16)

        @pl.loop(first_tile, last_tile)
        def _(tile):
            carry_tile(source, head, tile)

    full_tiles = window_rows // TILE
    own_prior.wait()
    for head in range(heads):
        turn_queries(head, 0, full_tiles)
        carry(me, head, 0, full_tiles)

    own_blob.wait()
    blob_copy(blob, partner, 0, partner).wait_recv()
    for step in range(1, chips):
        blob_copy(blob, across(step), 0, partner).wait_recv()
        blob_forward(step).start()
    for step in range(1, chips):
        blob_copy(blob, twin(across(step)), 0, partner).wait_recv()

    for head in range(heads):
        for source in range(n):
            key_rows[head, pl.ds(source * tok_rows, tok_rows), :] = land_blob[
                source, head, pl.ds(0, tok_rows), :
            ]
            value_rows[head, pl.ds(source * tok_rows, tok_rows), :] = land_blob[
                source, heads + head, pl.ds(0, tok_rows), :
            ]

        def picked(plane, first, count):
            total = land_blob[0, plane, pl.ds(first, count), :].astype(jnp.float32)
            for source in range(1, n):
                total += land_blob[source, plane, pl.ds(first, count), :].astype(jnp.float32)
            return total

        key_rows[head, pl.ds(window, step_count), :] = picked(head, tok_rows, step_count).astype(
            jnp.bfloat16
        )
        value_rows[head, pl.ds(window, step_count), :] = picked(
            heads + head, tok_rows, step_count
        ).astype(jnp.bfloat16)
        half = step_count * group // 2
        for side in range(2):
            step_rows[head, pl.ds(side * half, half), :] = picked(
                2 * head + side, tok_rows + step_count, half
            )
        own_steps = per_shard * group
        own_rows = step_rows[head, pl.ds(me * own_steps, own_steps), :]
        query_rows[head, pl.ds(window_rows, own_steps), :] = own_rows.astype(jnp.bfloat16)
        turn_queries(head, full_tiles, row_tiles)

    for head in range(heads):
        carry(me, head, full_tiles, row_tiles)
        prior_copy(prior.at[head], partner, head, 0, partner).wait_recv()
        carry(partner, head, 0, row_tiles)

    def state_copy(head):
        return pltpu.make_async_copy(state.at[head], state_out.at[head], local_sem.at[2 + head])

    def positions(tile):
        local = tile * TILE + lax.broadcasted_iota(jnp.int32, (TILE, 1), 0)
        return jnp.where(
            local < window_rows,
            local + me * window_rows,
            local - window_rows + window * group + me * (per_shard * group),
        )

    first_offset, lead = place(me)
    for head in range(heads):
        keys_turned = transposed(key_rows[head])
        chunks = padded_keys // LANES
        for chunk in range(chunks):
            piece = keys_turned[:, chunk * LANES : (chunk + 1) * LANES]
            turned[head, chunk, pl.ds(0, LANES), :] = piece
            turned[head, chunk, pl.ds(LANES, LANES), :] = piece

        def state_block(block):
            row = lax.broadcasted_iota(jnp.int32, (LANES, LANES), 0)
            early = row < LANES - lead
            plain = jnp.logical_and(early, first_offset + block == 0)
            factor = jnp.where(plain, 1.0, ROOT_TWO)
            near_row = lax.rem(lead + first_offset + block, LANES)
            far_row = lax.rem(lead + first_offset + block + 1, LANES)
            pieces = []
            for chunk in range(chunks):
                here = turned[head, chunk, pl.ds(lead, LANES), :]
                near = turned[head, chunk, pl.ds(near_row, LANES), :]
                far = turned[head, chunk, pl.ds(far_row, LANES), :]
                both = jnp.where(early, near, far) * factor
                pieces.append((here * both).astype(jnp.bfloat16))
            features = jnp.concatenate(pieces, axis=1)
            return jnp.dot(features, value_rows[head], preferred_element_type=jnp.float32)

        def before(rows):
            return prior[head, rows, :].astype(jnp.float32) if shifted else 0.0

        whole_blocks = state_rows // LANES

        @pl.loop(0, whole_blocks)
        def _(block):
            rows = pl.ds(pl.multiple_of(block * LANES, LANES), LANES)
            state[head, rows, :] = before(rows) + state_block(block)

        rest = state_rows - whole_blocks * LANES
        if rest > 0:
            rows = pl.ds(whole_blocks * LANES, rest)
            state[head, rows, :] = before(rows) + state_block(whole_blocks)[:rest]
        state_copy(head).start()

        @pl.loop(0, row_tiles)
        def _(tile):
            rows = pl.ds(pl.multiple_of(tile * TILE, TILE), TILE)
            scores = lax.dot_general(
                query_rows[head, rows, :],
                key_rows[head],
                contract_last,
                preferred_element_type=jnp.float32,
            )
            position = positions(tile)
            key_index = lax.broadcasted_iota(jnp.int32, scores.shape, 1)
            allowed = position >= key_index * group
            weights = jnp.where(allowed, scores * scores, 0.0).astype(jnp.bfloat16)
            out[head, rows, :] = jnp.dot(
                weights, value_rows[head], preferred_element_type=jnp.float32
            )

    for step in range(1, chips):
        source = across(step)
        for head in range(heads):
            prior_copy(prior.at[head], source, head, 0, partner).wait_recv()
            prior_forward(step, head).start()
            carry(source, head, 0, row_tiles)
            prior_copy(prior.at[head], twin(source), head, 0, partner).wait_recv()
            carry(twin(source), head, 0, row_tiles)

    for head in range(heads):
        for tile in range(row_tiles):
            first = tile * TILE
            token = jnp.floor((positions(tile).astype(jnp.float32) + 0.5) / group)
            place_in_prompt = token + (counts[0] + 1).astype(jnp.float32)
            scale = 1.0 / (LANES * jnp.sqrt(place_in_prompt))
            total = out[head, pl.ds(first, TILE), :] + total_turned[head, tile].T
            total = (total * scale).astype(jnp.bfloat16)
            split = min(max(window_rows - first, 0), TILE)
            if split > 0:
                window_out[head, pl.ds(first, split), :] = total[:split]
            if split < TILE:
                step_out[head, pl.ds(first + split - window_rows, TILE - split), :] = total[split:]
        state_copy(head).wait()

    for slot in range(chips):
        blob_own(slot).wait_send()
        for head in range(heads):
            prior_own(slot, head).wait_send()
    for step in range(1, chips):
        blob_forward(step).wait_send()
        for head in range(heads):
            prior_forward(step, head).wait_send()


def combine(sizes, counts, queries, blob, prior, out_rows):
    n, heads, group, tok_rows, step_count, rows_valid = sizes
    window_rows = tok_rows * group
    lead = max(source * rows_valid % LANES for source in range(n))
    padded_rows = round_up(lead + rows_valid, LANES)
    chunks = out_rows // LANES
    state_rows = round_up(rows_valid, 8)
    padded_keys = round_up(n * tok_rows + step_count, LANES)
    slots = 2 * (n // 2) - 1
    vmem = pl.BlockSpec(memory_space=pltpu.VMEM)
    return pl.pallas_call(
        functools.partial(main_kernel, sizes),
        out_shape=(
            jax.ShapeDtypeStruct((heads, window_rows, LANES), jnp.bfloat16),
            jax.ShapeDtypeStruct((heads, out_rows - window_rows, LANES), jnp.bfloat16),
            jax.ShapeDtypeStruct((heads, state_rows, LANES), jnp.float32),
        ),
        in_specs=[pl.BlockSpec(memory_space=pltpu.SMEM)] + [vmem] * 3,
        out_specs=(vmem, vmem, pl.BlockSpec(memory_space=pl.ANY)),
        scratch_shapes=[
            pltpu.VMEM((heads, out_rows, LANES), jnp.float32),
            pltpu.VMEM((heads, state_rows, LANES), jnp.float32),
            pltpu.VMEM((n,) + blob.shape, jnp.bfloat16),
            pltpu.VMEM((n, heads, padded_rows, LANES), jnp.bfloat16),
            pltpu.VMEM((heads, out_rows, LANES), jnp.bfloat16),
            pltpu.VMEM((heads, chunks, LANES, LANES), jnp.float32),
            pltpu.VMEM((heads, chunks, 2 * LANES, LANES), jnp.float32),
            pltpu.VMEM((LANES, padded_rows), jnp.bfloat16),
            pltpu.VMEM((heads, out_rows // TILE, LANES, TILE), jnp.float32),
            pltpu.VMEM((heads, step_count * group, LANES), jnp.float32),
            pltpu.VMEM((heads, padded_keys, LANES), jnp.bfloat16),
            pltpu.VMEM((heads, padded_keys, LANES), jnp.bfloat16),
            pltpu.VMEM((heads, padded_keys // LANES, 2 * LANES, LANES), jnp.float32),
            pltpu.SemaphoreType.DMA((slots,)),
            pltpu.SemaphoreType.DMA((n,)),
            pltpu.SemaphoreType.DMA((slots, heads)),
            pltpu.SemaphoreType.DMA((n, heads)),
            pltpu.SemaphoreType.DMA((2 + heads,)),
        ],
        compiler_params=pltpu.CompilerParams(
            collective_id=0, has_side_effects=True, vmem_limit_bytes=56 * 2**20
        ),
        name="combine",
    )(counts, queries, blob, prior)


def on_device_gather(queries, keys_values, prior_state, counts, continuation, query_table, pair_table):
    tok_rows, heads, group, head_size = queries.shape
    n = lax.axis_size("ctx")
    shard_index = lax.axis_index("ctx")
    step_count = continuation.shape[0]
    per_shard = step_count // n
    rows_valid = prior_state.shape[1]

    query_pick, pair_pick = pick_rows(
        continuation, query_table.transpose(0, 2, 1, 3), pair_table
    )

    window_planes = keys_values.transpose(2, 1, 0, 3).reshape(2 * heads, tok_rows, head_size)
    step_planes = pair_pick.transpose(2, 1, 0, 3)
    step_planes = step_planes.reshape(2 * heads, step_count, head_size)
    query_planes = query_pick.transpose(2, 0, 1, 3).reshape(
        2 * heads, step_count * group // 2, head_size
    )
    blob = jnp.concatenate([window_planes, step_planes, query_planes], axis=1)
    query_planes = queries.transpose(1, 0, 2, 3).reshape(heads, tok_rows * group, head_size)
    prior = prior_state
    if rows_valid % 16 != 0:
        leads = [source * rows_valid % LANES for source in range(n)]
        prior = lax.dynamic_update_slice(
            jnp.zeros((heads, round_up(max(leads) + rows_valid, LANES), LANES), prior.dtype),
            prior_state,
            (0, shard_index * rows_valid % LANES, 0),
        )
    out_rows = round_up((tok_rows + per_shard) * group, TILE)
    sizes = (n, heads, group, tok_rows, step_count, rows_valid)
    window_out, step_out, state = combine(sizes, counts, query_planes, blob, prior, out_rows)

    decode_state = state
    if rows_valid % 16 != 0:
        decode_state = prior_state.astype(jnp.float32) + state[:, :rows_valid]
    readout = window_out.reshape(heads, tok_rows, group, head_size).transpose(1, 0, 2, 3)
    decode_out = step_out[:, : per_shard * group]
    decode_out = decode_out.reshape(heads, per_shard, group, head_size).transpose(1, 0, 2, 3)
    return (readout, decode_out, decode_state)


def identity():
    row = lax.broadcasted_iota(jnp.int32, (LANES, LANES), 0)
    column = lax.broadcasted_iota(jnp.int32, (LANES, LANES), 1)
    return (row == column).astype(jnp.bfloat16)


def turned_rows(rows):
    return lax.dot_general(
        identity(), rows, CONTRACT_LAST, preferred_element_type=jnp.float32
    )


def turn_queries(load, count, plain, scaled):
    for chunk in range(count // LANES):
        piece = turned_rows(load(chunk * LANES))
        twice = piece * ROOT_TWO
        plain[chunk] = piece
        scaled[chunk, pl.ds(0, LANES), :] = twice
        scaled[chunk, pl.ds(LANES, LANES), :] = twice


def carry_tile(state_turned, first_offset, plain, scaled, tile):
    blocks = state_turned.shape[1] // LANES
    columns = []
    for side in range(TILE // LANES):
        chunk = tile * (TILE // LANES) + side
        here = plain[chunk]
        pieces = []
        for block in range(blocks):
            other = scaled[chunk, pl.ds(first_offset + block, LANES), :]
            if block == 0:
                other = jnp.where(first_offset == 0, here, other)
            pieces.append((here * other).astype(jnp.bfloat16))
        columns.append(jnp.concatenate(pieces, axis=0))
    features = jnp.concatenate(columns, axis=1)
    return jnp.dot(state_turned[...], features, preferred_element_type=jnp.float32).T


def chip_place(rows_valid):
    first = lax.div(lax.axis_index("ctx"), 2) * (2 * rows_valid)
    return lax.div(first, LANES), pl.multiple_of(lax.rem(first, LANES), 16)


def early_kernel(rows_valid, queries, own, other, turned, local, rows, plain, scaled):
    heads, padded = turned.shape[0], turned.shape[2]
    first_offset, lead = chip_place(rows_valid)
    core = lax.rem(lax.axis_index("ctx"), 2)
    count = local.shape[1]
    for head in range(heads):
        rows[pl.ds(0, LANES), :] = jnp.zeros((LANES, LANES), rows.dtype)
        spare = padded - 2 * rows_valid
        rows[pl.ds(padded - spare, spare), :] = jnp.zeros((spare, LANES), rows.dtype)
        for source, index in ((own, core), (other, 1 - core)):
            start = pl.multiple_of(lead + index * rows_valid, 16)
            rows[pl.ds(start, rows_valid), :] = source[head]
        for first in range(0, padded, 2 * LANES):
            size = min(2 * LANES, padded - first)
            turned[head, :, pl.ds(first, size)] = turned_rows(
                rows[pl.ds(first, size), :]
            ).astype(turned.dtype)
        turn_queries(
            lambda at: queries[head, pl.ds(at, LANES), :], count, plain, scaled
        )
        for tile in range(count // TILE):
            local[head, pl.ds(tile * TILE, TILE), :] = carry_tile(
                turned.at[head], first_offset, plain, scaled, tile
            )


def remote_kernel(rows_valid, queries, turned, partial, plain, scaled):
    first_offset, _ = chip_place(rows_valid)
    count = partial.shape[1]
    for head in range(turned.shape[0]):
        turn_queries(
            lambda at: queries[head, pl.ds(at, LANES), :], count, plain, scaled
        )
        for tile in range(count // TILE):
            partial[head, pl.ds(tile * TILE, TILE), :] = carry_tile(
                turned.at[head], first_offset, plain, scaled, tile
            ).astype(partial.dtype)


def fill_tail(head, queries, steps, first, tail):
    window = queries.shape[1] - first
    count = steps.shape[1]
    tail[...] = jnp.zeros_like(tail)
    tail[pl.ds(0, window), :] = queries[head, pl.ds(first, window), :]
    tail[pl.ds(window, count), :] = steps[head]


def remote_tail_kernel(rows_valid, first, queries, steps, turned, partial, tail, plain, scaled):
    first_offset, _ = chip_place(rows_valid)
    for head in range(turned.shape[0]):
        fill_tail(head, queries, steps, first, tail)
        turn_queries(lambda at: tail[pl.ds(at, LANES), :], TILE, plain, scaled)
        rows = carry_tile(turned.at[head], first_offset, plain, scaled, 0)
        partial[head] = rows[: partial.shape[1]].astype(partial.dtype)


def late_kernel(
    sizes,
    queries,
    steps,
    turned,
    local,
    own_pairs,
    twin_pairs,
    across_pairs,
    far_pairs,
    step_pairs,
    prior,
    result,
    state_out,
    tail,
    plain,
    scaled,
    key_rows,
    value_rows,
    keys_plain,
    keys_scaled,
    delta,
    state,
    state_sem,
):
    n, heads, group, tok_rows, step_count, rows_valid = sizes
    first_offset, _ = chip_place(rows_valid)
    me = lax.axis_index("ctx")
    twin = me + 1 - 2 * lax.rem(me, 2)
    window = n * tok_rows
    window_rows = tok_rows * group
    per_shard = step_count // n
    first_tail = local.shape[1]
    padded_keys = key_rows.shape[1]
    chunks = padded_keys // LANES
    blocks = delta.shape[0] // LANES
    my_first = me * rows_valid
    my_offset = lax.div(my_first, LANES)
    my_lead = pl.multiple_of(lax.rem(my_first, LANES), 8)
    places = (
        (own_pairs, me),
        (twin_pairs, twin),
        (across_pairs, lax.rem(me + 2, n)),
        (far_pairs, lax.rem(twin + 2, n)),
    )

    def state_copy(head):
        return pltpu.make_async_copy(state.at[head], state_out.at[head], state_sem.at[head])

    for head in range(heads):
        for plane, target in ((0, key_rows), (1, value_rows)):
            for pairs, source in places:
                start = pl.multiple_of(source * tok_rows, 16)
                target[head, pl.ds(start, tok_rows), :] = pairs[plane, head]
            target[head, pl.ds(window, step_count), :] = step_pairs[plane, head]
            spare = padded_keys - window - step_count
            if spare > 0:
                target[head, pl.ds(window + step_count, spare), :] = jnp.zeros(
                    (spare, LANES), target.dtype
                )
        for chunk in range(chunks):
            piece = turned_rows(key_rows[head, pl.ds(chunk * LANES, LANES), :])
            twice = piece * ROOT_TWO
            keys_plain[chunk] = piece
            keys_scaled[chunk, pl.ds(0, LANES), :] = twice
            keys_scaled[chunk, pl.ds(LANES, LANES), :] = twice

        def key_features(block, maybe_plain):
            pieces = []
            for chunk in range(chunks):
                here = keys_plain[chunk]
                other = keys_scaled[chunk, pl.ds(my_offset + block, LANES), :]
                if maybe_plain:
                    other = jnp.where(my_offset == 0, here, other)
                pieces.append((here * other).astype(jnp.bfloat16))
            return jnp.concatenate(pieces, axis=1)

        def add_block(features, first):
            delta[pl.ds(first, features.shape[0]), :] = jnp.dot(
                features, value_rows[head], preferred_element_type=jnp.float32
            )

        odd = 1 if blocks % 2 else 2
        for block in range(odd):
            add_block(key_features(block, block == 0), block * LANES)

        @pl.loop(0, (blocks - odd) // 2)
        def _(pair):
            block = odd + 2 * pair
            both = jnp.concatenate(
                [key_features(block, False), key_features(block + 1, False)], axis=0
            )
            add_block(both, pl.multiple_of(block * LANES, LANES))

        state[head] = prior[head].astype(jnp.float32) + delta[pl.ds(my_lead, rows_valid), :]
        state_copy(head).start()

    for head in range(heads):
        fill_tail(head, queries, steps, first_tail, tail)
        turn_queries(lambda at: tail[pl.ds(at, LANES), :], TILE, plain, scaled)
        carried_tail = carry_tile(turned.at[head], first_offset, plain, scaled, 0)
        for first in range(0, result.shape[1], TILE):
            last = first >= first_tail
            rows = tail[...] if last else queries[head, pl.ds(first, TILE), :]
            scores = lax.dot_general(
                rows, key_rows[head], CONTRACT_LAST, preferred_element_type=jnp.float32
            )
            at = first + lax.broadcasted_iota(jnp.int32, (TILE, 1), 0)
            position = jnp.where(
                at < window_rows,
                at + me * window_rows,
                at - window_rows + window * group + me * (per_shard * group),
            )
            key_index = lax.broadcasted_iota(jnp.int32, scores.shape, 1)
            weights = jnp.where(position >= key_index * group, scores * scores, 0.0)
            total = jnp.dot(
                weights.astype(jnp.bfloat16), value_rows[head], preferred_element_type=jnp.float32
            )
            carried = carried_tail if last else local[head, pl.ds(first, TILE), :]
            size = min(TILE, result.shape[1] - first)
            result[head, pl.ds(first, size), :] = (total + carried)[:size]
    for head in range(heads):
        state_copy(head).wait()


def vmem_call(kernel, out_shape, operands, scratch, limit, out_specs=None):
    vmem = pl.BlockSpec(memory_space=pltpu.VMEM)
    return pl.pallas_call(
        kernel,
        out_shape=out_shape,
        in_specs=[vmem] * len(operands),
        out_specs=out_specs if out_specs is not None else jax.tree.map(lambda _: vmem, out_shape),
        scratch_shapes=scratch,
        compiler_params=pltpu.CompilerParams(vmem_limit_bytes=limit * 2**20),
    )(*operands)


def turn_scratch(columns):
    chunks = columns // LANES
    return [
        pltpu.VMEM((chunks, LANES, LANES), jnp.float32),
        pltpu.VMEM((chunks, 2 * LANES, LANES), jnp.float32),
    ]


def on_device_exchange(
    queries, keys_values, prior, counts, continuation, query_table, pair_table
):
    tok_rows, heads, group, head_size = queries.shape
    n = lax.axis_size("ctx")
    me = lax.axis_index("ctx")
    core, chip = lax.rem(me, 2), lax.div(me, 2)
    step_count = continuation.shape[0]
    per_shard = step_count // n
    step_rows = per_shard * group
    rows_valid = prior.shape[1]
    window_rows = tok_rows * group
    early = window_rows // TILE * TILE
    rows_chip = 2 * rows_valid
    padded = max(
        round_up(chip_at * rows_chip % LANES + rows_chip, LANES) for chip_at in range(n // 2)
    )
    blocks = max(
        round_up(source * rows_valid % LANES + rows_valid, LANES) // LANES for source in range(n)
    )
    padded_keys = round_up(n * tok_rows + step_count, LANES)
    bf16, f32 = jnp.bfloat16, jnp.float32
    shape = jax.ShapeDtypeStruct

    def swap_across(value):
        return lax.ppermute(value, "ctx", [(i, (i + 2) % n) for i in range(n)])

    def swap_twin(value):
        return lax.ppermute(value, "ctx", [(i, i ^ 1) for i in range(n)])

    def query_planes(value):
        return value.transpose(1, 0, 2, 3).reshape(heads, -1, head_size)

    def pair_planes(value):
        return value.transpose(2, 1, 0, 3)

    across_queries = swap_across(queries)
    across_pairs = swap_across(keys_values)
    twin_prior = swap_twin(prior)
    twin_pairs = swap_twin(keys_values)
    query_pick, pair_pick = pick_rows(
        continuation, query_table.transpose(0, 2, 1, 3), pair_table
    )
    query_chip = query_pick + swap_twin(query_pick)
    pair_chip = pair_pick + swap_twin(pair_pick)
    mine = [
        lax.dynamic_slice_in_dim(query_chip, (core + 2 * at) * per_shard, per_shard)
        for at in range(n // 2)
    ]
    send = jnp.concatenate(
        [part.reshape(step_rows, heads, head_size) for part in mine]
        + [pair_chip.reshape(step_count * heads, 2, head_size)]
    )
    steps = send + swap_across(send)
    step_pairs = pair_planes(steps[n // 2 * step_rows :].reshape(step_count, heads, 2, head_size))
    step_queries = steps[: n // 2 * step_rows].transpose(1, 0, 2)
    own_steps = lax.dynamic_slice_in_dim(step_queries, chip * step_rows, step_rows, 1)
    across_steps = lax.dynamic_slice_in_dim(step_queries, (1 - chip) * step_rows, step_rows, 1)

    own_rows = query_planes(queries)
    turned, local = vmem_call(
        functools.partial(early_kernel, rows_valid),
        (shape((heads, LANES, padded), bf16), shape((heads, early, LANES), f32)),
        (own_rows, prior, twin_prior),
        [pltpu.VMEM((padded, LANES), bf16)] + turn_scratch(early),
        16,
    )
    across_rows = query_planes(across_queries)
    partial = vmem_call(
        functools.partial(remote_kernel, rows_valid),
        shape((heads, early, LANES), bf16),
        (across_rows, turned),
        turn_scratch(early),
        16,
    )
    got = swap_across(partial)
    partial_tail = vmem_call(
        functools.partial(remote_tail_kernel, rows_valid, early),
        shape((heads, window_rows - early + step_rows, LANES), bf16),
        (across_rows, across_steps, turned),
        [pltpu.VMEM((TILE, LANES), bf16)] + turn_scratch(TILE),
        16,
    )
    got_tail = swap_across(partial_tail)
    far_pairs = swap_twin(across_pairs)
    sizes = (n, heads, group, tok_rows, step_count, rows_valid)
    vmem = pl.BlockSpec(memory_space=pltpu.VMEM)
    chunks = padded_keys // LANES
    result, decode_state = vmem_call(
        functools.partial(late_kernel, sizes),
        (
            shape((heads, window_rows + step_rows, LANES), f32),
            shape((heads, rows_valid, LANES), f32),
        ),
        (
            own_rows,
            own_steps,
            turned,
            local,
            pair_planes(keys_values),
            pair_planes(twin_pairs),
            pair_planes(across_pairs),
            pair_planes(far_pairs),
            step_pairs,
            prior,
        ),
        [pltpu.VMEM((TILE, LANES), bf16)]
        + turn_scratch(TILE)
        + [
            pltpu.VMEM((heads, padded_keys, LANES), bf16),
            pltpu.VMEM((heads, padded_keys, LANES), bf16),
            pltpu.VMEM((chunks, LANES, LANES), f32),
            pltpu.VMEM((chunks, 2 * LANES, LANES), f32),
            pltpu.VMEM((blocks * LANES, LANES), f32),
            pltpu.VMEM((heads, rows_valid, LANES), f32),
            pltpu.SemaphoreType.DMA((heads,)),
        ],
        24,
        (vmem, pl.BlockSpec(memory_space=pl.ANY)),
    )
    window_at = counts[0] + 1 + me * tok_rows + jnp.arange(window_rows, dtype=jnp.int32) // group
    steps_at = counts[0] + 1 + n * tok_rows + me * per_shard
    steps_at = steps_at + jnp.arange(step_rows, dtype=jnp.int32) // group
    scale = 1.0 / (head_size * jnp.sqrt(jnp.concatenate([window_at, steps_at]).astype(f32)))
    total = result + jnp.concatenate([got, got_tail], axis=1).astype(f32)
    total = (total * scale[None, :, None]).astype(bf16)
    readout = total[:, :window_rows].reshape(heads, tok_rows, group, head_size)
    decode_out = total[:, window_rows:].reshape(heads, per_shard, group, head_size)
    return (readout.transpose(1, 0, 2, 3), decode_out.transpose(1, 0, 2, 3), decode_state)


def solution(mesh):
    in_specs = (
        P(("groups", "ctx"), "head", None, None),
        P(("groups", "ctx"), "head", None, None),
        P(("groups", "head"), "ctx", None),
        P("groups"),
        P("groups"),
        P("ctx", "head", None, None),
        P("ctx", "head", None, None),
    )
    out_specs = (
        P(("groups", "ctx"), "head", None, None),
        P(("groups", "ctx"), "head", None, None),
        P(("groups", "head"), "ctx", None),
    )

    def on_device(*arguments):
        n, rows_valid = lax.axis_size("ctx"), arguments[2].shape[1]
        if n == 4 and rows_valid % 16 == 0:
            return on_device_exchange(*arguments)
        return on_device_gather(*arguments)

    return jax.shard_map(
        on_device, mesh=mesh, in_specs=in_specs, out_specs=out_specs, check_vma=False
    )
```

```python
import functools

import jax
import jax.numpy as jnp
from jax import lax
from jax.experimental import pallas as pl
from jax.experimental.pallas import tpu as pltpu
from jax.sharding import PartitionSpec as P


ROOT_TWO = 2.0**0.5
MESH = pl.DeviceIdType.MESH
TILE = 256
LANES = 128
CONTRACT_LAST = (((1,), (1,)), ((), ()))


def round_up(number, multiple):
    return (number + multiple - 1) // multiple * multiple


def pick_kernel(ids_ref, query_table, pair_table, query_out, pair_out, query_sem, pair_sem):
    vocab_rows = query_table.shape[0]
    first_row = lax.axis_index("ctx") * vocab_rows
    query_out[...] = jnp.zeros_like(query_out)
    pair_out[...] = jnp.zeros_like(pair_out)

    def each(step, act):
        row = ids_ref[step] - first_row

        @pl.when(jnp.logical_and(row >= 0, row < vocab_rows))
        def _():
            act(pltpu.make_async_copy(query_table.at[row], query_out.at[step], query_sem.at[step]))
            act(pltpu.make_async_copy(pair_table.at[row], pair_out.at[step], pair_sem.at[step]))

    for step in range(query_out.shape[0]):
        each(step, lambda copy: copy.start())
    for step in range(query_out.shape[0]):
        each(step, lambda copy: copy.wait())


def pick_rows(ids, query_table, pair_table):
    steps = ids.shape[0]
    return pl.pallas_call(
        pick_kernel,
        out_shape=(
            jax.ShapeDtypeStruct((steps,) + query_table.shape[1:], query_table.dtype),
            jax.ShapeDtypeStruct((steps,) + pair_table.shape[1:], pair_table.dtype),
        ),
        in_specs=[
            pl.BlockSpec(memory_space=pltpu.SMEM),
            pl.BlockSpec(memory_space=pl.ANY),
            pl.BlockSpec(memory_space=pl.ANY),
        ],
        out_specs=(
            pl.BlockSpec(memory_space=pltpu.VMEM),
            pl.BlockSpec(memory_space=pltpu.VMEM),
        ),
        scratch_shapes=[pltpu.SemaphoreType.DMA((steps,)), pltpu.SemaphoreType.DMA((steps,))],
        name="pick_rows",
    )(ids, query_table, pair_table)


def main_kernel(
    sizes,
    counts,
    queries,
    blob,
    prior,
    window_out,
    step_out,
    state_out,
    out,
    state,
    land_blob,
    land_prior,
    query_rows,
    query_plain,
    query_scaled,
    prior_turned,
    total_turned,
    step_rows,
    key_rows,
    value_rows,
    turned,
    blob_send,
    blob_recv,
    prior_send,
    prior_recv,
    local_sem,
):
    n, heads, group, tok_rows, step_count, rows_valid = sizes
    chips = n // 2
    per_shard = step_count // n
    window_rows = tok_rows * group
    window = n * tok_rows
    prior_rows = prior.shape[1]
    shifted = prior_rows == rows_valid
    state_rows = state.shape[1]
    blocks = land_prior.shape[2] // LANES
    row_tiles = out.shape[1] // TILE
    padded_keys = key_rows.shape[1]
    me = lax.axis_index("ctx")
    core = lax.rem(me, 2)
    partner = me + 1 - 2 * core

    def across(step):
        return lax.rem(me + 2 * step, n)

    def twin(index):
        return index + 1 - 2 * lax.rem(index, 2)

    barrier = pltpu.get_barrier_semaphore()
    pl.semaphore_signal(barrier, inc=1, device_id={"ctx": partner}, device_id_type=MESH)
    for step in range(1, chips):
        pl.semaphore_signal(barrier, inc=1, device_id={"ctx": across(step)}, device_id_type=MESH)
    pl.semaphore_wait(barrier, chips)

    def blob_copy(src, source, slot, target):
        return pltpu.make_async_remote_copy(
            src_ref=src,
            dst_ref=land_blob.at[source],
            send_sem=blob_send.at[slot],
            recv_sem=blob_recv.at[source],
            device_id={"ctx": target},
            device_id_type=MESH,
        )

    def landing(source):
        first = pl.multiple_of(lax.rem(source * rows_valid, LANES), 16) if shifted else 0
        return pl.ds(first, prior_rows)

    def prior_copy(src, source, head, slot, target):
        return pltpu.make_async_remote_copy(
            src_ref=src,
            dst_ref=land_prior.at[source, head, landing(source)],
            send_sem=prior_send.at[slot, head],
            recv_sem=prior_recv.at[source, head],
            device_id={"ctx": target},
            device_id_type=MESH,
        )

    def blob_own(slot):
        return blob_copy(blob, me, slot, partner if slot == 0 else across(slot))

    def blob_forward(step):
        source = across(step)
        return blob_copy(land_blob.at[source], source, chips - 1 + step, partner)

    def prior_own(slot, head):
        target = partner if slot == 0 else across(slot)
        return prior_copy(prior.at[head], me, head, slot, target)

    def prior_forward(step, head):
        source = across(step)
        return prior_copy(
            land_prior.at[source, head, landing(source)],
            source,
            head,
            chips - 1 + step,
            partner,
        )

    for slot in list(range(1, chips)) + [0]:
        blob_own(slot).start()
    for head in range(heads):
        for slot in list(range(1, chips)) + [0]:
            prior_own(slot, head).start()
    own_blob = pltpu.make_async_copy(blob, land_blob.at[me], local_sem.at[0])
    own_prior = pltpu.make_async_copy(
        prior, land_prior.at[me, :, landing(me)], local_sem.at[1]
    )
    own_blob.start()
    own_prior.start()

    if shifted:
        for source in range(n):
            lead_rows = source * rows_valid % LANES
            for first, last in (
                (0, lead_rows),
                (lead_rows + prior_rows, blocks * LANES),
            ):
                if last > first:
                    for head in range(heads):
                        land_prior[source, head, pl.ds(first, last - first), :] = jnp.zeros(
                            (last - first, LANES), jnp.bfloat16
                        )
    total_turned[...] = jnp.zeros_like(total_turned)
    for head in range(heads):
        query_rows[head, pl.ds(0, window_rows), :] = queries[head]
        query_rows[head, pl.ds(window_rows, out.shape[1] - window_rows), :] = jnp.zeros(
            (out.shape[1] - window_rows, LANES), jnp.bfloat16
        )
        spare = padded_keys - window - step_count
        if spare > 0:
            key_rows[head, pl.ds(window + step_count, spare), :] = jnp.zeros(
                (spare, LANES), jnp.bfloat16
            )
            value_rows[head, pl.ds(window + step_count, spare), :] = jnp.zeros(
                (spare, LANES), jnp.bfloat16
            )

    def place(source):
        first = source * rows_valid
        return lax.div(first, LANES), lax.rem(first, LANES)

    identity = (
        lax.broadcasted_iota(jnp.int32, (LANES, LANES), 0)
        == lax.broadcasted_iota(jnp.int32, (LANES, LANES), 1)
    ).astype(jnp.bfloat16)
    contract_last = (((1,), (1,)), ((), ()))

    def transposed(rows):
        return lax.dot_general(identity, rows, contract_last, preferred_element_type=jnp.float32)

    chunks_per_tile = TILE // LANES

    def turn_queries(head, first_tile, last_tile):
        for chunk in range(first_tile * chunks_per_tile, last_tile * chunks_per_tile):
            piece = transposed(query_rows[head, pl.ds(chunk * LANES, LANES), :])
            scaled = piece * ROOT_TWO
            query_plain[head, chunk] = piece
            query_scaled[head, chunk, pl.ds(0, LANES), :] = scaled
            query_scaled[head, chunk, pl.ds(LANES, LANES), :] = scaled

    def carry_tile(source, head, tile):
        first_offset, _ = place(source)
        columns = []
        for side in range(chunks_per_tile):
            chunk = tile * chunks_per_tile + side
            here = query_plain[head, chunk]
            pieces = []
            for block in range(blocks):
                row = lax.rem(first_offset + block, LANES)
                other = query_scaled[head, chunk, pl.ds(row, LANES), :]
                if block == 0:
                    other = jnp.where(first_offset == 0, here, other)
                pieces.append((here * other).astype(jnp.bfloat16))
            columns.append(jnp.concatenate(pieces, axis=0))
        features = jnp.concatenate(columns, axis=1)
        total_turned[head, tile] += jnp.dot(
            prior_turned[...], features, preferred_element_type=jnp.float32
        )

    def carry(source, head, first_tile, last_tile):
        prior_turned[...] = transposed(land_prior[source, head]).astype(jnp.bfloat16)

        @pl.loop(first_tile, last_tile)
        def _(tile):
            carry_tile(source, head, tile)

    full_tiles = window_rows // TILE
    own_prior.wait()
    for head in range(heads):
        turn_queries(head, 0, full_tiles)
        carry(me, head, 0, full_tiles)

    own_blob.wait()
    blob_copy(blob, partner, 0, partner).wait_recv()
    for step in range(1, chips):
        blob_copy(blob, across(step), 0, partner).wait_recv()
        blob_forward(step).start()
    for step in range(1, chips):
        blob_copy(blob, twin(across(step)), 0, partner).wait_recv()

    for head in range(heads):
        for source in range(n):
            key_rows[head, pl.ds(source * tok_rows, tok_rows), :] = land_blob[
                source, head, pl.ds(0, tok_rows), :
            ]
            value_rows[head, pl.ds(source * tok_rows, tok_rows), :] = land_blob[
                source, heads + head, pl.ds(0, tok_rows), :
            ]

        def picked(plane, first, count):
            total = land_blob[0, plane, pl.ds(first, count), :].astype(jnp.float32)
            for source in range(1, n):
                total += land_blob[source, plane, pl.ds(first, count), :].astype(jnp.float32)
            return total

        key_rows[head, pl.ds(window, step_count), :] = picked(head, tok_rows, step_count).astype(
            jnp.bfloat16
        )
        value_rows[head, pl.ds(window, step_count), :] = picked(
            heads + head, tok_rows, step_count
        ).astype(jnp.bfloat16)
        half = step_count * group // 2
        for side in range(2):
            step_rows[head, pl.ds(side * half, half), :] = picked(
                2 * head + side, tok_rows + step_count, half
            )
        own_steps = per_shard * group
        own_rows = step_rows[head, pl.ds(me * own_steps, own_steps), :]
        query_rows[head, pl.ds(window_rows, own_steps), :] = own_rows.astype(jnp.bfloat16)
        turn_queries(head, full_tiles, row_tiles)

    for head in range(heads):
        carry(me, head, full_tiles, row_tiles)
        prior_copy(prior.at[head], partner, head, 0, partner).wait_recv()
        carry(partner, head, 0, row_tiles)

    def state_copy(head):
        return pltpu.make_async_copy(state.at[head], state_out.at[head], local_sem.at[2 + head])

    def positions(tile):
        local = tile * TILE + lax.broadcasted_iota(jnp.int32, (TILE, 1), 0)
        return jnp.where(
            local < window_rows,
            local + me * window_rows,
            local - window_rows + window * group + me * (per_shard * group),
        )

    first_offset, lead = place(me)
    for head in range(heads):
        keys_turned = transposed(key_rows[head])
        chunks = padded_keys // LANES
        for chunk in range(chunks):
            piece = keys_turned[:, chunk * LANES : (chunk + 1) * LANES]
            turned[head, chunk, pl.ds(0, LANES), :] = piece
            turned[head, chunk, pl.ds(LANES, LANES), :] = piece

        def state_block(block):
            row = lax.broadcasted_iota(jnp.int32, (LANES, LANES), 0)
            early = row < LANES - lead
            plain = jnp.logical_and(early, first_offset + block == 0)
            factor = jnp.where(plain, 1.0, ROOT_TWO)
            near_row = lax.rem(lead + first_offset + block, LANES)
            far_row = lax.rem(lead + first_offset + block + 1, LANES)
            pieces = []
            for chunk in range(chunks):
                here = turned[head, chunk, pl.ds(lead, LANES), :]
                near = turned[head, chunk, pl.ds(near_row, LANES), :]
                far = turned[head, chunk, pl.ds(far_row, LANES), :]
                both = jnp.where(early, near, far) * factor
                pieces.append((here * both).astype(jnp.bfloat16))
            features = jnp.concatenate(pieces, axis=1)
            return jnp.dot(features, value_rows[head], preferred_element_type=jnp.float32)

        def before(rows):
            return prior[head, rows, :].astype(jnp.float32) if shifted else 0.0

        whole_blocks = state_rows // LANES

        @pl.loop(0, whole_blocks)
        def _(block):
            rows = pl.ds(pl.multiple_of(block * LANES, LANES), LANES)
            state[head, rows, :] = before(rows) + state_block(block)

        rest = state_rows - whole_blocks * LANES
        if rest > 0:
            rows = pl.ds(whole_blocks * LANES, rest)
            state[head, rows, :] = before(rows) + state_block(whole_blocks)[:rest]
        state_copy(head).start()

        @pl.loop(0, row_tiles)
        def _(tile):
            rows = pl.ds(pl.multiple_of(tile * TILE, TILE), TILE)
            scores = lax.dot_general(
                query_rows[head, rows, :],
                key_rows[head],
                contract_last,
                preferred_element_type=jnp.float32,
            )
            position = positions(tile)
            key_index = lax.broadcasted_iota(jnp.int32, scores.shape, 1)
            allowed = position >= key_index * group
            weights = jnp.where(allowed, scores * scores, 0.0).astype(jnp.bfloat16)
            out[head, rows, :] = jnp.dot(
                weights, value_rows[head], preferred_element_type=jnp.float32
            )

    for step in range(1, chips):
        source = across(step)
        for head in range(heads):
            prior_copy(prior.at[head], source, head, 0, partner).wait_recv()
            prior_forward(step, head).start()
            carry(source, head, 0, row_tiles)
            prior_copy(prior.at[head], twin(source), head, 0, partner).wait_recv()
            carry(twin(source), head, 0, row_tiles)

    for head in range(heads):
        for tile in range(row_tiles):
            first = tile * TILE
            token = jnp.floor((positions(tile).astype(jnp.float32) + 0.5) / group)
            place_in_prompt = token + (counts[0] + 1).astype(jnp.float32)
            scale = 1.0 / (LANES * jnp.sqrt(place_in_prompt))
            total = out[head, pl.ds(first, TILE), :] + total_turned[head, tile].T
            total = (total * scale).astype(jnp.bfloat16)
            split = min(max(window_rows - first, 0), TILE)
            if split > 0:
                window_out[head, pl.ds(first, split), :] = total[:split]
            if split < TILE:
                step_out[head, pl.ds(first + split - window_rows, TILE - split), :] = total[split:]
        state_copy(head).wait()

    for slot in range(chips):
        blob_own(slot).wait_send()
        for head in range(heads):
            prior_own(slot, head).wait_send()
    for step in range(1, chips):
        blob_forward(step).wait_send()
        for head in range(heads):
            prior_forward(step, head).wait_send()


def combine(sizes, counts, queries, blob, prior, out_rows):
    n, heads, group, tok_rows, step_count, rows_valid = sizes
    window_rows = tok_rows * group
    lead = max(source * rows_valid % LANES for source in range(n))
    padded_rows = round_up(lead + rows_valid, LANES)
    chunks = out_rows // LANES
    state_rows = round_up(rows_valid, 8)
    padded_keys = round_up(n * tok_rows + step_count, LANES)
    slots = 2 * (n // 2) - 1
    vmem = pl.BlockSpec(memory_space=pltpu.VMEM)
    return pl.pallas_call(
        functools.partial(main_kernel, sizes),
        out_shape=(
            jax.ShapeDtypeStruct((heads, window_rows, LANES), jnp.bfloat16),
            jax.ShapeDtypeStruct((heads, out_rows - window_rows, LANES), jnp.bfloat16),
            jax.ShapeDtypeStruct((heads, state_rows, LANES), jnp.float32),
        ),
        in_specs=[pl.BlockSpec(memory_space=pltpu.SMEM)] + [vmem] * 3,
        out_specs=(vmem, vmem, pl.BlockSpec(memory_space=pl.ANY)),
        scratch_shapes=[
            pltpu.VMEM((heads, out_rows, LANES), jnp.float32),
            pltpu.VMEM((heads, state_rows, LANES), jnp.float32),
            pltpu.VMEM((n,) + blob.shape, jnp.bfloat16),
            pltpu.VMEM((n, heads, padded_rows, LANES), jnp.bfloat16),
            pltpu.VMEM((heads, out_rows, LANES), jnp.bfloat16),
            pltpu.VMEM((heads, chunks, LANES, LANES), jnp.float32),
            pltpu.VMEM((heads, chunks, 2 * LANES, LANES), jnp.float32),
            pltpu.VMEM((LANES, padded_rows), jnp.bfloat16),
            pltpu.VMEM((heads, out_rows // TILE, LANES, TILE), jnp.float32),
            pltpu.VMEM((heads, step_count * group, LANES), jnp.float32),
            pltpu.VMEM((heads, padded_keys, LANES), jnp.bfloat16),
            pltpu.VMEM((heads, padded_keys, LANES), jnp.bfloat16),
            pltpu.VMEM((heads, padded_keys // LANES, 2 * LANES, LANES), jnp.float32),
            pltpu.SemaphoreType.DMA((slots,)),
            pltpu.SemaphoreType.DMA((n,)),
            pltpu.SemaphoreType.DMA((slots, heads)),
            pltpu.SemaphoreType.DMA((n, heads)),
            pltpu.SemaphoreType.DMA((2 + heads,)),
        ],
        compiler_params=pltpu.CompilerParams(
            collective_id=0, has_side_effects=True, vmem_limit_bytes=48 * 2**20
        ),
        name="combine",
    )(counts, queries, blob, prior)


def on_device_gather(queries, keys_values, prior_state, counts, continuation, query_table, pair_table):
    tok_rows, heads, group, head_size = queries.shape
    n = lax.axis_size("ctx")
    shard_index = lax.axis_index("ctx")
    step_count = continuation.shape[0]
    per_shard = step_count // n
    rows_valid = prior_state.shape[1]

    query_pick, pair_pick = pick_rows(
        continuation, query_table.transpose(0, 2, 1, 3), pair_table
    )

    window_planes = keys_values.transpose(2, 1, 0, 3).reshape(2 * heads, tok_rows, head_size)
    step_planes = pair_pick.transpose(2, 1, 0, 3)
    step_planes = step_planes.reshape(2 * heads, step_count, head_size)
    query_planes = query_pick.transpose(2, 0, 1, 3).reshape(
        2 * heads, step_count * group // 2, head_size
    )
    blob = jnp.concatenate([window_planes, step_planes, query_planes], axis=1)
    query_planes = queries.transpose(1, 0, 2, 3).reshape(heads, tok_rows * group, head_size)
    prior = prior_state
    if rows_valid % 16 != 0:
        leads = [source * rows_valid % LANES for source in range(n)]
        prior = lax.dynamic_update_slice(
            jnp.zeros((heads, round_up(max(leads) + rows_valid, LANES), LANES), prior.dtype),
            prior_state,
            (0, shard_index * rows_valid % LANES, 0),
        )
    out_rows = round_up((tok_rows + per_shard) * group, TILE)
    sizes = (n, heads, group, tok_rows, step_count, rows_valid)
    window_out, step_out, state = combine(sizes, counts, query_planes, blob, prior, out_rows)

    decode_state = state
    if rows_valid % 16 != 0:
        decode_state = prior_state.astype(jnp.float32) + state[:, :rows_valid]
    readout = window_out.reshape(heads, tok_rows, group, head_size).transpose(1, 0, 2, 3)
    decode_out = step_out[:, : per_shard * group]
    decode_out = decode_out.reshape(heads, per_shard, group, head_size).transpose(1, 0, 2, 3)
    return (readout, decode_out, decode_state)


def identity():
    row = lax.broadcasted_iota(jnp.int32, (LANES, LANES), 0)
    column = lax.broadcasted_iota(jnp.int32, (LANES, LANES), 1)
    return (row == column).astype(jnp.bfloat16)


def turned_rows(rows):
    return lax.dot_general(
        identity(), rows, CONTRACT_LAST, preferred_element_type=jnp.float32
    )


def turn_queries(load, count, plain, scaled):
    for chunk in range(count // LANES):
        piece = turned_rows(load(chunk * LANES))
        twice = piece * ROOT_TWO
        plain[chunk] = piece
        scaled[chunk, pl.ds(0, LANES), :] = twice
        scaled[chunk, pl.ds(LANES, LANES), :] = twice


def carry_tile(state_turned, first_offset, plain, scaled, tile):
    blocks = state_turned.shape[1] // LANES
    columns = []
    for side in range(TILE // LANES):
        chunk = tile * (TILE // LANES) + side
        here = plain[chunk]
        pieces = []
        for block in range(blocks):
            other = scaled[chunk, pl.ds(first_offset + block, LANES), :]
            if block == 0:
                other = jnp.where(first_offset == 0, here, other)
            pieces.append((here * other).astype(jnp.bfloat16))
        columns.append(jnp.concatenate(pieces, axis=0))
    features = jnp.concatenate(columns, axis=1)
    return jnp.dot(state_turned[...], features, preferred_element_type=jnp.float32).T


def chip_place(rows_valid):
    first = lax.div(lax.axis_index("ctx"), 2) * (2 * rows_valid)
    return lax.div(first, LANES), pl.multiple_of(lax.rem(first, LANES), 16)


def early_kernel(rows_valid, queries, own, other, turned, local, rows, plain, scaled):
    heads, padded = turned.shape[0], turned.shape[2]
    first_offset, lead = chip_place(rows_valid)
    core = lax.rem(lax.axis_index("ctx"), 2)
    count = local.shape[1]
    for head in range(heads):
        rows[pl.ds(0, LANES), :] = jnp.zeros((LANES, LANES), rows.dtype)
        spare = padded - 2 * rows_valid
        rows[pl.ds(padded - spare, spare), :] = jnp.zeros((spare, LANES), rows.dtype)
        for source, index in ((own, core), (other, 1 - core)):
            start = pl.multiple_of(lead + index * rows_valid, 16)
            rows[pl.ds(start, rows_valid), :] = source[head]
        for first in range(0, padded, 2 * LANES):
            size = min(2 * LANES, padded - first)
            turned[head, :, pl.ds(first, size)] = turned_rows(
                rows[pl.ds(first, size), :]
            ).astype(turned.dtype)
        turn_queries(
            lambda at: queries[head, pl.ds(at, LANES), :], count, plain, scaled
        )
        for tile in range(count // TILE):
            local[head, pl.ds(tile * TILE, TILE), :] = carry_tile(
                turned.at[head], first_offset, plain, scaled, tile
            )


def fill_tail(queries, steps, first, tail):
    window = queries.shape[0] - first
    count = steps.shape[0]
    tail[...] = jnp.zeros_like(tail)
    tail[pl.ds(0, window), :] = queries[pl.ds(first, window), :]
    tail[pl.ds(window, count), :] = steps


def rows_at(sizes, who, first):
    n, _, group, tok_rows, step_count, _ = sizes
    window_rows = tok_rows * group
    at = first + lax.broadcasted_iota(jnp.int32, (TILE, 1), 0)
    return jnp.where(
        at < window_rows,
        at + who * window_rows,
        at + (n - 1) * window_rows + who * (step_count // n * group),
    )


def rows_scale(sizes, counts, position):
    token = jnp.floor((position.astype(jnp.float32) + 0.5) / sizes[2])
    place_in_prompt = token + (counts[0] + 1).astype(jnp.float32)
    return 1.0 / (LANES * jnp.sqrt(place_in_prompt))


def remote_kernel(
    sizes, early, counts, queries, steps, turned, partial, tail, mixed, plain, scaled
):
    n, heads, rows_valid = sizes[0], sizes[1], sizes[5]
    first_offset, _ = chip_place(rows_valid)
    across = lax.rem(lax.axis_index("ctx") + 2, n)
    there = lax.div(across, 2)
    for head in range(heads):
        turn_queries(
            lambda at: queries[head, pl.ds(at, LANES), :], early, plain, scaled
        )
        for tile in range(early // TILE + 1):
            first = tile * TILE
            if first == early:
                fill_tail(queries.at[head], steps[there, head], early, tail)
                turn_queries(lambda at: tail[pl.ds(at, LANES), :], TILE, plain, scaled)
            rows = carry_tile(
                turned.at[head], first_offset, plain, scaled, tile if first < early else 0
            )
            rows = rows * rows_scale(sizes, counts, rows_at(sizes, across, first))
            size = min(TILE, partial.shape[0] // heads - first)
            mixed[pl.ds(first * heads + head, size, stride=heads), :] = rows[:size]
    partial[...] = mixed[...].astype(partial.dtype)


def merge_kernel(n, own, twin, send):
    core = lax.rem(lax.axis_index("ctx"), 2)
    step_count, rows, heads = own.shape[:3]
    group = rows - heads
    per_shard = step_count // n

    def both(step, first, count):
        at = (step, pl.ds(first, count))
        return own[at] + twin[at]

    for at in range(n // 2):
        for step in range(per_shard):
            row = (at * per_shard + step) * group
            send[pl.ds(row, group)] = both((core + 2 * at) * per_shard + step, 0, group)
    for step in range(step_count):
        row = n // 2 * per_shard * group + step * heads
        send[pl.ds(row, heads)] = both(step, group, heads)


def own_tail_kernel(rows_valid, early, queries, steps, turned, local, tail, plain, scaled):
    first_offset, _ = chip_place(rows_valid)
    here = lax.div(lax.axis_index("ctx"), 2)
    for head in range(turned.shape[0]):
        fill_tail(queries.at[head], steps[here, head], early, tail)
        turn_queries(lambda at: tail[pl.ds(at, LANES), :], TILE, plain, scaled)
        local[head] = carry_tile(turned.at[head], first_offset, plain, scaled, 0)


def finish_kernel(result, got, window_out, step_out, total, sems):
    rows = window_out.shape[0]
    total[...] = (result[...] + got[...].astype(jnp.float32)).astype(total.dtype)
    copies = (
        pltpu.make_async_copy(total.at[pl.ds(0, rows)], window_out, sems.at[0]),
        pltpu.make_async_copy(
            total.at[pl.ds(rows, total.shape[0] - rows)], step_out, sems.at[1]
        ),
    )
    for copy in copies:
        copy.start()
    for copy in copies:
        copy.wait()


def late_kernel(
    sizes,
    counts,
    queries,
    steps,
    local_tail,
    local,
    own_pairs,
    twin_pairs,
    across_pairs,
    far_pairs,
    step_pairs,
    prior,
    result,
    state_out,
    tail,
    key_rows,
    value_rows,
    keys_plain,
    keys_scaled,
    delta,
    state,
    state_sem,
):
    n, heads, group, tok_rows, step_count, rows_valid = sizes
    me = lax.axis_index("ctx")
    twin = me + 1 - 2 * lax.rem(me, 2)
    window = n * tok_rows
    first_tail = local.shape[1]
    padded_keys = key_rows.shape[1]
    chunks = padded_keys // LANES
    blocks = delta.shape[0] // LANES
    my_first = me * rows_valid
    my_offset = lax.div(my_first, LANES)
    my_lead = pl.multiple_of(lax.rem(my_first, LANES), 8)
    places = (
        (own_pairs, me),
        (twin_pairs, twin),
        (across_pairs, lax.rem(me + 2, n)),
        (far_pairs, lax.rem(twin + 2, n)),
    )

    def state_copy(head):
        return pltpu.make_async_copy(state.at[head], state_out.at[head], state_sem.at[head])

    for head in range(heads):
        for plane, target in ((0, key_rows), (1, value_rows)):
            for pairs, source in places:
                start = pl.multiple_of(source * tok_rows, 16)
                target[head, pl.ds(start, tok_rows), :] = pairs[plane, head]
            target[head, pl.ds(window, step_count), :] = step_pairs[plane, head]
            spare = padded_keys - window - step_count
            if spare > 0:
                target[head, pl.ds(window + step_count, spare), :] = jnp.zeros(
                    (spare, LANES), target.dtype
                )
        for chunk in range(chunks):
            piece = turned_rows(key_rows[head, pl.ds(chunk * LANES, LANES), :])
            twice = piece * ROOT_TWO
            keys_plain[chunk] = piece
            keys_scaled[chunk, pl.ds(0, LANES), :] = twice
            keys_scaled[chunk, pl.ds(LANES, LANES), :] = twice

        def key_features(block, maybe_plain):
            pieces = []
            for chunk in range(chunks):
                here = keys_plain[chunk]
                other = keys_scaled[chunk, pl.ds(my_offset + block, LANES), :]
                if maybe_plain:
                    other = jnp.where(my_offset == 0, here, other)
                pieces.append((here * other).astype(jnp.bfloat16))
            return jnp.concatenate(pieces, axis=1)

        def add_block(features, first):
            delta[pl.ds(first, features.shape[0]), :] = jnp.dot(
                features, value_rows[head], preferred_element_type=jnp.float32
            )

        odd = 1 if blocks % 2 else 2
        for block in range(odd):
            add_block(key_features(block, block == 0), block * LANES)

        @pl.loop(0, (blocks - odd) // 2)
        def _(pair):
            block = odd + 2 * pair
            both = jnp.concatenate(
                [key_features(block, False), key_features(block + 1, False)], axis=0
            )
            add_block(both, pl.multiple_of(block * LANES, LANES))

        state[head] = prior[head].astype(jnp.float32) + delta[pl.ds(my_lead, rows_valid), :]
        state_copy(head).start()

    for head in range(heads):
        fill_tail(queries.at[head], steps[lax.div(me, 2), head], first_tail, tail)
        rows_out = result.shape[0] // heads
        for first in range(0, rows_out, TILE):
            last = first >= first_tail
            rows = tail[...] if last else queries[head, pl.ds(first, TILE), :]
            scores = lax.dot_general(
                rows, key_rows[head], CONTRACT_LAST, preferred_element_type=jnp.float32
            )
            position = rows_at(sizes, me, first)
            key_index = lax.broadcasted_iota(jnp.int32, scores.shape, 1)
            weights = jnp.where(position >= key_index * group, scores * scores, 0.0)
            total = jnp.dot(
                weights.astype(jnp.bfloat16), value_rows[head], preferred_element_type=jnp.float32
            )
            carried = local_tail[head] if last else local[head, pl.ds(first, TILE), :]
            size = min(TILE, rows_out - first)
            total = (total + carried) * rows_scale(sizes, counts, position)
            result[pl.ds(first * heads + head, size, stride=heads), :] = total[:size]
    for head in range(heads):
        state_copy(head).wait()


def pick_both_kernel(ids_ref, query_table, pair_table, picked, query_sem, pair_sem):
    vocab_rows, group = query_table.shape[:2]
    first_row = lax.axis_index("ctx") * vocab_rows
    heads = pair_table.shape[1]
    picked[...] = jnp.zeros_like(picked)

    def each(step, act):
        row = ids_ref[step] - first_row

        @pl.when(jnp.logical_and(row >= 0, row < vocab_rows))
        def _():
            to_queries = picked.at[step, pl.ds(0, group)]
            to_pairs = picked.at[step, pl.ds(group, heads)]
            act(pltpu.make_async_copy(query_table.at[row], to_queries, query_sem.at[step]))
            act(pltpu.make_async_copy(pair_table.at[row], to_pairs, pair_sem.at[step]))

    for step in range(picked.shape[0]):
        each(step, lambda copy: copy.start())
    for step in range(picked.shape[0]):
        each(step, lambda copy: copy.wait())


def pick_both(ids, query_table, pair_table):
    steps, group, heads = ids.shape[0], query_table.shape[1], pair_table.shape[1]
    shape = (steps, group + heads) + pair_table.shape[2:]
    return pl.pallas_call(
        pick_both_kernel,
        out_shape=jax.ShapeDtypeStruct(shape, pair_table.dtype),
        in_specs=[
            pl.BlockSpec(memory_space=pltpu.SMEM),
            pl.BlockSpec(memory_space=pl.ANY),
            pl.BlockSpec(memory_space=pl.ANY),
        ],
        out_specs=pl.BlockSpec(memory_space=pltpu.VMEM),
        scratch_shapes=[pltpu.SemaphoreType.DMA((steps,)), pltpu.SemaphoreType.DMA((steps,))],
        compiler_params=pltpu.CompilerParams(vmem_limit_bytes=56 * 2**20),
        name="pick_both",
    )(ids, query_table, pair_table)


def vmem_call(kernel, out_shape, operands, scratch, limit, out_specs=None):
    smem = pl.BlockSpec(memory_space=pltpu.SMEM)
    vmem = pl.BlockSpec(memory_space=pltpu.VMEM)
    return pl.pallas_call(
        kernel,
        out_shape=out_shape,
        in_specs=[smem if operand.ndim == 1 else vmem for operand in operands],
        out_specs=out_specs if out_specs is not None else jax.tree.map(lambda _: vmem, out_shape),
        scratch_shapes=scratch,
        compiler_params=pltpu.CompilerParams(vmem_limit_bytes=limit * 2**20),
    )(*operands)


def turn_scratch(columns):
    chunks = columns // LANES
    return [
        pltpu.VMEM((chunks, LANES, LANES), jnp.float32),
        pltpu.VMEM((chunks, 2 * LANES, LANES), jnp.float32),
    ]


def on_device_exchange(
    queries, keys_values, prior, counts, continuation, query_table, pair_table
):
    tok_rows, heads, group, head_size = queries.shape
    n = lax.axis_size("ctx")
    step_count = continuation.shape[0]
    per_shard = step_count // n
    step_rows = per_shard * group
    rows_valid = prior.shape[1]
    window_rows = tok_rows * group
    early = window_rows // TILE * TILE
    rows_chip = 2 * rows_valid
    padded = max(
        round_up(chip_at * rows_chip % LANES + rows_chip, LANES) for chip_at in range(n // 2)
    )
    blocks = max(
        round_up(source * rows_valid % LANES + rows_valid, LANES) // LANES for source in range(n)
    )
    padded_keys = round_up(n * tok_rows + step_count, LANES)
    bf16, f32 = jnp.bfloat16, jnp.float32
    sizes = (n, heads, group, tok_rows, step_count, rows_valid)
    shape = jax.ShapeDtypeStruct

    def swap_across(value):
        return lax.ppermute(value, "ctx", [(i, (i + 2) % n) for i in range(n)])

    def swap_twin(value):
        return lax.ppermute(value, "ctx", [(i, i ^ 1) for i in range(n)])

    def query_planes(value):
        return value.transpose(1, 0, 2, 3).reshape(heads, -1, head_size)

    def pair_planes(value):
        return value.transpose(2, 1, 0, 3)

    across_queries = swap_across(queries)
    across_pairs = swap_across(keys_values)
    twin_prior = swap_twin(prior)
    twin_pairs = swap_twin(keys_values)
    picked = pick_both(continuation, query_table.transpose(0, 2, 1, 3), pair_table)
    twin_picked = swap_twin(picked)
    send = vmem_call(
        functools.partial(merge_kernel, n),
        shape((n // 2 * step_rows + step_count * heads, 2, head_size), bf16),
        (picked, twin_picked),
        [],
        4,
    )
    steps = send + swap_across(send)
    step_pairs = pair_planes(steps[n // 2 * step_rows :].reshape(step_count, heads, 2, head_size))
    step_queries = steps[: n // 2 * step_rows].reshape(n // 2, step_rows, heads, head_size)
    step_queries = step_queries.transpose(0, 2, 1, 3)

    own_rows = query_planes(queries)
    turned, local = vmem_call(
        functools.partial(early_kernel, rows_valid),
        (shape((heads, LANES, padded), bf16), shape((heads, early, LANES), f32)),
        (own_rows, prior, twin_prior),
        [pltpu.VMEM((padded, LANES), bf16)] + turn_scratch(early),
        16,
    )
    across_rows = query_planes(across_queries)
    partial = vmem_call(
        functools.partial(remote_kernel, sizes, early),
        shape((heads * (window_rows + step_rows), LANES), bf16),
        (counts, across_rows, step_queries, turned),
        [
            pltpu.VMEM((TILE, LANES), bf16),
            pltpu.VMEM((heads * (window_rows + step_rows), LANES), f32),
        ]
        + turn_scratch(early),
        16,
    )
    got = swap_across(partial)
    far_pairs = swap_twin(across_pairs)
    local_tail = vmem_call(
        functools.partial(own_tail_kernel, rows_valid, early),
        shape((heads, TILE, LANES), f32),
        (own_rows, step_queries, turned),
        [pltpu.VMEM((TILE, LANES), bf16)] + turn_scratch(TILE),
        16,
    )
    vmem = pl.BlockSpec(memory_space=pltpu.VMEM)
    chunks = padded_keys // LANES
    result, decode_state = vmem_call(
        functools.partial(late_kernel, sizes),
        (
            shape((heads * (window_rows + step_rows), LANES), f32),
            shape((heads, rows_valid, LANES), f32),
        ),
        (
            counts,
            own_rows,
            step_queries,
            local_tail,
            local,
            pair_planes(keys_values),
            pair_planes(twin_pairs),
            pair_planes(across_pairs),
            pair_planes(far_pairs),
            step_pairs,
            prior,
        ),
        [
            pltpu.VMEM((TILE, LANES), bf16),
            pltpu.VMEM((heads, padded_keys, LANES), bf16),
            pltpu.VMEM((heads, padded_keys, LANES), bf16),
            pltpu.VMEM((chunks, LANES, LANES), f32),
            pltpu.VMEM((chunks, 2 * LANES, LANES), f32),
            pltpu.VMEM((blocks * LANES, LANES), f32),
            pltpu.VMEM((heads, rows_valid, LANES), f32),
            pltpu.SemaphoreType.DMA((heads,)),
        ],
        24,
        (vmem, pl.BlockSpec(memory_space=pl.ANY)),
    )
    hbm = pl.BlockSpec(memory_space=pl.ANY)
    readout, decode_out = vmem_call(
        finish_kernel,
        (shape((heads * window_rows, LANES), bf16), shape((heads * step_rows, LANES), bf16)),
        (result, got),
        [pltpu.VMEM(got.shape, bf16), pltpu.SemaphoreType.DMA((2,))],
        8,
        (hbm, hbm),
    )
    readout = readout.reshape(tok_rows, group, heads, head_size)
    decode_out = decode_out.reshape(per_shard, group, heads, head_size)
    return (readout.transpose(0, 2, 1, 3), decode_out.transpose(0, 2, 1, 3), decode_state)


def solution(mesh):
    in_specs = (
        P(("groups", "ctx"), "head", None, None),
        P(("groups", "ctx"), "head", None, None),
        P(("groups", "head"), "ctx", None),
        P("groups"),
        P("groups"),
        P("ctx", "head", None, None),
        P("ctx", "head", None, None),
    )
    out_specs = (
        P(("groups", "ctx"), "head", None, None),
        P(("groups", "ctx"), "head", None, None),
        P(("groups", "head"), "ctx", None),
    )

    def on_device(*arguments):
        n, rows_valid = lax.axis_size("ctx"), arguments[2].shape[1]
        if n == 4 and rows_valid % 16 == 0:
            return on_device_exchange(*arguments)
        return on_device_gather(*arguments)

    return jax.shard_map(
        on_device, mesh=mesh, in_specs=in_specs, out_specs=out_specs, check_vma=False
    )
```

```python
import functools

import jax
import jax.numpy as jnp
from jax import lax
from jax.experimental import pallas as pl
from jax.experimental.pallas import tpu as pltpu
from jax.sharding import PartitionSpec as P


ROOT_TWO = 2.0**0.5
MESH = pl.DeviceIdType.MESH
TILE = 256
LANES = 128
CONTRACT_LAST = (((1,), (1,)), ((), ()))


def round_up(number, multiple):
    return (number + multiple - 1) // multiple * multiple


def pick_kernel(ids_ref, query_table, pair_table, query_out, pair_out, query_sem, pair_sem):
    vocab_rows = query_table.shape[0]
    first_row = lax.axis_index("ctx") * vocab_rows
    query_out[...] = jnp.zeros_like(query_out)
    pair_out[...] = jnp.zeros_like(pair_out)

    def each(step, act):
        row = ids_ref[step] - first_row

        @pl.when(jnp.logical_and(row >= 0, row < vocab_rows))
        def _():
            act(pltpu.make_async_copy(query_table.at[row], query_out.at[step], query_sem.at[step]))
            act(pltpu.make_async_copy(pair_table.at[row], pair_out.at[step], pair_sem.at[step]))

    for step in range(query_out.shape[0]):
        each(step, lambda copy: copy.start())
    for step in range(query_out.shape[0]):
        each(step, lambda copy: copy.wait())


def pick_rows(ids, query_table, pair_table):
    steps = ids.shape[0]
    return pl.pallas_call(
        pick_kernel,
        out_shape=(
            jax.ShapeDtypeStruct((steps,) + query_table.shape[1:], query_table.dtype),
            jax.ShapeDtypeStruct((steps,) + pair_table.shape[1:], pair_table.dtype),
        ),
        in_specs=[
            pl.BlockSpec(memory_space=pltpu.SMEM),
            pl.BlockSpec(memory_space=pl.ANY),
            pl.BlockSpec(memory_space=pl.ANY),
        ],
        out_specs=(
            pl.BlockSpec(memory_space=pltpu.VMEM),
            pl.BlockSpec(memory_space=pltpu.VMEM),
        ),
        scratch_shapes=[pltpu.SemaphoreType.DMA((steps,)), pltpu.SemaphoreType.DMA((steps,))],
        name="pick_rows",
    )(ids, query_table, pair_table)


def main_kernel(
    sizes,
    counts,
    queries,
    blob,
    prior,
    window_out,
    step_out,
    state_out,
    out,
    state,
    land_blob,
    land_prior,
    query_rows,
    query_plain,
    query_scaled,
    prior_turned,
    total_turned,
    step_rows,
    key_rows,
    value_rows,
    turned,
    blob_send,
    blob_recv,
    prior_send,
    prior_recv,
    local_sem,
):
    n, heads, group, tok_rows, step_count, rows_valid = sizes
    chips = n // 2
    per_shard = step_count // n
    window_rows = tok_rows * group
    window = n * tok_rows
    prior_rows = prior.shape[1]
    shifted = prior_rows == rows_valid
    state_rows = state.shape[1]
    blocks = land_prior.shape[2] // LANES
    row_tiles = out.shape[1] // TILE
    padded_keys = key_rows.shape[1]
    me = lax.axis_index("ctx")
    core = lax.rem(me, 2)
    partner = me + 1 - 2 * core

    def across(step):
        return lax.rem(me + 2 * step, n)

    def twin(index):
        return index + 1 - 2 * lax.rem(index, 2)

    barrier = pltpu.get_barrier_semaphore()
    pl.semaphore_signal(barrier, inc=1, device_id={"ctx": partner}, device_id_type=MESH)
    for step in range(1, chips):
        pl.semaphore_signal(barrier, inc=1, device_id={"ctx": across(step)}, device_id_type=MESH)
    pl.semaphore_wait(barrier, chips)

    def blob_copy(src, source, slot, target):
        return pltpu.make_async_remote_copy(
            src_ref=src,
            dst_ref=land_blob.at[source],
            send_sem=blob_send.at[slot],
            recv_sem=blob_recv.at[source],
            device_id={"ctx": target},
            device_id_type=MESH,
        )

    def landing(source):
        first = pl.multiple_of(lax.rem(source * rows_valid, LANES), 16) if shifted else 0
        return pl.ds(first, prior_rows)

    def prior_copy(src, source, head, slot, target):
        return pltpu.make_async_remote_copy(
            src_ref=src,
            dst_ref=land_prior.at[source, head, landing(source)],
            send_sem=prior_send.at[slot, head],
            recv_sem=prior_recv.at[source, head],
            device_id={"ctx": target},
            device_id_type=MESH,
        )

    def blob_own(slot):
        return blob_copy(blob, me, slot, partner if slot == 0 else across(slot))

    def blob_forward(step):
        source = across(step)
        return blob_copy(land_blob.at[source], source, chips - 1 + step, partner)

    def prior_own(slot, head):
        target = partner if slot == 0 else across(slot)
        return prior_copy(prior.at[head], me, head, slot, target)

    def prior_forward(step, head):
        source = across(step)
        return prior_copy(
            land_prior.at[source, head, landing(source)],
            source,
            head,
            chips - 1 + step,
            partner,
        )

    for slot in list(range(1, chips)) + [0]:
        blob_own(slot).start()
    for head in range(heads):
        for slot in list(range(1, chips)) + [0]:
            prior_own(slot, head).start()
    own_blob = pltpu.make_async_copy(blob, land_blob.at[me], local_sem.at[0])
    own_prior = pltpu.make_async_copy(
        prior, land_prior.at[me, :, landing(me)], local_sem.at[1]
    )
    own_blob.start()
    own_prior.start()

    if shifted:
        for source in range(n):
            lead_rows = source * rows_valid % LANES
            for first, last in (
                (0, lead_rows),
                (lead_rows + prior_rows, blocks * LANES),
            ):
                if last > first:
                    for head in range(heads):
                        land_prior[source, head, pl.ds(first, last - first), :] = jnp.zeros(
                            (last - first, LANES), jnp.bfloat16
                        )
    total_turned[...] = jnp.zeros_like(total_turned)
    for head in range(heads):
        query_rows[head, pl.ds(0, window_rows), :] = queries[head]
        query_rows[head, pl.ds(window_rows, out.shape[1] - window_rows), :] = jnp.zeros(
            (out.shape[1] - window_rows, LANES), jnp.bfloat16
        )
        spare = padded_keys - window - step_count
        if spare > 0:
            key_rows[head, pl.ds(window + step_count, spare), :] = jnp.zeros(
                (spare, LANES), jnp.bfloat16
            )
            value_rows[head, pl.ds(window + step_count, spare), :] = jnp.zeros(
                (spare, LANES), jnp.bfloat16
            )

    def place(source):
        first = source * rows_valid
        return lax.div(first, LANES), lax.rem(first, LANES)

    identity = (
        lax.broadcasted_iota(jnp.int32, (LANES, LANES), 0)
        == lax.broadcasted_iota(jnp.int32, (LANES, LANES), 1)
    ).astype(jnp.bfloat16)
    contract_last = (((1,), (1,)), ((), ()))

    def transposed(rows):
        return lax.dot_general(identity, rows, contract_last, preferred_element_type=jnp.float32)

    chunks_per_tile = TILE // LANES

    def turn_queries(head, first_tile, last_tile):
        for chunk in range(first_tile * chunks_per_tile, last_tile * chunks_per_tile):
            piece = transposed(query_rows[head, pl.ds(chunk * LANES, LANES), :])
            scaled = piece * ROOT_TWO
            query_plain[head, chunk] = piece
            query_scaled[head, chunk, pl.ds(0, LANES), :] = scaled
            query_scaled[head, chunk, pl.ds(LANES, LANES), :] = scaled

    def carry_tile(source, head, tile):
        first_offset, _ = place(source)
        columns = []
        for side in range(chunks_per_tile):
            chunk = tile * chunks_per_tile + side
            here = query_plain[head, chunk]
            pieces = []
            for block in range(blocks):
                row = lax.rem(first_offset + block, LANES)
                other = query_scaled[head, chunk, pl.ds(row, LANES), :]
                if block == 0:
                    other = jnp.where(first_offset == 0, here, other)
                pieces.append((here * other).astype(jnp.bfloat16))
            columns.append(jnp.concatenate(pieces, axis=0))
        features = jnp.concatenate(columns, axis=1)
        total_turned[head, tile] += jnp.dot(
            prior_turned[...], features, preferred_element_type=jnp.float32
        )

    def carry(source, head, first_tile, last_tile):
        prior_turned[...] = transposed(land_prior[source, head]).astype(jnp.bfloat16)

        @pl.loop(first_tile, last_tile)
        def _(tile):
            carry_tile(source, head, tile)

    full_tiles = window_rows // TILE
    own_prior.wait()
    for head in range(heads):
        turn_queries(head, 0, full_tiles)
        carry(me, head, 0, full_tiles)

    own_blob.wait()
    blob_copy(blob, partner, 0, partner).wait_recv()
    for step in range(1, chips):
        blob_copy(blob, across(step), 0, partner).wait_recv()
        blob_forward(step).start()
    for step in range(1, chips):
        blob_copy(blob, twin(across(step)), 0, partner).wait_recv()

    for head in range(heads):
        for source in range(n):
            key_rows[head, pl.ds(source * tok_rows, tok_rows), :] = land_blob[
                source, head, pl.ds(0, tok_rows), :
            ]
            value_rows[head, pl.ds(source * tok_rows, tok_rows), :] = land_blob[
                source, heads + head, pl.ds(0, tok_rows), :
            ]

        def picked(plane, first, count):
            total = land_blob[0, plane, pl.ds(first, count), :].astype(jnp.float32)
            for source in range(1, n):
                total += land_blob[source, plane, pl.ds(first, count), :].astype(jnp.float32)
            return total

        key_rows[head, pl.ds(window, step_count), :] = picked(head, tok_rows, step_count).astype(
            jnp.bfloat16
        )
        value_rows[head, pl.ds(window, step_count), :] = picked(
            heads + head, tok_rows, step_count
        ).astype(jnp.bfloat16)
        half = step_count * group // 2
        for side in range(2):
            step_rows[head, pl.ds(side * half, half), :] = picked(
                2 * head + side, tok_rows + step_count, half
            )
        own_steps = per_shard * group
        own_rows = step_rows[head, pl.ds(me * own_steps, own_steps), :]
        query_rows[head, pl.ds(window_rows, own_steps), :] = own_rows.astype(jnp.bfloat16)
        turn_queries(head, full_tiles, row_tiles)

    for head in range(heads):
        carry(me, head, full_tiles, row_tiles)
        prior_copy(prior.at[head], partner, head, 0, partner).wait_recv()
        carry(partner, head, 0, row_tiles)

    def state_copy(head):
        return pltpu.make_async_copy(state.at[head], state_out.at[head], local_sem.at[2 + head])

    def positions(tile):
        local = tile * TILE + lax.broadcasted_iota(jnp.int32, (TILE, 1), 0)
        return jnp.where(
            local < window_rows,
            local + me * window_rows,
            local - window_rows + window * group + me * (per_shard * group),
        )

    first_offset, lead = place(me)
    for head in range(heads):
        keys_turned = transposed(key_rows[head])
        chunks = padded_keys // LANES
        for chunk in range(chunks):
            piece = keys_turned[:, chunk * LANES : (chunk + 1) * LANES]
            turned[head, chunk, pl.ds(0, LANES), :] = piece
            turned[head, chunk, pl.ds(LANES, LANES), :] = piece

        def state_block(block):
            row = lax.broadcasted_iota(jnp.int32, (LANES, LANES), 0)
            early = row < LANES - lead
            plain = jnp.logical_and(early, first_offset + block == 0)
            factor = jnp.where(plain, 1.0, ROOT_TWO)
            near_row = lax.rem(lead + first_offset + block, LANES)
            far_row = lax.rem(lead + first_offset + block + 1, LANES)
            pieces = []
            for chunk in range(chunks):
                here = turned[head, chunk, pl.ds(lead, LANES), :]
                near = turned[head, chunk, pl.ds(near_row, LANES), :]
                far = turned[head, chunk, pl.ds(far_row, LANES), :]
                both = jnp.where(early, near, far) * factor
                pieces.append((here * both).astype(jnp.bfloat16))
            features = jnp.concatenate(pieces, axis=1)
            return jnp.dot(features, value_rows[head], preferred_element_type=jnp.float32)

        def before(rows):
            return prior[head, rows, :].astype(jnp.float32) if shifted else 0.0

        whole_blocks = state_rows // LANES

        @pl.loop(0, whole_blocks)
        def _(block):
            rows = pl.ds(pl.multiple_of(block * LANES, LANES), LANES)
            state[head, rows, :] = before(rows) + state_block(block)

        rest = state_rows - whole_blocks * LANES
        if rest > 0:
            rows = pl.ds(whole_blocks * LANES, rest)
            state[head, rows, :] = before(rows) + state_block(whole_blocks)[:rest]
        state_copy(head).start()

        @pl.loop(0, row_tiles)
        def _(tile):
            rows = pl.ds(pl.multiple_of(tile * TILE, TILE), TILE)
            scores = lax.dot_general(
                query_rows[head, rows, :],
                key_rows[head],
                contract_last,
                preferred_element_type=jnp.float32,
            )
            position = positions(tile)
            key_index = lax.broadcasted_iota(jnp.int32, scores.shape, 1)
            allowed = position >= key_index * group
            weights = jnp.where(allowed, scores * scores, 0.0).astype(jnp.bfloat16)
            out[head, rows, :] = jnp.dot(
                weights, value_rows[head], preferred_element_type=jnp.float32
            )

    for step in range(1, chips):
        source = across(step)
        for head in range(heads):
            prior_copy(prior.at[head], source, head, 0, partner).wait_recv()
            prior_forward(step, head).start()
            carry(source, head, 0, row_tiles)
            prior_copy(prior.at[head], twin(source), head, 0, partner).wait_recv()
            carry(twin(source), head, 0, row_tiles)

    for head in range(heads):
        for tile in range(row_tiles):
            first = tile * TILE
            token = jnp.floor((positions(tile).astype(jnp.float32) + 0.5) / group)
            place_in_prompt = token + (counts[0] + 1).astype(jnp.float32)
            scale = 1.0 / (LANES * jnp.sqrt(place_in_prompt))
            total = out[head, pl.ds(first, TILE), :] + total_turned[head, tile].T
            total = (total * scale).astype(jnp.bfloat16)
            split = min(max(window_rows - first, 0), TILE)
            if split > 0:
                window_out[head, pl.ds(first, split), :] = total[:split]
            if split < TILE:
                step_out[head, pl.ds(first + split - window_rows, TILE - split), :] = total[split:]
        state_copy(head).wait()

    for slot in range(chips):
        blob_own(slot).wait_send()
        for head in range(heads):
            prior_own(slot, head).wait_send()
    for step in range(1, chips):
        blob_forward(step).wait_send()
        for head in range(heads):
            prior_forward(step, head).wait_send()


def combine(sizes, counts, queries, blob, prior, out_rows):
    n, heads, group, tok_rows, step_count, rows_valid = sizes
    window_rows = tok_rows * group
    lead = max(source * rows_valid % LANES for source in range(n))
    padded_rows = round_up(lead + rows_valid, LANES)
    chunks = out_rows // LANES
    state_rows = round_up(rows_valid, 8)
    padded_keys = round_up(n * tok_rows + step_count, LANES)
    slots = 2 * (n // 2) - 1
    vmem = pl.BlockSpec(memory_space=pltpu.VMEM)
    return pl.pallas_call(
        functools.partial(main_kernel, sizes),
        out_shape=(
            jax.ShapeDtypeStruct((heads, window_rows, LANES), jnp.bfloat16),
            jax.ShapeDtypeStruct((heads, out_rows - window_rows, LANES), jnp.bfloat16),
            jax.ShapeDtypeStruct((heads, state_rows, LANES), jnp.float32),
        ),
        in_specs=[pl.BlockSpec(memory_space=pltpu.SMEM)] + [vmem] * 3,
        out_specs=(vmem, vmem, pl.BlockSpec(memory_space=pl.ANY)),
        scratch_shapes=[
            pltpu.VMEM((heads, out_rows, LANES), jnp.float32),
            pltpu.VMEM((heads, state_rows, LANES), jnp.float32),
            pltpu.VMEM((n,) + blob.shape, jnp.bfloat16),
            pltpu.VMEM((n, heads, padded_rows, LANES), jnp.bfloat16),
            pltpu.VMEM((heads, out_rows, LANES), jnp.bfloat16),
            pltpu.VMEM((heads, chunks, LANES, LANES), jnp.float32),
            pltpu.VMEM((heads, chunks, 2 * LANES, LANES), jnp.float32),
            pltpu.VMEM((LANES, padded_rows), jnp.bfloat16),
            pltpu.VMEM((heads, out_rows // TILE, LANES, TILE), jnp.float32),
            pltpu.VMEM((heads, step_count * group, LANES), jnp.float32),
            pltpu.VMEM((heads, padded_keys, LANES), jnp.bfloat16),
            pltpu.VMEM((heads, padded_keys, LANES), jnp.bfloat16),
            pltpu.VMEM((heads, padded_keys // LANES, 2 * LANES, LANES), jnp.float32),
            pltpu.SemaphoreType.DMA((slots,)),
            pltpu.SemaphoreType.DMA((n,)),
            pltpu.SemaphoreType.DMA((slots, heads)),
            pltpu.SemaphoreType.DMA((n, heads)),
            pltpu.SemaphoreType.DMA((2 + heads,)),
        ],
        compiler_params=pltpu.CompilerParams(
            collective_id=0, has_side_effects=True, vmem_limit_bytes=48 * 2**20
        ),
        name="combine",
    )(counts, queries, blob, prior)


def on_device_gather(queries, keys_values, prior_state, counts, continuation, query_table, pair_table):
    tok_rows, heads, group, head_size = queries.shape
    n = lax.axis_size("ctx")
    shard_index = lax.axis_index("ctx")
    step_count = continuation.shape[0]
    per_shard = step_count // n
    rows_valid = prior_state.shape[1]

    query_pick, pair_pick = pick_rows(
        continuation, query_table.transpose(0, 2, 1, 3), pair_table
    )

    window_planes = keys_values.transpose(2, 1, 0, 3).reshape(2 * heads, tok_rows, head_size)
    step_planes = pair_pick.transpose(2, 1, 0, 3)
    step_planes = step_planes.reshape(2 * heads, step_count, head_size)
    query_planes = query_pick.transpose(2, 0, 1, 3).reshape(
        2 * heads, step_count * group // 2, head_size
    )
    blob = jnp.concatenate([window_planes, step_planes, query_planes], axis=1)
    query_planes = queries.transpose(1, 0, 2, 3).reshape(heads, tok_rows * group, head_size)
    prior = prior_state
    if rows_valid % 16 != 0:
        leads = [source * rows_valid % LANES for source in range(n)]
        prior = lax.dynamic_update_slice(
            jnp.zeros((heads, round_up(max(leads) + rows_valid, LANES), LANES), prior.dtype),
            prior_state,
            (0, shard_index * rows_valid % LANES, 0),
        )
    out_rows = round_up((tok_rows + per_shard) * group, TILE)
    sizes = (n, heads, group, tok_rows, step_count, rows_valid)
    window_out, step_out, state = combine(sizes, counts, query_planes, blob, prior, out_rows)

    decode_state = state
    if rows_valid % 16 != 0:
        decode_state = prior_state.astype(jnp.float32) + state[:, :rows_valid]
    readout = window_out.reshape(heads, tok_rows, group, head_size).transpose(1, 0, 2, 3)
    decode_out = step_out[:, : per_shard * group]
    decode_out = decode_out.reshape(heads, per_shard, group, head_size).transpose(1, 0, 2, 3)
    return (readout, decode_out, decode_state)


def identity():
    row = lax.broadcasted_iota(jnp.int32, (LANES, LANES), 0)
    column = lax.broadcasted_iota(jnp.int32, (LANES, LANES), 1)
    return (row == column).astype(jnp.bfloat16)


def turned_rows(rows):
    return lax.dot_general(
        identity(), rows, CONTRACT_LAST, preferred_element_type=jnp.float32
    )


def turn_queries(load, count, plain, scaled):
    for chunk in range(count // LANES):
        piece = turned_rows(load(chunk * LANES))
        twice = piece * ROOT_TWO
        plain[chunk] = piece
        scaled[chunk, pl.ds(0, LANES), :] = twice
        scaled[chunk, pl.ds(LANES, LANES), :] = twice


def carry_tile(state_turned, first_offset, plain, scaled, tile):
    blocks = state_turned.shape[1] // LANES
    columns = []
    for side in range(TILE // LANES):
        chunk = tile * (TILE // LANES) + side
        here = plain[chunk]
        pieces = []
        for block in range(blocks):
            other = scaled[chunk, pl.ds(first_offset + block, LANES), :]
            if block == 0:
                other = jnp.where(first_offset == 0, here, other)
            pieces.append((here * other).astype(jnp.bfloat16))
        columns.append(jnp.concatenate(pieces, axis=0))
    features = jnp.concatenate(columns, axis=1)
    return jnp.dot(state_turned[...], features, preferred_element_type=jnp.float32).T


def chip_place(rows_valid):
    first = lax.div(lax.axis_index("ctx"), 2) * (2 * rows_valid)
    return lax.div(first, LANES), pl.multiple_of(lax.rem(first, LANES), 16)


def early_kernel(rows_valid, queries, own, other, turned, local, rows, plain, scaled):
    heads, padded = turned.shape[0], turned.shape[2]
    first_offset, lead = chip_place(rows_valid)
    core = lax.rem(lax.axis_index("ctx"), 2)
    count = local.shape[1]
    for head in range(heads):
        rows[pl.ds(0, LANES), :] = jnp.zeros((LANES, LANES), rows.dtype)
        spare = padded - 2 * rows_valid
        rows[pl.ds(padded - spare, spare), :] = jnp.zeros((spare, LANES), rows.dtype)
        for source, index in ((own, core), (other, 1 - core)):
            start = pl.multiple_of(lead + index * rows_valid, 16)
            rows[pl.ds(start, rows_valid), :] = source[head]
        for first in range(0, padded, 2 * LANES):
            size = min(2 * LANES, padded - first)
            turned[head, :, pl.ds(first, size)] = turned_rows(
                rows[pl.ds(first, size), :]
            ).astype(turned.dtype)
        turn_queries(
            lambda at: queries[head, pl.ds(at, LANES), :], count, plain, scaled
        )
        for tile in range(count // TILE):
            local[head, pl.ds(tile * TILE, TILE), :] = carry_tile(
                turned.at[head], first_offset, plain, scaled, tile
            )


def fill_tail(queries, steps, first, tail):
    window = queries.shape[0] - first
    count = steps.shape[0]
    tail[...] = jnp.zeros_like(tail)
    tail[pl.ds(0, window), :] = queries[pl.ds(first, window), :]
    tail[pl.ds(window, count), :] = steps


def rows_at(sizes, who, first):
    n, _, group, tok_rows, step_count, _ = sizes
    window_rows = tok_rows * group
    at = first + lax.broadcasted_iota(jnp.int32, (TILE, 1), 0)
    return jnp.where(
        at < window_rows,
        at + who * window_rows,
        at + (n - 1) * window_rows + who * (step_count // n * group),
    )


def rows_scale(sizes, counts, position):
    token = jnp.floor((position.astype(jnp.float32) + 0.5) / sizes[2])
    place_in_prompt = token + (counts[0] + 1).astype(jnp.float32)
    return 1.0 / (LANES * jnp.sqrt(place_in_prompt))


def send_tile(sizes, counts, head, first, rows, mixed, base):
    n, heads = sizes[:2]
    across = lax.rem(lax.axis_index("ctx") + 2, n)
    rows = rows * rows_scale(sizes, counts, rows_at(sizes, across, first))
    size = min(TILE, mixed.shape[0] // heads - (first - base))
    mixed[pl.ds((first - base) * heads + head, size, stride=heads), :] = rows[:size]


def remote_kernel(sizes, counts, queries, turned, partial, mixed, plain, scaled):
    heads, rows_valid = sizes[1], sizes[5]
    first_offset, _ = chip_place(rows_valid)
    count = partial.shape[0] // heads
    for head in range(heads):
        turn_queries(
            lambda at: queries[head, pl.ds(at, LANES), :], count, plain, scaled
        )
        for tile in range(count // TILE):
            rows = carry_tile(turned.at[head], first_offset, plain, scaled, tile)
            send_tile(sizes, counts, head, tile * TILE, rows, mixed, 0)
    partial[...] = mixed[...].astype(partial.dtype)


def remote_tail_kernel(
    sizes, base, early, counts, queries, steps, turned, partial, tail, mixed, plain, scaled
):
    n, heads, rows_valid = sizes[0], sizes[1], sizes[5]
    first_offset, _ = chip_place(rows_valid)
    there = lax.div(lax.rem(lax.axis_index("ctx") + 2, n), 2)
    for head in range(heads):
        turn_queries(
            lambda at: queries[head, pl.ds(base + at, LANES), :], early - base, plain, scaled
        )
        for first in range(base, early, TILE):
            rows = carry_tile(
                turned.at[head], first_offset, plain, scaled, (first - base) // TILE
            )
            send_tile(sizes, counts, head, first, rows, mixed, base)
        fill_tail(queries.at[head], steps[there, head], early, tail)
        turn_queries(lambda at: tail[pl.ds(at, LANES), :], TILE, plain, scaled)
        rows = carry_tile(turned.at[head], first_offset, plain, scaled, 0)
        send_tile(sizes, counts, head, early, rows, mixed, base)
    partial[...] = mixed[...].astype(partial.dtype)


def merge_kernel(n, own, twin, send):
    core = lax.rem(lax.axis_index("ctx"), 2)
    step_count, rows, heads = own.shape[:3]
    group = rows - heads
    per_shard = step_count // n

    def both(step, first, count):
        at = (step, pl.ds(first, count))
        return own[at] + twin[at]

    for at in range(n // 2):
        for step in range(per_shard):
            row = (at * per_shard + step) * group
            send[pl.ds(row, group)] = both((core + 2 * at) * per_shard + step, 0, group)
    for step in range(step_count):
        row = n // 2 * per_shard * group + step * heads
        send[pl.ds(row, heads)] = both(step, group, heads)


def own_tail_kernel(rows_valid, early, queries, steps, turned, local, tail, plain, scaled):
    first_offset, _ = chip_place(rows_valid)
    here = lax.div(lax.axis_index("ctx"), 2)
    for head in range(turned.shape[0]):
        fill_tail(queries.at[head], steps[here, head], early, tail)
        turn_queries(lambda at: tail[pl.ds(at, LANES), :], TILE, plain, scaled)
        local[head] = carry_tile(turned.at[head], first_offset, plain, scaled, 0)


def finish_kernel(result, got, got_tail, window_out, step_out, total, sems):
    rows = window_out.shape[0]
    for part, first in ((got, 0), (got_tail, got.shape[0])):
        at = pl.ds(first, part.shape[0])
        total[at, :] = (result[at, :] + part[...].astype(jnp.float32)).astype(total.dtype)
    copies = (
        pltpu.make_async_copy(total.at[pl.ds(0, rows)], window_out, sems.at[0]),
        pltpu.make_async_copy(
            total.at[pl.ds(rows, total.shape[0] - rows)], step_out, sems.at[1]
        ),
    )
    for copy in copies:
        copy.start()
    for copy in copies:
        copy.wait()


def state_blocks(load_keys, chunks, values, delta, keys_plain, keys_scaled, my_offset):
    for chunk in range(chunks):
        piece = turned_rows(load_keys(chunk))
        twice = piece * ROOT_TWO
        keys_plain[chunk] = piece
        keys_scaled[chunk, pl.ds(0, LANES), :] = twice
        keys_scaled[chunk, pl.ds(LANES, LANES), :] = twice

    def key_features(block):
        pieces = []
        for chunk in range(chunks):
            here = keys_plain[chunk]
            other = keys_scaled[chunk, pl.ds(my_offset + block, LANES), :]
            if block == 0:
                other = jnp.where(my_offset == 0, here, other)
            pieces.append((here * other).astype(jnp.bfloat16))
        return jnp.concatenate(pieces, axis=1)

    for block in range(delta.shape[0] // LANES):
        delta[pl.ds(block * LANES, LANES), :] = jnp.dot(
            key_features(block), values, preferred_element_type=jnp.float32
        )


def part_kernel(sizes, own_pairs, twin_pairs, delta, keys, values, keys_plain, keys_scaled):
    heads, tok_rows, rows_valid = sizes[1], sizes[3], sizes[5]
    my_offset = lax.div(lax.axis_index("ctx") * rows_valid, LANES)
    for head in range(heads):
        for plane, target in ((0, keys), (1, values)):
            target[pl.ds(0, tok_rows), :] = own_pairs[plane, head]
            target[pl.ds(tok_rows, tok_rows), :] = twin_pairs[plane, head]
        state_blocks(
            lambda chunk: keys[pl.ds(chunk * LANES, LANES), :],
            keys.shape[0] // LANES,
            values[...],
            delta.at[head],
            keys_plain,
            keys_scaled,
            my_offset,
        )


def late_kernel(
    sizes,
    counts,
    queries,
    steps,
    local_tail,
    local,
    own_pairs,
    twin_pairs,
    across_pairs,
    far_pairs,
    step_pairs,
    prior,
    part,
    result,
    state_out,
    tail,
    key_rows,
    value_rows,
    keys_plain,
    keys_scaled,
    delta,
    state,
    state_sem,
):
    n, heads, group, tok_rows, step_count, rows_valid = sizes
    me = lax.axis_index("ctx")
    twin = me + 1 - 2 * lax.rem(me, 2)
    window = n * tok_rows
    first_tail = local.shape[1]
    padded_keys = key_rows.shape[1]
    my_first = me * rows_valid
    my_offset = lax.div(my_first, LANES)
    my_lead = pl.multiple_of(lax.rem(my_first, LANES), 8)
    places = (
        (own_pairs, me),
        (twin_pairs, twin),
        (across_pairs, lax.rem(me + 2, n)),
        (far_pairs, lax.rem(twin + 2, n)),
    )

    def state_copy(head):
        return pltpu.make_async_copy(state.at[head], state_out.at[head], state_sem.at[head])

    for head in range(heads):
        for plane, target in ((0, key_rows), (1, value_rows)):
            for pairs, source in places:
                start = pl.multiple_of(source * tok_rows, 16)
                target[head, pl.ds(start, tok_rows), :] = pairs[plane, head]
            target[head, pl.ds(window, step_count), :] = step_pairs[plane, head]
            spare = padded_keys - window - step_count
            if spare > 0:
                target[head, pl.ds(window + step_count, spare), :] = jnp.zeros(
                    (spare, LANES), target.dtype
                )
        chip_rows = 2 * tok_rows
        far = pl.multiple_of((1 - lax.div(me, 2)) * chip_rows, LANES)
        chip_chunks = chip_rows // LANES
        last = padded_keys - n * tok_rows

        def load_keys(chunk):
            first = far if chunk < chip_chunks else window - chip_rows
            return key_rows[head, pl.ds(first + chunk * LANES, LANES), :]

        values = jnp.concatenate(
            [value_rows[head, pl.ds(far, chip_rows), :], value_rows[head, pl.ds(window, last), :]]
        )
        state_blocks(
            load_keys,
            (chip_rows + last) // LANES,
            values,
            delta,
            keys_plain,
            keys_scaled,
            my_offset,
        )
        mine = pl.ds(my_lead, rows_valid)
        state[head] = prior[head].astype(jnp.float32) + part[head, mine, :] + delta[mine, :]
        state_copy(head).start()

    for head in range(heads):
        fill_tail(queries.at[head], steps[lax.div(me, 2), head], first_tail, tail)
        rows_out = result.shape[0] // heads
        for first in range(0, rows_out, TILE):
            last = first >= first_tail
            rows = tail[...] if last else queries[head, pl.ds(first, TILE), :]
            scores = lax.dot_general(
                rows, key_rows[head], CONTRACT_LAST, preferred_element_type=jnp.float32
            )
            position = rows_at(sizes, me, first)
            key_index = lax.broadcasted_iota(jnp.int32, scores.shape, 1)
            weights = jnp.where(position >= key_index * group, scores * scores, 0.0)
            total = jnp.dot(
                weights.astype(jnp.bfloat16), value_rows[head], preferred_element_type=jnp.float32
            )
            carried = local_tail[head] if last else local[head, pl.ds(first, TILE), :]
            size = min(TILE, rows_out - first)
            total = (total + carried) * rows_scale(sizes, counts, position)
            result[pl.ds(first * heads + head, size, stride=heads), :] = total[:size]
    for head in range(heads):
        state_copy(head).wait()


def pick_both_kernel(ids_ref, query_table, pair_table, picked, query_sem, pair_sem):
    vocab_rows, group = query_table.shape[:2]
    first_row = lax.axis_index("ctx") * vocab_rows
    heads = pair_table.shape[1]
    picked[...] = jnp.zeros_like(picked)

    def each(step, act):
        row = ids_ref[step] - first_row

        @pl.when(jnp.logical_and(row >= 0, row < vocab_rows))
        def _():
            to_queries = picked.at[step, pl.ds(0, group)]
            to_pairs = picked.at[step, pl.ds(group, heads)]
            act(pltpu.make_async_copy(query_table.at[row], to_queries, query_sem.at[step]))
            act(pltpu.make_async_copy(pair_table.at[row], to_pairs, pair_sem.at[step]))

    for step in range(picked.shape[0]):
        each(step, lambda copy: copy.start())
    for step in range(picked.shape[0]):
        each(step, lambda copy: copy.wait())


def pick_both(ids, query_table, pair_table):
    steps, group, heads = ids.shape[0], query_table.shape[1], pair_table.shape[1]
    shape = (steps, group + heads) + pair_table.shape[2:]
    return pl.pallas_call(
        pick_both_kernel,
        out_shape=jax.ShapeDtypeStruct(shape, pair_table.dtype),
        in_specs=[
            pl.BlockSpec(memory_space=pltpu.SMEM),
            pl.BlockSpec(memory_space=pl.ANY),
            pl.BlockSpec(memory_space=pl.ANY),
        ],
        out_specs=pl.BlockSpec(memory_space=pltpu.VMEM),
        scratch_shapes=[pltpu.SemaphoreType.DMA((steps,)), pltpu.SemaphoreType.DMA((steps,))],
        compiler_params=pltpu.CompilerParams(vmem_limit_bytes=56 * 2**20),
        name="pick_both",
    )(ids, query_table, pair_table)


def vmem_call(kernel, out_shape, operands, scratch, limit, out_specs=None):
    smem = pl.BlockSpec(memory_space=pltpu.SMEM)
    vmem = pl.BlockSpec(memory_space=pltpu.VMEM)
    return pl.pallas_call(
        kernel,
        out_shape=out_shape,
        in_specs=[smem if operand.ndim == 1 else vmem for operand in operands],
        out_specs=out_specs if out_specs is not None else jax.tree.map(lambda _: vmem, out_shape),
        scratch_shapes=scratch,
        compiler_params=pltpu.CompilerParams(vmem_limit_bytes=limit * 2**20),
    )(*operands)


def turn_scratch(columns):
    chunks = columns // LANES
    return [
        pltpu.VMEM((chunks, LANES, LANES), jnp.float32),
        pltpu.VMEM((chunks, 2 * LANES, LANES), jnp.float32),
    ]


def on_device_exchange(
    queries, keys_values, prior, counts, continuation, query_table, pair_table
):
    tok_rows, heads, group, head_size = queries.shape
    n = lax.axis_size("ctx")
    step_count = continuation.shape[0]
    per_shard = step_count // n
    step_rows = per_shard * group
    rows_valid = prior.shape[1]
    window_rows = tok_rows * group
    early = window_rows // TILE * TILE
    rows_chip = 2 * rows_valid
    padded = max(
        round_up(chip_at * rows_chip % LANES + rows_chip, LANES) for chip_at in range(n // 2)
    )
    blocks = max(
        round_up(source * rows_valid % LANES + rows_valid, LANES) // LANES for source in range(n)
    )
    padded_keys = round_up(n * tok_rows + step_count, LANES)
    bf16, f32 = jnp.bfloat16, jnp.float32
    sizes = (n, heads, group, tok_rows, step_count, rows_valid)
    shape = jax.ShapeDtypeStruct

    def swap_across(value):
        return lax.ppermute(value, "ctx", [(i, (i + 2) % n) for i in range(n)])

    def swap_twin(value):
        return lax.ppermute(value, "ctx", [(i, i ^ 1) for i in range(n)])

    def query_planes(value):
        return value.transpose(1, 0, 2, 3).reshape(heads, -1, head_size)

    def pair_planes(value):
        return value.transpose(2, 1, 0, 3)

    across_queries = swap_across(queries)
    across_pairs = swap_across(keys_values)
    twin_prior = swap_twin(prior)
    twin_pairs = swap_twin(keys_values)
    picked = pick_both(continuation, query_table.transpose(0, 2, 1, 3), pair_table)
    twin_picked = swap_twin(picked)
    send = vmem_call(
        functools.partial(merge_kernel, n),
        shape((n // 2 * step_rows + step_count * heads, 2, head_size), bf16),
        (picked, twin_picked),
        [],
        4,
    )
    steps = send + swap_across(send)
    step_pairs = pair_planes(steps[n // 2 * step_rows :].reshape(step_count, heads, 2, head_size))
    step_queries = steps[: n // 2 * step_rows].reshape(n // 2, step_rows, heads, head_size)
    step_queries = step_queries.transpose(0, 2, 1, 3)

    own_rows = query_planes(queries)
    turned, local = vmem_call(
        functools.partial(early_kernel, rows_valid),
        (shape((heads, LANES, padded), bf16), shape((heads, early, LANES), f32)),
        (own_rows, prior, twin_prior),
        [pltpu.VMEM((padded, LANES), bf16)] + turn_scratch(early),
        16,
    )
    own_planes, twin_planes = pair_planes(keys_values), pair_planes(twin_pairs)
    chip_chunks = 2 * tok_rows // LANES
    part = vmem_call(
        functools.partial(part_kernel, sizes),
        shape((heads, blocks * LANES, LANES), f32),
        (own_planes, twin_planes),
        [
            pltpu.VMEM((2 * tok_rows, LANES), bf16),
            pltpu.VMEM((2 * tok_rows, LANES), bf16),
            pltpu.VMEM((chip_chunks, LANES, LANES), f32),
            pltpu.VMEM((chip_chunks, 2 * LANES, LANES), f32),
        ],
        16,
    )
    across_rows = query_planes(across_queries)
    half = (early // TILE + 1) // 2 * TILE
    partial = vmem_call(
        functools.partial(remote_kernel, sizes),
        shape((heads * half, LANES), bf16),
        (counts, across_rows, turned),
        [pltpu.VMEM((heads * half, LANES), f32)] + turn_scratch(half),
        16,
    )
    got = swap_across(partial)
    rest = heads * (window_rows + step_rows - half)
    partial_tail = vmem_call(
        functools.partial(remote_tail_kernel, sizes, half, early),
        shape((rest, LANES), bf16),
        (counts, across_rows, step_queries, turned),
        [pltpu.VMEM((TILE, LANES), bf16), pltpu.VMEM((rest, LANES), f32)]
        + turn_scratch(max(early - half, TILE)),
        16,
    )
    got_tail = swap_across(partial_tail)
    far_pairs = swap_twin(across_pairs)
    local_tail = vmem_call(
        functools.partial(own_tail_kernel, rows_valid, early),
        shape((heads, TILE, LANES), f32),
        (own_rows, step_queries, turned),
        [pltpu.VMEM((TILE, LANES), bf16)] + turn_scratch(TILE),
        16,
    )
    vmem = pl.BlockSpec(memory_space=pltpu.VMEM)
    chunks = (padded_keys - (n - 2) * tok_rows) // LANES
    result, decode_state = vmem_call(
        functools.partial(late_kernel, sizes),
        (
            shape((heads * (window_rows + step_rows), LANES), f32),
            shape((heads, rows_valid, LANES), f32),
        ),
        (
            counts,
            own_rows,
            step_queries,
            local_tail,
            local,
            own_planes,
            twin_planes,
            pair_planes(across_pairs),
            pair_planes(far_pairs),
            step_pairs,
            prior,
            part,
        ),
        [
            pltpu.VMEM((TILE, LANES), bf16),
            pltpu.VMEM((heads, padded_keys, LANES), bf16),
            pltpu.VMEM((heads, padded_keys, LANES), bf16),
            pltpu.VMEM((chunks, LANES, LANES), f32),
            pltpu.VMEM((chunks, 2 * LANES, LANES), f32),
            pltpu.VMEM((blocks * LANES, LANES), f32),
            pltpu.VMEM((heads, rows_valid, LANES), f32),
            pltpu.SemaphoreType.DMA((heads,)),
        ],
        24,
        (vmem, pl.BlockSpec(memory_space=pl.ANY)),
    )
    hbm = pl.BlockSpec(memory_space=pl.ANY)
    readout, decode_out = vmem_call(
        finish_kernel,
        (shape((heads * window_rows, LANES), bf16), shape((heads * step_rows, LANES), bf16)),
        (result, got, got_tail),
        [pltpu.VMEM(result.shape, bf16), pltpu.SemaphoreType.DMA((2,))],
        8,
        (hbm, hbm),
    )
    readout = readout.reshape(tok_rows, group, heads, head_size)
    decode_out = decode_out.reshape(per_shard, group, heads, head_size)
    return (readout.transpose(0, 2, 1, 3), decode_out.transpose(0, 2, 1, 3), decode_state)


def solution(mesh):
    in_specs = (
        P(("groups", "ctx"), "head", None, None),
        P(("groups", "ctx"), "head", None, None),
        P(("groups", "head"), "ctx", None),
        P("groups"),
        P("groups"),
        P("ctx", "head", None, None),
        P("ctx", "head", None, None),
    )
    out_specs = (
        P(("groups", "ctx"), "head", None, None),
        P(("groups", "ctx"), "head", None, None),
        P(("groups", "head"), "ctx", None),
    )

    def on_device(*arguments):
        n, rows_valid = lax.axis_size("ctx"), arguments[2].shape[1]
        if n == 4 and rows_valid % 16 == 0 and 2 * arguments[0].shape[0] % LANES == 0:
            return on_device_exchange(*arguments)
        return on_device_gather(*arguments)

    return jax.shard_map(
        on_device, mesh=mesh, in_specs=in_specs, out_specs=out_specs, check_vma=False
    )
```

```python
import functools

import jax
import jax.numpy as jnp
from jax import lax
from jax.experimental import pallas as pl
from jax.experimental.pallas import tpu as pltpu
from jax.sharding import PartitionSpec as P


ROOT_TWO = 2.0**0.5
MESH = pl.DeviceIdType.MESH
TILE = 256
LANES = 128
PIECES = 4
CONTRACT_LAST = (((1,), (1,)), ((), ()))


def round_up(number, multiple):
    return (number + multiple - 1) // multiple * multiple


def pick_kernel(ids_ref, query_table, pair_table, query_out, pair_out, query_sem, pair_sem):
    vocab_rows = query_table.shape[0]
    first_row = lax.axis_index("ctx") * vocab_rows
    query_out[...] = jnp.zeros_like(query_out)
    pair_out[...] = jnp.zeros_like(pair_out)

    def each(step, act):
        row = ids_ref[step] - first_row

        @pl.when(jnp.logical_and(row >= 0, row < vocab_rows))
        def _():
            act(pltpu.make_async_copy(query_table.at[row], query_out.at[step], query_sem.at[step]))
            act(pltpu.make_async_copy(pair_table.at[row], pair_out.at[step], pair_sem.at[step]))

    for step in range(query_out.shape[0]):
        each(step, lambda copy: copy.start())
    for step in range(query_out.shape[0]):
        each(step, lambda copy: copy.wait())


def pick_rows(ids, query_table, pair_table):
    steps = ids.shape[0]
    return pl.pallas_call(
        pick_kernel,
        out_shape=(
            jax.ShapeDtypeStruct((steps,) + query_table.shape[1:], query_table.dtype),
            jax.ShapeDtypeStruct((steps,) + pair_table.shape[1:], pair_table.dtype),
        ),
        in_specs=[
            pl.BlockSpec(memory_space=pltpu.SMEM),
            pl.BlockSpec(memory_space=pl.ANY),
            pl.BlockSpec(memory_space=pl.ANY),
        ],
        out_specs=(
            pl.BlockSpec(memory_space=pltpu.VMEM),
            pl.BlockSpec(memory_space=pltpu.VMEM),
        ),
        scratch_shapes=[pltpu.SemaphoreType.DMA((steps,)), pltpu.SemaphoreType.DMA((steps,))],
        name="pick_rows",
    )(ids, query_table, pair_table)


def main_kernel(
    sizes,
    counts,
    queries,
    blob,
    prior,
    window_out,
    step_out,
    state_out,
    out,
    state,
    land_blob,
    land_prior,
    query_rows,
    query_plain,
    query_scaled,
    prior_turned,
    total_turned,
    step_rows,
    key_rows,
    value_rows,
    turned,
    blob_send,
    blob_recv,
    prior_send,
    prior_recv,
    local_sem,
):
    n, heads, group, tok_rows, step_count, rows_valid = sizes
    chips = n // 2
    per_shard = step_count // n
    window_rows = tok_rows * group
    window = n * tok_rows
    prior_rows = prior.shape[1]
    shifted = prior_rows == rows_valid
    state_rows = state.shape[1]
    blocks = land_prior.shape[2] // LANES
    row_tiles = out.shape[1] // TILE
    padded_keys = key_rows.shape[1]
    me = lax.axis_index("ctx")
    core = lax.rem(me, 2)
    partner = me + 1 - 2 * core

    def across(step):
        return lax.rem(me + 2 * step, n)

    def twin(index):
        return index + 1 - 2 * lax.rem(index, 2)

    barrier = pltpu.get_barrier_semaphore()
    pl.semaphore_signal(barrier, inc=1, device_id={"ctx": partner}, device_id_type=MESH)
    for step in range(1, chips):
        pl.semaphore_signal(barrier, inc=1, device_id={"ctx": across(step)}, device_id_type=MESH)
    pl.semaphore_wait(barrier, chips)

    def blob_copy(src, source, slot, target):
        return pltpu.make_async_remote_copy(
            src_ref=src,
            dst_ref=land_blob.at[source],
            send_sem=blob_send.at[slot],
            recv_sem=blob_recv.at[source],
            device_id={"ctx": target},
            device_id_type=MESH,
        )

    def landing(source):
        first = pl.multiple_of(lax.rem(source * rows_valid, LANES), 16) if shifted else 0
        return pl.ds(first, prior_rows)

    def prior_copy(src, source, head, slot, target):
        return pltpu.make_async_remote_copy(
            src_ref=src,
            dst_ref=land_prior.at[source, head, landing(source)],
            send_sem=prior_send.at[slot, head],
            recv_sem=prior_recv.at[source, head],
            device_id={"ctx": target},
            device_id_type=MESH,
        )

    def blob_own(slot):
        return blob_copy(blob, me, slot, partner if slot == 0 else across(slot))

    def blob_forward(step):
        source = across(step)
        return blob_copy(land_blob.at[source], source, chips - 1 + step, partner)

    def prior_own(slot, head):
        target = partner if slot == 0 else across(slot)
        return prior_copy(prior.at[head], me, head, slot, target)

    def prior_forward(step, head):
        source = across(step)
        return prior_copy(
            land_prior.at[source, head, landing(source)],
            source,
            head,
            chips - 1 + step,
            partner,
        )

    for slot in list(range(1, chips)) + [0]:
        blob_own(slot).start()
    for head in range(heads):
        for slot in list(range(1, chips)) + [0]:
            prior_own(slot, head).start()
    own_blob = pltpu.make_async_copy(blob, land_blob.at[me], local_sem.at[0])
    own_prior = pltpu.make_async_copy(
        prior, land_prior.at[me, :, landing(me)], local_sem.at[1]
    )
    own_blob.start()
    own_prior.start()

    if shifted:
        for source in range(n):
            lead_rows = source * rows_valid % LANES
            for first, last in (
                (0, lead_rows),
                (lead_rows + prior_rows, blocks * LANES),
            ):
                if last > first:
                    for head in range(heads):
                        land_prior[source, head, pl.ds(first, last - first), :] = jnp.zeros(
                            (last - first, LANES), jnp.bfloat16
                        )
    total_turned[...] = jnp.zeros_like(total_turned)
    for head in range(heads):
        query_rows[head, pl.ds(0, window_rows), :] = queries[head]
        query_rows[head, pl.ds(window_rows, out.shape[1] - window_rows), :] = jnp.zeros(
            (out.shape[1] - window_rows, LANES), jnp.bfloat16
        )
        spare = padded_keys - window - step_count
        if spare > 0:
            key_rows[head, pl.ds(window + step_count, spare), :] = jnp.zeros(
                (spare, LANES), jnp.bfloat16
            )
            value_rows[head, pl.ds(window + step_count, spare), :] = jnp.zeros(
                (spare, LANES), jnp.bfloat16
            )

    def place(source):
        first = source * rows_valid
        return lax.div(first, LANES), lax.rem(first, LANES)

    identity = (
        lax.broadcasted_iota(jnp.int32, (LANES, LANES), 0)
        == lax.broadcasted_iota(jnp.int32, (LANES, LANES), 1)
    ).astype(jnp.bfloat16)
    contract_last = (((1,), (1,)), ((), ()))

    def transposed(rows):
        return lax.dot_general(identity, rows, contract_last, preferred_element_type=jnp.float32)

    chunks_per_tile = TILE // LANES

    def turn_queries(head, first_tile, last_tile):
        for chunk in range(first_tile * chunks_per_tile, last_tile * chunks_per_tile):
            piece = transposed(query_rows[head, pl.ds(chunk * LANES, LANES), :])
            scaled = piece * ROOT_TWO
            query_plain[head, chunk] = piece
            query_scaled[head, chunk, pl.ds(0, LANES), :] = scaled
            query_scaled[head, chunk, pl.ds(LANES, LANES), :] = scaled

    def carry_tile(source, head, tile):
        first_offset, _ = place(source)
        columns = []
        for side in range(chunks_per_tile):
            chunk = tile * chunks_per_tile + side
            here = query_plain[head, chunk]
            pieces = []
            for block in range(blocks):
                row = lax.rem(first_offset + block, LANES)
                other = query_scaled[head, chunk, pl.ds(row, LANES), :]
                if block == 0:
                    other = jnp.where(first_offset == 0, here, other)
                pieces.append((here * other).astype(jnp.bfloat16))
            columns.append(jnp.concatenate(pieces, axis=0))
        features = jnp.concatenate(columns, axis=1)
        total_turned[head, tile] += jnp.dot(
            prior_turned[...], features, preferred_element_type=jnp.float32
        )

    def carry(source, head, first_tile, last_tile):
        prior_turned[...] = transposed(land_prior[source, head]).astype(jnp.bfloat16)

        @pl.loop(first_tile, last_tile)
        def _(tile):
            carry_tile(source, head, tile)

    full_tiles = window_rows // TILE
    own_prior.wait()
    for head in range(heads):
        turn_queries(head, 0, full_tiles)
        carry(me, head, 0, full_tiles)

    own_blob.wait()
    blob_copy(blob, partner, 0, partner).wait_recv()
    for step in range(1, chips):
        blob_copy(blob, across(step), 0, partner).wait_recv()
        blob_forward(step).start()
    for step in range(1, chips):
        blob_copy(blob, twin(across(step)), 0, partner).wait_recv()

    for head in range(heads):
        for source in range(n):
            key_rows[head, pl.ds(source * tok_rows, tok_rows), :] = land_blob[
                source, head, pl.ds(0, tok_rows), :
            ]
            value_rows[head, pl.ds(source * tok_rows, tok_rows), :] = land_blob[
                source, heads + head, pl.ds(0, tok_rows), :
            ]

        def picked(plane, first, count):
            total = land_blob[0, plane, pl.ds(first, count), :].astype(jnp.float32)
            for source in range(1, n):
                total += land_blob[source, plane, pl.ds(first, count), :].astype(jnp.float32)
            return total

        key_rows[head, pl.ds(window, step_count), :] = picked(head, tok_rows, step_count).astype(
            jnp.bfloat16
        )
        value_rows[head, pl.ds(window, step_count), :] = picked(
            heads + head, tok_rows, step_count
        ).astype(jnp.bfloat16)
        half = step_count * group // 2
        for side in range(2):
            step_rows[head, pl.ds(side * half, half), :] = picked(
                2 * head + side, tok_rows + step_count, half
            )
        own_steps = per_shard * group
        own_rows = step_rows[head, pl.ds(me * own_steps, own_steps), :]
        query_rows[head, pl.ds(window_rows, own_steps), :] = own_rows.astype(jnp.bfloat16)
        turn_queries(head, full_tiles, row_tiles)

    for head in range(heads):
        carry(me, head, full_tiles, row_tiles)
        prior_copy(prior.at[head], partner, head, 0, partner).wait_recv()
        carry(partner, head, 0, row_tiles)

    def state_copy(head):
        return pltpu.make_async_copy(state.at[head], state_out.at[head], local_sem.at[2 + head])

    def positions(tile):
        local = tile * TILE + lax.broadcasted_iota(jnp.int32, (TILE, 1), 0)
        return jnp.where(
            local < window_rows,
            local + me * window_rows,
            local - window_rows + window * group + me * (per_shard * group),
        )

    first_offset, lead = place(me)
    for head in range(heads):
        keys_turned = transposed(key_rows[head])
        chunks = padded_keys // LANES
        for chunk in range(chunks):
            piece = keys_turned[:, chunk * LANES : (chunk + 1) * LANES]
            turned[head, chunk, pl.ds(0, LANES), :] = piece
            turned[head, chunk, pl.ds(LANES, LANES), :] = piece

        def state_block(block):
            row = lax.broadcasted_iota(jnp.int32, (LANES, LANES), 0)
            early = row < LANES - lead
            plain = jnp.logical_and(early, first_offset + block == 0)
            factor = jnp.where(plain, 1.0, ROOT_TWO)
            near_row = lax.rem(lead + first_offset + block, LANES)
            far_row = lax.rem(lead + first_offset + block + 1, LANES)
            pieces = []
            for chunk in range(chunks):
                here = turned[head, chunk, pl.ds(lead, LANES), :]
                near = turned[head, chunk, pl.ds(near_row, LANES), :]
                far = turned[head, chunk, pl.ds(far_row, LANES), :]
                both = jnp.where(early, near, far) * factor
                pieces.append((here * both).astype(jnp.bfloat16))
            features = jnp.concatenate(pieces, axis=1)
            return jnp.dot(features, value_rows[head], preferred_element_type=jnp.float32)

        def before(rows):
            return prior[head, rows, :].astype(jnp.float32) if shifted else 0.0

        whole_blocks = state_rows // LANES

        @pl.loop(0, whole_blocks)
        def _(block):
            rows = pl.ds(pl.multiple_of(block * LANES, LANES), LANES)
            state[head, rows, :] = before(rows) + state_block(block)

        rest = state_rows - whole_blocks * LANES
        if rest > 0:
            rows = pl.ds(whole_blocks * LANES, rest)
            state[head, rows, :] = before(rows) + state_block(whole_blocks)[:rest]
        state_copy(head).start()

        @pl.loop(0, row_tiles)
        def _(tile):
            rows = pl.ds(pl.multiple_of(tile * TILE, TILE), TILE)
            scores = lax.dot_general(
                query_rows[head, rows, :],
                key_rows[head],
                contract_last,
                preferred_element_type=jnp.float32,
            )
            position = positions(tile)
            key_index = lax.broadcasted_iota(jnp.int32, scores.shape, 1)
            allowed = position >= key_index * group
            weights = jnp.where(allowed, scores * scores, 0.0).astype(jnp.bfloat16)
            out[head, rows, :] = jnp.dot(
                weights, value_rows[head], preferred_element_type=jnp.float32
            )

    for step in range(1, chips):
        source = across(step)
        for head in range(heads):
            prior_copy(prior.at[head], source, head, 0, partner).wait_recv()
            prior_forward(step, head).start()
            carry(source, head, 0, row_tiles)
            prior_copy(prior.at[head], twin(source), head, 0, partner).wait_recv()
            carry(twin(source), head, 0, row_tiles)

    for head in range(heads):
        for tile in range(row_tiles):
            first = tile * TILE
            token = jnp.floor((positions(tile).astype(jnp.float32) + 0.5) / group)
            place_in_prompt = token + (counts[0] + 1).astype(jnp.float32)
            scale = 1.0 / (LANES * jnp.sqrt(place_in_prompt))
            total = out[head, pl.ds(first, TILE), :] + total_turned[head, tile].T
            total = (total * scale).astype(jnp.bfloat16)
            split = min(max(window_rows - first, 0), TILE)
            if split > 0:
                window_out[head, pl.ds(first, split), :] = total[:split]
            if split < TILE:
                step_out[head, pl.ds(first + split - window_rows, TILE - split), :] = total[split:]
        state_copy(head).wait()

    for slot in range(chips):
        blob_own(slot).wait_send()
        for head in range(heads):
            prior_own(slot, head).wait_send()
    for step in range(1, chips):
        blob_forward(step).wait_send()
        for head in range(heads):
            prior_forward(step, head).wait_send()


def combine(sizes, counts, queries, blob, prior, out_rows):
    n, heads, group, tok_rows, step_count, rows_valid = sizes
    window_rows = tok_rows * group
    lead = max(source * rows_valid % LANES for source in range(n))
    padded_rows = round_up(lead + rows_valid, LANES)
    chunks = out_rows // LANES
    state_rows = round_up(rows_valid, 8)
    padded_keys = round_up(n * tok_rows + step_count, LANES)
    slots = 2 * (n // 2) - 1
    vmem = pl.BlockSpec(memory_space=pltpu.VMEM)
    return pl.pallas_call(
        functools.partial(main_kernel, sizes),
        out_shape=(
            jax.ShapeDtypeStruct((heads, window_rows, LANES), jnp.bfloat16),
            jax.ShapeDtypeStruct((heads, out_rows - window_rows, LANES), jnp.bfloat16),
            jax.ShapeDtypeStruct((heads, state_rows, LANES), jnp.float32),
        ),
        in_specs=[pl.BlockSpec(memory_space=pltpu.SMEM)] + [vmem] * 3,
        out_specs=(vmem, vmem, pl.BlockSpec(memory_space=pl.ANY)),
        scratch_shapes=[
            pltpu.VMEM((heads, out_rows, LANES), jnp.float32),
            pltpu.VMEM((heads, state_rows, LANES), jnp.float32),
            pltpu.VMEM((n,) + blob.shape, jnp.bfloat16),
            pltpu.VMEM((n, heads, padded_rows, LANES), jnp.bfloat16),
            pltpu.VMEM((heads, out_rows, LANES), jnp.bfloat16),
            pltpu.VMEM((heads, chunks, LANES, LANES), jnp.float32),
            pltpu.VMEM((heads, chunks, 2 * LANES, LANES), jnp.float32),
            pltpu.VMEM((LANES, padded_rows), jnp.bfloat16),
            pltpu.VMEM((heads, out_rows // TILE, LANES, TILE), jnp.float32),
            pltpu.VMEM((heads, step_count * group, LANES), jnp.float32),
            pltpu.VMEM((heads, padded_keys, LANES), jnp.bfloat16),
            pltpu.VMEM((heads, padded_keys, LANES), jnp.bfloat16),
            pltpu.VMEM((heads, padded_keys // LANES, 2 * LANES, LANES), jnp.float32),
            pltpu.SemaphoreType.DMA((slots,)),
            pltpu.SemaphoreType.DMA((n,)),
            pltpu.SemaphoreType.DMA((slots, heads)),
            pltpu.SemaphoreType.DMA((n, heads)),
            pltpu.SemaphoreType.DMA((2 + heads,)),
        ],
        compiler_params=pltpu.CompilerParams(
            collective_id=0, has_side_effects=True, vmem_limit_bytes=48 * 2**20
        ),
        name="combine",
    )(counts, queries, blob, prior)


def on_device_gather(queries, keys_values, prior_state, counts, continuation, query_table, pair_table):
    tok_rows, heads, group, head_size = queries.shape
    n = lax.axis_size("ctx")
    shard_index = lax.axis_index("ctx")
    step_count = continuation.shape[0]
    per_shard = step_count // n
    rows_valid = prior_state.shape[1]

    query_pick, pair_pick = pick_rows(
        continuation, query_table.transpose(0, 2, 1, 3), pair_table
    )

    window_planes = keys_values.transpose(2, 1, 0, 3).reshape(2 * heads, tok_rows, head_size)
    step_planes = pair_pick.transpose(2, 1, 0, 3)
    step_planes = step_planes.reshape(2 * heads, step_count, head_size)
    query_planes = query_pick.transpose(2, 0, 1, 3).reshape(
        2 * heads, step_count * group // 2, head_size
    )
    blob = jnp.concatenate([window_planes, step_planes, query_planes], axis=1)
    query_planes = queries.transpose(1, 0, 2, 3).reshape(heads, tok_rows * group, head_size)
    prior = prior_state
    if rows_valid % 16 != 0:
        leads = [source * rows_valid % LANES for source in range(n)]
        prior = lax.dynamic_update_slice(
            jnp.zeros((heads, round_up(max(leads) + rows_valid, LANES), LANES), prior.dtype),
            prior_state,
            (0, shard_index * rows_valid % LANES, 0),
        )
    out_rows = round_up((tok_rows + per_shard) * group, TILE)
    sizes = (n, heads, group, tok_rows, step_count, rows_valid)
    window_out, step_out, state = combine(sizes, counts, query_planes, blob, prior, out_rows)

    decode_state = state
    if rows_valid % 16 != 0:
        decode_state = prior_state.astype(jnp.float32) + state[:, :rows_valid]
    readout = window_out.reshape(heads, tok_rows, group, head_size).transpose(1, 0, 2, 3)
    decode_out = step_out[:, : per_shard * group]
    decode_out = decode_out.reshape(heads, per_shard, group, head_size).transpose(1, 0, 2, 3)
    return (readout, decode_out, decode_state)


def identity():
    row = lax.broadcasted_iota(jnp.int32, (LANES, LANES), 0)
    column = lax.broadcasted_iota(jnp.int32, (LANES, LANES), 1)
    return (row == column).astype(jnp.bfloat16)


def turned_rows(rows):
    return lax.dot_general(
        identity(), rows, CONTRACT_LAST, preferred_element_type=jnp.float32
    )


def turn_queries(load, count, plain, scaled):
    for chunk in range(count // LANES):
        piece = turned_rows(load(chunk * LANES))
        twice = piece * ROOT_TWO
        plain[chunk] = piece
        scaled[chunk, pl.ds(0, LANES), :] = twice
        scaled[chunk, pl.ds(LANES, LANES), :] = twice


def carry_tile(state_turned, first_offset, plain, scaled, tile):
    blocks = state_turned.shape[1] // LANES
    columns = []
    for side in range(TILE // LANES):
        chunk = tile * (TILE // LANES) + side
        here = plain[chunk]
        pieces = []
        for block in range(blocks):
            other = scaled[chunk, pl.ds(first_offset + block, LANES), :]
            if block == 0:
                other = jnp.where(first_offset == 0, here, other)
            pieces.append((here * other).astype(jnp.bfloat16))
        columns.append(jnp.concatenate(pieces, axis=0))
    features = jnp.concatenate(columns, axis=1)
    return jnp.dot(state_turned[...], features, preferred_element_type=jnp.float32).T


def chip_place(rows_valid):
    first = lax.div(lax.axis_index("ctx"), 2) * (2 * rows_valid)
    return lax.div(first, LANES), pl.multiple_of(lax.rem(first, LANES), 16)


def early_kernel(rows_valid, queries, own, other, turned, local, rows, plain, scaled):
    heads, padded = turned.shape[0], turned.shape[2]
    first_offset, lead = chip_place(rows_valid)
    core = lax.rem(lax.axis_index("ctx"), 2)
    count = local.shape[1]
    for head in range(heads):
        rows[pl.ds(0, LANES), :] = jnp.zeros((LANES, LANES), rows.dtype)
        spare = padded - 2 * rows_valid
        rows[pl.ds(padded - spare, spare), :] = jnp.zeros((spare, LANES), rows.dtype)
        for source, index in ((own, core), (other, 1 - core)):
            start = pl.multiple_of(lead + index * rows_valid, 16)
            rows[pl.ds(start, rows_valid), :] = source[head]
        for first in range(0, padded, 2 * LANES):
            size = min(2 * LANES, padded - first)
            turned[head, :, pl.ds(first, size)] = turned_rows(
                rows[pl.ds(first, size), :]
            ).astype(turned.dtype)
        turn_queries(
            lambda at: queries[head, pl.ds(at, LANES), :], count, plain, scaled
        )
        for tile in range(count // TILE):
            local[head, pl.ds(tile * TILE, TILE), :] = carry_tile(
                turned.at[head], first_offset, plain, scaled, tile
            )


def fill_tail(queries, steps, first, tail):
    window = queries.shape[0] - first
    count = steps.shape[0]
    tail[...] = jnp.zeros_like(tail)
    tail[pl.ds(0, window), :] = queries[pl.ds(first, window), :]
    tail[pl.ds(window, count), :] = steps


def rows_at(sizes, who, first):
    n, _, group, tok_rows, step_count, _ = sizes
    window_rows = tok_rows * group
    at = first + lax.broadcasted_iota(jnp.int32, (TILE, 1), 0)
    return jnp.where(
        at < window_rows,
        at + who * window_rows,
        at + (n - 1) * window_rows + who * (step_count // n * group),
    )


def rows_scale(sizes, counts, position):
    token = jnp.floor((position.astype(jnp.float32) + 0.5) / sizes[2])
    place_in_prompt = token + counts[pl.ds(0, 1), pl.ds(0, 1)]
    return 1.0 / (LANES * jnp.sqrt(place_in_prompt))


def send_tile(sizes, counts, head, first, rows, mixed, base):
    n, heads = sizes[:2]
    across = lax.rem(lax.axis_index("ctx") + 2, n)
    rows = rows * rows_scale(sizes, counts, rows_at(sizes, across, first))
    size = min(TILE, mixed.shape[0] // heads - (first - base))
    mixed[pl.ds((first - base) * heads + head, size, stride=heads), :] = rows[:size]


def remote_kernel(sizes, counts, queries, turned, partial, mixed, plain, scaled):
    heads, rows_valid = sizes[1], sizes[5]
    first_offset, _ = chip_place(rows_valid)
    count = partial.shape[0] // heads
    for head in range(heads):
        turn_queries(
            lambda at: queries[head, pl.ds(at, LANES), :], count, plain, scaled
        )
        for tile in range(count // TILE):
            rows = carry_tile(turned.at[head], first_offset, plain, scaled, tile)
            send_tile(sizes, counts, head, tile * TILE, rows, mixed, 0)
    partial[...] = mixed[...].astype(partial.dtype)


def remote_tail_kernel(
    sizes, base, early, counts, queries, steps, turned, partial, tail, mixed, plain, scaled
):
    n, heads, rows_valid = sizes[0], sizes[1], sizes[5]
    first_offset, _ = chip_place(rows_valid)
    there = lax.div(lax.rem(lax.axis_index("ctx") + 2, n), 2)
    for head in range(heads):
        turn_queries(
            lambda at: queries[head, pl.ds(base + at, LANES), :], early - base, plain, scaled
        )
        for first in range(base, early, TILE):
            rows = carry_tile(
                turned.at[head], first_offset, plain, scaled, (first - base) // TILE
            )
            send_tile(sizes, counts, head, first, rows, mixed, base)
        fill_tail(queries.at[head], steps[there, head], early, tail)
        turn_queries(lambda at: tail[pl.ds(at, LANES), :], TILE, plain, scaled)
        rows = carry_tile(turned.at[head], first_offset, plain, scaled, 0)
        send_tile(sizes, counts, head, early, rows, mixed, base)
    partial[...] = mixed[...].astype(partial.dtype)


def merge_kernel(n, own, twin, send):
    core = lax.rem(lax.axis_index("ctx"), 2)
    step_count, rows, heads = own.shape[:3]
    group = rows - heads
    per_shard = step_count // n

    def both(step, first, count):
        at = (step, pl.ds(first, count))
        return own[at] + twin[at]

    for at in range(n // 2):
        for step in range(per_shard):
            row = (at * per_shard + step) * group
            send[pl.ds(row, group)] = both((core + 2 * at) * per_shard + step, 0, group)
    for step in range(step_count):
        row = n // 2 * per_shard * group + step * heads
        send[pl.ds(row, heads)] = both(step, group, heads)


def own_tail_kernel(rows_valid, early, queries, steps, turned, local, tail, plain, scaled):
    first_offset, _ = chip_place(rows_valid)
    here = lax.div(lax.axis_index("ctx"), 2)
    for head in range(turned.shape[0]):
        fill_tail(queries.at[head], steps[here, head], early, tail)
        turn_queries(lambda at: tail[pl.ds(at, LANES), :], TILE, plain, scaled)
        local[head] = carry_tile(turned.at[head], first_offset, plain, scaled, 0)


def finish_kernel(result, got, got_tail, window_out, step_out, total, sems):
    split = window_out.shape[0]
    piece = round_up(total.shape[0], 16 * PIECES) // PIECES
    cuts = sorted({*range(0, total.shape[0], piece), got.shape[0], split, total.shape[0]})
    copies = []
    for first, last in zip(cuts, cuts[1:]):
        at = pl.ds(first, last - first)
        part, base = (got, 0) if last <= got.shape[0] else (got_tail, got.shape[0])
        rows = part[pl.ds(first - base, last - first), :].astype(jnp.float32)
        total[at, :] = (result[at, :] + rows).astype(total.dtype)
        target, base = (window_out, 0) if last <= split else (step_out, split)
        copy = pltpu.make_async_copy(
            total.at[at],
            target.at[pl.ds(first - base, last - first)],
            sems.at[len(copies)],
        )
        copy.start()
        copies.append(copy)
    for copy in copies:
        copy.wait()


def state_blocks(load_keys, chunks, values, delta, keys_plain, keys_scaled, my_offset):
    for chunk in range(chunks):
        piece = turned_rows(load_keys(chunk))
        twice = piece * ROOT_TWO
        keys_plain[chunk] = piece
        keys_scaled[chunk, pl.ds(0, LANES), :] = twice
        keys_scaled[chunk, pl.ds(LANES, LANES), :] = twice

    def key_features(block):
        pieces = []
        for chunk in range(chunks):
            here = keys_plain[chunk]
            other = keys_scaled[chunk, pl.ds(my_offset + block, LANES), :]
            if block == 0:
                other = jnp.where(my_offset == 0, here, other)
            pieces.append((here * other).astype(jnp.bfloat16))
        return jnp.concatenate(pieces, axis=1)

    for block in range(delta.shape[0] // LANES):
        delta[pl.ds(block * LANES, LANES), :] = jnp.dot(
            key_features(block), values, preferred_element_type=jnp.float32
        )


def part_kernel(sizes, own_pairs, twin_pairs, delta, keys, values, keys_plain, keys_scaled):
    heads, tok_rows, rows_valid = sizes[1], sizes[3], sizes[5]
    my_offset = lax.div(lax.axis_index("ctx") * rows_valid, LANES)
    for head in range(heads):
        for plane, target in ((0, keys), (1, values)):
            target[pl.ds(0, tok_rows), :] = own_pairs[plane, head]
            target[pl.ds(tok_rows, tok_rows), :] = twin_pairs[plane, head]
        state_blocks(
            lambda chunk: keys[pl.ds(chunk * LANES, LANES), :],
            keys.shape[0] // LANES,
            values[...],
            delta.at[head],
            keys_plain,
            keys_scaled,
            my_offset,
        )


def late_kernel(
    sizes,
    counts,
    queries,
    steps,
    local_tail,
    local,
    own_pairs,
    twin_pairs,
    across_pairs,
    far_pairs,
    step_pairs,
    prior,
    part,
    result,
    state_out,
    tail,
    key_rows,
    value_rows,
    keys_plain,
    keys_scaled,
    delta,
    state,
    state_sem,
):
    n, heads, group, tok_rows, step_count, rows_valid = sizes
    me = lax.axis_index("ctx")
    twin = me + 1 - 2 * lax.rem(me, 2)
    window = n * tok_rows
    first_tail = local.shape[1]
    padded_keys = key_rows.shape[1]
    my_first = me * rows_valid
    my_offset = lax.div(my_first, LANES)
    my_lead = pl.multiple_of(lax.rem(my_first, LANES), 8)
    places = (
        (own_pairs, me),
        (twin_pairs, twin),
        (across_pairs, lax.rem(me + 2, n)),
        (far_pairs, lax.rem(twin + 2, n)),
    )

    def state_copy(head):
        return pltpu.make_async_copy(state.at[head], state_out.at[head], state_sem.at[head])

    for head in range(heads):
        for plane, target in ((0, key_rows), (1, value_rows)):
            for pairs, source in places:
                start = pl.multiple_of(source * tok_rows, 16)
                target[head, pl.ds(start, tok_rows), :] = pairs[plane, head]
            target[head, pl.ds(window, step_count), :] = step_pairs[plane, head]
            spare = padded_keys - window - step_count
            if spare > 0:
                target[head, pl.ds(window + step_count, spare), :] = jnp.zeros(
                    (spare, LANES), target.dtype
                )
        chip_rows = 2 * tok_rows
        far = pl.multiple_of((1 - lax.div(me, 2)) * chip_rows, LANES)
        chip_chunks = chip_rows // LANES
        last = padded_keys - n * tok_rows

        def load_keys(chunk):
            first = far if chunk < chip_chunks else window - chip_rows
            return key_rows[head, pl.ds(first + chunk * LANES, LANES), :]

        values = jnp.concatenate(
            [value_rows[head, pl.ds(far, chip_rows), :], value_rows[head, pl.ds(window, last), :]]
        )
        state_blocks(
            load_keys,
            (chip_rows + last) // LANES,
            values,
            delta,
            keys_plain,
            keys_scaled,
            my_offset,
        )
        mine = pl.ds(my_lead, rows_valid)
        state[head] = prior[head].astype(jnp.float32) + part[head, mine, :] + delta[mine, :]
        state_copy(head).start()

    for head in range(heads):
        fill_tail(queries.at[head], steps[lax.div(me, 2), head], first_tail, tail)
        rows_out = result.shape[0] // heads
        for first in range(0, rows_out, TILE):
            last = first >= first_tail
            rows = tail[...] if last else queries[head, pl.ds(first, TILE), :]
            scores = lax.dot_general(
                rows, key_rows[head], CONTRACT_LAST, preferred_element_type=jnp.float32
            )
            position = rows_at(sizes, me, first)
            key_index = lax.broadcasted_iota(jnp.int32, scores.shape, 1)
            weights = jnp.where(position >= key_index * group, scores * scores, 0.0)
            total = jnp.dot(
                weights.astype(jnp.bfloat16), value_rows[head], preferred_element_type=jnp.float32
            )
            carried = local_tail[head] if last else local[head, pl.ds(first, TILE), :]
            size = min(TILE, rows_out - first)
            total = (total + carried) * rows_scale(sizes, counts, position)
            result[pl.ds(first * heads + head, size, stride=heads), :] = total[:size]
    for head in range(heads):
        state_copy(head).wait()


def pick_both_kernel(
    ids_ref, counts, query_table, pair_table, picked, origin, query_sem, pair_sem
):
    vocab_rows, group = query_table.shape[:2]
    first_row = lax.axis_index("ctx") * vocab_rows
    heads = pair_table.shape[1]
    picked[...] = jnp.zeros_like(picked)

    def each(step, act):
        row = ids_ref[step] - first_row

        @pl.when(jnp.logical_and(row >= 0, row < vocab_rows))
        def _():
            to_queries = picked.at[step, pl.ds(0, group)]
            to_pairs = picked.at[step, pl.ds(group, heads)]
            act(pltpu.make_async_copy(query_table.at[row], to_queries, query_sem.at[step]))
            act(pltpu.make_async_copy(pair_table.at[row], to_pairs, pair_sem.at[step]))

    for step in range(picked.shape[0]):
        each(step, lambda copy: copy.start())
    for step in range(picked.shape[0]):
        each(step, lambda copy: copy.wait())
    origin[...] = jnp.full(origin.shape, counts[0] + 1, jnp.int32).astype(jnp.float32)


def pick_both(ids, counts, query_table, pair_table):
    steps, group, heads = ids.shape[0], query_table.shape[1], pair_table.shape[1]
    shape = (steps, group + heads) + pair_table.shape[2:]
    return pl.pallas_call(
        pick_both_kernel,
        out_shape=(pltpu.VMEM(shape, pair_table.dtype), pltpu.VMEM((8, LANES), jnp.float32)),
        in_specs=[
            pl.BlockSpec(memory_space=pltpu.SMEM),
            pl.BlockSpec(memory_space=pltpu.SMEM),
            pl.BlockSpec(memory_space=pl.ANY),
            pl.BlockSpec(memory_space=pl.ANY),
        ],
        out_specs=(pl.BlockSpec(memory_space=pltpu.VMEM), pl.BlockSpec(memory_space=pltpu.VMEM)),
        scratch_shapes=[
            pltpu.SemaphoreType.DMA((steps,)),
            pltpu.SemaphoreType.DMA((steps,)),
        ],
        compiler_params=pltpu.CompilerParams(vmem_limit_bytes=56 * 2**20),
        name="pick_both",
    )(ids, counts, query_table, pair_table)


def vmem_call(kernel, out_shape, operands, scratch, limit, out_specs=None):
    vmem = pl.BlockSpec(memory_space=pltpu.VMEM)
    return pl.pallas_call(
        kernel,
        out_shape=out_shape,
        in_specs=[vmem] * len(operands),
        out_specs=out_specs if out_specs is not None else jax.tree.map(lambda _: vmem, out_shape),
        scratch_shapes=scratch,
        compiler_params=pltpu.CompilerParams(vmem_limit_bytes=limit * 2**20),
    )(*operands)


def turn_scratch(columns):
    chunks = columns // LANES
    return [
        pltpu.VMEM((chunks, LANES, LANES), jnp.float32),
        pltpu.VMEM((chunks, 2 * LANES, LANES), jnp.float32),
    ]


def on_device_exchange(
    queries, keys_values, prior, counts, continuation, query_table, pair_table
):
    tok_rows, heads, group, head_size = queries.shape
    n = lax.axis_size("ctx")
    step_count = continuation.shape[0]
    per_shard = step_count // n
    step_rows = per_shard * group
    rows_valid = prior.shape[1]
    window_rows = tok_rows * group
    early = window_rows // TILE * TILE
    rows_chip = 2 * rows_valid
    padded = max(
        round_up(chip_at * rows_chip % LANES + rows_chip, LANES) for chip_at in range(n // 2)
    )
    blocks = max(
        round_up(source * rows_valid % LANES + rows_valid, LANES) // LANES for source in range(n)
    )
    padded_keys = round_up(n * tok_rows + step_count, LANES)
    bf16, f32 = jnp.bfloat16, jnp.float32
    sizes = (n, heads, group, tok_rows, step_count, rows_valid)
    shape = jax.ShapeDtypeStruct

    def swap_across(value):
        return lax.ppermute(value, "ctx", [(i, (i + 2) % n) for i in range(n)])

    def swap_twin(value):
        return lax.ppermute(value, "ctx", [(i, i ^ 1) for i in range(n)])

    def query_planes(value):
        return value.transpose(1, 0, 2, 3).reshape(heads, -1, head_size)

    def pair_planes(value):
        return value.transpose(2, 1, 0, 3)

    across_queries = swap_across(queries)
    across_pairs = swap_across(keys_values)
    twin_prior = swap_twin(prior)
    twin_pairs = swap_twin(keys_values)
    picked, counts = pick_both(continuation, counts, query_table.transpose(0, 2, 1, 3), pair_table)
    twin_picked = swap_twin(picked)
    send = vmem_call(
        functools.partial(merge_kernel, n),
        shape((n // 2 * step_rows + step_count * heads, 2, head_size), bf16),
        (picked, twin_picked),
        [],
        4,
    )
    steps = send + swap_across(send)
    step_pairs = pair_planes(steps[n // 2 * step_rows :].reshape(step_count, heads, 2, head_size))
    step_queries = steps[: n // 2 * step_rows].reshape(n // 2, step_rows, heads, head_size)
    step_queries = step_queries.transpose(0, 2, 1, 3)

    own_rows = query_planes(queries)
    turned, local = vmem_call(
        functools.partial(early_kernel, rows_valid),
        (shape((heads, LANES, padded), bf16), shape((heads, early, LANES), f32)),
        (own_rows, prior, twin_prior),
        [pltpu.VMEM((padded, LANES), bf16)] + turn_scratch(early),
        16,
    )
    own_planes, twin_planes = pair_planes(keys_values), pair_planes(twin_pairs)
    chip_chunks = 2 * tok_rows // LANES
    part = vmem_call(
        functools.partial(part_kernel, sizes),
        shape((heads, blocks * LANES, LANES), f32),
        (own_planes, twin_planes),
        [
            pltpu.VMEM((2 * tok_rows, LANES), bf16),
            pltpu.VMEM((2 * tok_rows, LANES), bf16),
            pltpu.VMEM((chip_chunks, LANES, LANES), f32),
            pltpu.VMEM((chip_chunks, 2 * LANES, LANES), f32),
        ],
        16,
    )
    across_rows = query_planes(across_queries)
    half = (early // TILE + 1) // 2 * TILE
    partial = vmem_call(
        functools.partial(remote_kernel, sizes),
        shape((heads * half, LANES), bf16),
        (counts, across_rows, turned),
        [pltpu.VMEM((heads * half, LANES), f32)] + turn_scratch(half),
        16,
    )
    got = swap_across(partial)
    rest = heads * (window_rows + step_rows - half)
    partial_tail = vmem_call(
        functools.partial(remote_tail_kernel, sizes, half, early),
        shape((rest, LANES), bf16),
        (counts, across_rows, step_queries, turned),
        [pltpu.VMEM((TILE, LANES), bf16), pltpu.VMEM((rest, LANES), f32)]
        + turn_scratch(max(early - half, TILE)),
        16,
    )
    got_tail = swap_across(partial_tail)
    far_pairs = swap_twin(across_pairs)
    local_tail = vmem_call(
        functools.partial(own_tail_kernel, rows_valid, early),
        shape((heads, TILE, LANES), f32),
        (own_rows, step_queries, turned),
        [pltpu.VMEM((TILE, LANES), bf16)] + turn_scratch(TILE),
        16,
    )
    vmem = pl.BlockSpec(memory_space=pltpu.VMEM)
    chunks = (padded_keys - (n - 2) * tok_rows) // LANES
    result, decode_state = vmem_call(
        functools.partial(late_kernel, sizes),
        (
            shape((heads * (window_rows + step_rows), LANES), f32),
            shape((heads, rows_valid, LANES), f32),
        ),
        (
            counts,
            own_rows,
            step_queries,
            local_tail,
            local,
            own_planes,
            twin_planes,
            pair_planes(across_pairs),
            pair_planes(far_pairs),
            step_pairs,
            prior,
            part,
        ),
        [
            pltpu.VMEM((TILE, LANES), bf16),
            pltpu.VMEM((heads, padded_keys, LANES), bf16),
            pltpu.VMEM((heads, padded_keys, LANES), bf16),
            pltpu.VMEM((chunks, LANES, LANES), f32),
            pltpu.VMEM((chunks, 2 * LANES, LANES), f32),
            pltpu.VMEM((blocks * LANES, LANES), f32),
            pltpu.VMEM((heads, rows_valid, LANES), f32),
            pltpu.SemaphoreType.DMA((heads,)),
        ],
        24,
        (vmem, pl.BlockSpec(memory_space=pl.ANY)),
    )
    hbm = pl.BlockSpec(memory_space=pl.ANY)
    readout, decode_out = vmem_call(
        finish_kernel,
        (shape((heads * window_rows, LANES), bf16), shape((heads * step_rows, LANES), bf16)),
        (result, got, got_tail),
        [pltpu.VMEM(result.shape, bf16), pltpu.SemaphoreType.DMA((PIECES + 3,))],
        8,
        (hbm, hbm),
    )
    readout = readout.reshape(tok_rows, group, heads, head_size)
    decode_out = decode_out.reshape(per_shard, group, heads, head_size)
    return (readout.transpose(0, 2, 1, 3), decode_out.transpose(0, 2, 1, 3), decode_state)


def solution(mesh):
    in_specs = (
        P(("groups", "ctx"), "head", None, None),
        P(("groups", "ctx"), "head", None, None),
        P(("groups", "head"), "ctx", None),
        P("groups"),
        P("groups"),
        P("ctx", "head", None, None),
        P("ctx", "head", None, None),
    )
    out_specs = (
        P(("groups", "ctx"), "head", None, None),
        P(("groups", "ctx"), "head", None, None),
        P(("groups", "head"), "ctx", None),
    )

    def on_device(*arguments):
        n, rows_valid = lax.axis_size("ctx"), arguments[2].shape[1]
        if n == 4 and rows_valid % 16 == 0 and 2 * arguments[0].shape[0] % LANES == 0:
            return on_device_exchange(*arguments)
        return on_device_gather(*arguments)

    return jax.shard_map(
        on_device, mesh=mesh, in_specs=in_specs, out_specs=out_specs, check_vma=False
    )
```

```python
import functools

import jax
import jax.numpy as jnp
from jax import lax
from jax.experimental import pallas as pl
from jax.experimental.pallas import tpu as pltpu
from jax.sharding import PartitionSpec as P


ROOT_TWO = 2.0**0.5
MESH = pl.DeviceIdType.MESH
TILE = 256
LANES = 128
PIECES = 4
CONTRACT_LAST = (((1,), (1,)), ((), ()))


def round_up(number, multiple):
    return (number + multiple - 1) // multiple * multiple


def pick_kernel(ids_ref, query_table, pair_table, query_out, pair_out, query_sem, pair_sem):
    vocab_rows = query_table.shape[0]
    first_row = lax.axis_index("ctx") * vocab_rows
    query_out[...] = jnp.zeros_like(query_out)
    pair_out[...] = jnp.zeros_like(pair_out)

    def each(step, act):
        row = ids_ref[step] - first_row

        @pl.when(jnp.logical_and(row >= 0, row < vocab_rows))
        def _():
            act(pltpu.make_async_copy(query_table.at[row], query_out.at[step], query_sem.at[step]))
            act(pltpu.make_async_copy(pair_table.at[row], pair_out.at[step], pair_sem.at[step]))

    for step in range(query_out.shape[0]):
        each(step, lambda copy: copy.start())
    for step in range(query_out.shape[0]):
        each(step, lambda copy: copy.wait())


def pick_rows(ids, query_table, pair_table):
    steps = ids.shape[0]
    return pl.pallas_call(
        pick_kernel,
        out_shape=(
            jax.ShapeDtypeStruct((steps,) + query_table.shape[1:], query_table.dtype),
            jax.ShapeDtypeStruct((steps,) + pair_table.shape[1:], pair_table.dtype),
        ),
        in_specs=[
            pl.BlockSpec(memory_space=pltpu.SMEM),
            pl.BlockSpec(memory_space=pl.ANY),
            pl.BlockSpec(memory_space=pl.ANY),
        ],
        out_specs=(
            pl.BlockSpec(memory_space=pltpu.VMEM),
            pl.BlockSpec(memory_space=pltpu.VMEM),
        ),
        scratch_shapes=[pltpu.SemaphoreType.DMA((steps,)), pltpu.SemaphoreType.DMA((steps,))],
        name="pick_rows",
    )(ids, query_table, pair_table)


def main_kernel(
    sizes,
    counts,
    queries,
    blob,
    prior,
    window_out,
    step_out,
    state_out,
    out,
    state,
    land_blob,
    land_prior,
    query_rows,
    query_plain,
    query_scaled,
    prior_turned,
    total_turned,
    step_rows,
    key_rows,
    value_rows,
    turned,
    blob_send,
    blob_recv,
    prior_send,
    prior_recv,
    local_sem,
):
    n, heads, group, tok_rows, step_count, rows_valid = sizes
    chips = n // 2
    per_shard = step_count // n
    window_rows = tok_rows * group
    window = n * tok_rows
    prior_rows = prior.shape[1]
    shifted = prior_rows == rows_valid
    state_rows = state.shape[1]
    blocks = land_prior.shape[2] // LANES
    row_tiles = out.shape[1] // TILE
    padded_keys = key_rows.shape[1]
    me = lax.axis_index("ctx")
    core = lax.rem(me, 2)
    partner = me + 1 - 2 * core

    def across(step):
        return lax.rem(me + 2 * step, n)

    def twin(index):
        return index + 1 - 2 * lax.rem(index, 2)

    barrier = pltpu.get_barrier_semaphore()
    pl.semaphore_signal(barrier, inc=1, device_id={"ctx": partner}, device_id_type=MESH)
    for step in range(1, chips):
        pl.semaphore_signal(barrier, inc=1, device_id={"ctx": across(step)}, device_id_type=MESH)
    pl.semaphore_wait(barrier, chips)

    def blob_copy(src, source, slot, target):
        return pltpu.make_async_remote_copy(
            src_ref=src,
            dst_ref=land_blob.at[source],
            send_sem=blob_send.at[slot],
            recv_sem=blob_recv.at[source],
            device_id={"ctx": target},
            device_id_type=MESH,
        )

    def landing(source):
        first = pl.multiple_of(lax.rem(source * rows_valid, LANES), 16) if shifted else 0
        return pl.ds(first, prior_rows)

    def prior_copy(src, source, head, slot, target):
        return pltpu.make_async_remote_copy(
            src_ref=src,
            dst_ref=land_prior.at[source, head, landing(source)],
            send_sem=prior_send.at[slot, head],
            recv_sem=prior_recv.at[source, head],
            device_id={"ctx": target},
            device_id_type=MESH,
        )

    def blob_own(slot):
        return blob_copy(blob, me, slot, partner if slot == 0 else across(slot))

    def blob_forward(step):
        source = across(step)
        return blob_copy(land_blob.at[source], source, chips - 1 + step, partner)

    def prior_own(slot, head):
        target = partner if slot == 0 else across(slot)
        return prior_copy(prior.at[head], me, head, slot, target)

    def prior_forward(step, head):
        source = across(step)
        return prior_copy(
            land_prior.at[source, head, landing(source)],
            source,
            head,
            chips - 1 + step,
            partner,
        )

    for slot in list(range(1, chips)) + [0]:
        blob_own(slot).start()
    for head in range(heads):
        for slot in list(range(1, chips)) + [0]:
            prior_own(slot, head).start()
    own_blob = pltpu.make_async_copy(blob, land_blob.at[me], local_sem.at[0])
    own_prior = pltpu.make_async_copy(
        prior, land_prior.at[me, :, landing(me)], local_sem.at[1]
    )
    own_blob.start()
    own_prior.start()

    if shifted:
        for source in range(n):
            lead_rows = source * rows_valid % LANES
            for first, last in (
                (0, lead_rows),
                (lead_rows + prior_rows, blocks * LANES),
            ):
                if last > first:
                    for head in range(heads):
                        land_prior[source, head, pl.ds(first, last - first), :] = jnp.zeros(
                            (last - first, LANES), jnp.bfloat16
                        )
    total_turned[...] = jnp.zeros_like(total_turned)
    for head in range(heads):
        query_rows[head, pl.ds(0, window_rows), :] = queries[head]
        query_rows[head, pl.ds(window_rows, out.shape[1] - window_rows), :] = jnp.zeros(
            (out.shape[1] - window_rows, LANES), jnp.bfloat16
        )
        spare = padded_keys - window - step_count
        if spare > 0:
            key_rows[head, pl.ds(window + step_count, spare), :] = jnp.zeros(
                (spare, LANES), jnp.bfloat16
            )
            value_rows[head, pl.ds(window + step_count, spare), :] = jnp.zeros(
                (spare, LANES), jnp.bfloat16
            )

    def place(source):
        first = source * rows_valid
        return lax.div(first, LANES), lax.rem(first, LANES)

    identity = (
        lax.broadcasted_iota(jnp.int32, (LANES, LANES), 0)
        == lax.broadcasted_iota(jnp.int32, (LANES, LANES), 1)
    ).astype(jnp.bfloat16)
    contract_last = (((1,), (1,)), ((), ()))

    def transposed(rows):
        return lax.dot_general(identity, rows, contract_last, preferred_element_type=jnp.float32)

    chunks_per_tile = TILE // LANES

    def turn_queries(head, first_tile, last_tile):
        for chunk in range(first_tile * chunks_per_tile, last_tile * chunks_per_tile):
            piece = transposed(query_rows[head, pl.ds(chunk * LANES, LANES), :])
            scaled = piece * ROOT_TWO
            query_plain[head, chunk] = piece
            query_scaled[head, chunk, pl.ds(0, LANES), :] = scaled
            query_scaled[head, chunk, pl.ds(LANES, LANES), :] = scaled

    def carry_tile(source, head, tile):
        first_offset, _ = place(source)
        columns = []
        for side in range(chunks_per_tile):
            chunk = tile * chunks_per_tile + side
            here = query_plain[head, chunk]
            pieces = []
            for block in range(blocks):
                row = lax.rem(first_offset + block, LANES)
                other = query_scaled[head, chunk, pl.ds(row, LANES), :]
                if block == 0:
                    other = jnp.where(first_offset == 0, here, other)
                pieces.append((here * other).astype(jnp.bfloat16))
            columns.append(jnp.concatenate(pieces, axis=0))
        features = jnp.concatenate(columns, axis=1)
        total_turned[head, tile] += jnp.dot(
            prior_turned[...], features, preferred_element_type=jnp.float32
        )

    def carry(source, head, first_tile, last_tile):
        prior_turned[...] = transposed(land_prior[source, head]).astype(jnp.bfloat16)

        @pl.loop(first_tile, last_tile)
        def _(tile):
            carry_tile(source, head, tile)

    full_tiles = window_rows // TILE
    own_prior.wait()
    for head in range(heads):
        turn_queries(head, 0, full_tiles)
        carry(me, head, 0, full_tiles)

    own_blob.wait()
    blob_copy(blob, partner, 0, partner).wait_recv()
    for step in range(1, chips):
        blob_copy(blob, across(step), 0, partner).wait_recv()
        blob_forward(step).start()
    for step in range(1, chips):
        blob_copy(blob, twin(across(step)), 0, partner).wait_recv()

    for head in range(heads):
        for source in range(n):
            key_rows[head, pl.ds(source * tok_rows, tok_rows), :] = land_blob[
                source, head, pl.ds(0, tok_rows), :
            ]
            value_rows[head, pl.ds(source * tok_rows, tok_rows), :] = land_blob[
                source, heads + head, pl.ds(0, tok_rows), :
            ]

        def picked(plane, first, count):
            total = land_blob[0, plane, pl.ds(first, count), :].astype(jnp.float32)
            for source in range(1, n):
                total += land_blob[source, plane, pl.ds(first, count), :].astype(jnp.float32)
            return total

        key_rows[head, pl.ds(window, step_count), :] = picked(head, tok_rows, step_count).astype(
            jnp.bfloat16
        )
        value_rows[head, pl.ds(window, step_count), :] = picked(
            heads + head, tok_rows, step_count
        ).astype(jnp.bfloat16)
        half = step_count * group // 2
        for side in range(2):
            step_rows[head, pl.ds(side * half, half), :] = picked(
                2 * head + side, tok_rows + step_count, half
            )
        own_steps = per_shard * group
        own_rows = step_rows[head, pl.ds(me * own_steps, own_steps), :]
        query_rows[head, pl.ds(window_rows, own_steps), :] = own_rows.astype(jnp.bfloat16)
        turn_queries(head, full_tiles, row_tiles)

    for head in range(heads):
        carry(me, head, full_tiles, row_tiles)
        prior_copy(prior.at[head], partner, head, 0, partner).wait_recv()
        carry(partner, head, 0, row_tiles)

    def state_copy(head):
        return pltpu.make_async_copy(state.at[head], state_out.at[head], local_sem.at[2 + head])

    def positions(tile):
        local = tile * TILE + lax.broadcasted_iota(jnp.int32, (TILE, 1), 0)
        return jnp.where(
            local < window_rows,
            local + me * window_rows,
            local - window_rows + window * group + me * (per_shard * group),
        )

    first_offset, lead = place(me)
    for head in range(heads):
        keys_turned = transposed(key_rows[head])
        chunks = padded_keys // LANES
        for chunk in range(chunks):
            piece = keys_turned[:, chunk * LANES : (chunk + 1) * LANES]
            turned[head, chunk, pl.ds(0, LANES), :] = piece
            turned[head, chunk, pl.ds(LANES, LANES), :] = piece

        def state_block(block):
            row = lax.broadcasted_iota(jnp.int32, (LANES, LANES), 0)
            early = row < LANES - lead
            plain = jnp.logical_and(early, first_offset + block == 0)
            factor = jnp.where(plain, 1.0, ROOT_TWO)
            near_row = lax.rem(lead + first_offset + block, LANES)
            far_row = lax.rem(lead + first_offset + block + 1, LANES)
            pieces = []
            for chunk in range(chunks):
                here = turned[head, chunk, pl.ds(lead, LANES), :]
                near = turned[head, chunk, pl.ds(near_row, LANES), :]
                far = turned[head, chunk, pl.ds(far_row, LANES), :]
                both = jnp.where(early, near, far) * factor
                pieces.append((here * both).astype(jnp.bfloat16))
            features = jnp.concatenate(pieces, axis=1)
            return jnp.dot(features, value_rows[head], preferred_element_type=jnp.float32)

        def before(rows):
            return prior[head, rows, :].astype(jnp.float32) if shifted else 0.0

        whole_blocks = state_rows // LANES

        @pl.loop(0, whole_blocks)
        def _(block):
            rows = pl.ds(pl.multiple_of(block * LANES, LANES), LANES)
            state[head, rows, :] = before(rows) + state_block(block)

        rest = state_rows - whole_blocks * LANES
        if rest > 0:
            rows = pl.ds(whole_blocks * LANES, rest)
            state[head, rows, :] = before(rows) + state_block(whole_blocks)[:rest]
        state_copy(head).start()

        @pl.loop(0, row_tiles)
        def _(tile):
            rows = pl.ds(pl.multiple_of(tile * TILE, TILE), TILE)
            scores = lax.dot_general(
                query_rows[head, rows, :],
                key_rows[head],
                contract_last,
                preferred_element_type=jnp.float32,
            )
            position = positions(tile)
            key_index = lax.broadcasted_iota(jnp.int32, scores.shape, 1)
            allowed = position >= key_index * group
            weights = jnp.where(allowed, scores * scores, 0.0).astype(jnp.bfloat16)
            out[head, rows, :] = jnp.dot(
                weights, value_rows[head], preferred_element_type=jnp.float32
            )

    for step in range(1, chips):
        source = across(step)
        for head in range(heads):
            prior_copy(prior.at[head], source, head, 0, partner).wait_recv()
            prior_forward(step, head).start()
            carry(source, head, 0, row_tiles)
            prior_copy(prior.at[head], twin(source), head, 0, partner).wait_recv()
            carry(twin(source), head, 0, row_tiles)

    for head in range(heads):
        for tile in range(row_tiles):
            first = tile * TILE
            token = jnp.floor((positions(tile).astype(jnp.float32) + 0.5) / group)
            place_in_prompt = token + (counts[0] + 1).astype(jnp.float32)
            scale = 1.0 / (LANES * jnp.sqrt(place_in_prompt))
            total = out[head, pl.ds(first, TILE), :] + total_turned[head, tile].T
            total = (total * scale).astype(jnp.bfloat16)
            split = min(max(window_rows - first, 0), TILE)
            if split > 0:
                window_out[head, pl.ds(first, split), :] = total[:split]
            if split < TILE:
                step_out[head, pl.ds(first + split - window_rows, TILE - split), :] = total[split:]
        state_copy(head).wait()

    for slot in range(chips):
        blob_own(slot).wait_send()
        for head in range(heads):
            prior_own(slot, head).wait_send()
    for step in range(1, chips):
        blob_forward(step).wait_send()
        for head in range(heads):
            prior_forward(step, head).wait_send()


def combine(sizes, counts, queries, blob, prior, out_rows):
    n, heads, group, tok_rows, step_count, rows_valid = sizes
    window_rows = tok_rows * group
    lead = max(source * rows_valid % LANES for source in range(n))
    padded_rows = round_up(lead + rows_valid, LANES)
    chunks = out_rows // LANES
    state_rows = round_up(rows_valid, 8)
    padded_keys = round_up(n * tok_rows + step_count, LANES)
    slots = 2 * (n // 2) - 1
    vmem = pl.BlockSpec(memory_space=pltpu.VMEM)
    return pl.pallas_call(
        functools.partial(main_kernel, sizes),
        out_shape=(
            jax.ShapeDtypeStruct((heads, window_rows, LANES), jnp.bfloat16),
            jax.ShapeDtypeStruct((heads, out_rows - window_rows, LANES), jnp.bfloat16),
            jax.ShapeDtypeStruct((heads, state_rows, LANES), jnp.float32),
        ),
        in_specs=[pl.BlockSpec(memory_space=pltpu.SMEM)] + [vmem] * 3,
        out_specs=(vmem, vmem, pl.BlockSpec(memory_space=pl.ANY)),
        scratch_shapes=[
            pltpu.VMEM((heads, out_rows, LANES), jnp.float32),
            pltpu.VMEM((heads, state_rows, LANES), jnp.float32),
            pltpu.VMEM((n,) + blob.shape, jnp.bfloat16),
            pltpu.VMEM((n, heads, padded_rows, LANES), jnp.bfloat16),
            pltpu.VMEM((heads, out_rows, LANES), jnp.bfloat16),
            pltpu.VMEM((heads, chunks, LANES, LANES), jnp.float32),
            pltpu.VMEM((heads, chunks, 2 * LANES, LANES), jnp.float32),
            pltpu.VMEM((LANES, padded_rows), jnp.bfloat16),
            pltpu.VMEM((heads, out_rows // TILE, LANES, TILE), jnp.float32),
            pltpu.VMEM((heads, step_count * group, LANES), jnp.float32),
            pltpu.VMEM((heads, padded_keys, LANES), jnp.bfloat16),
            pltpu.VMEM((heads, padded_keys, LANES), jnp.bfloat16),
            pltpu.VMEM((heads, padded_keys // LANES, 2 * LANES, LANES), jnp.float32),
            pltpu.SemaphoreType.DMA((slots,)),
            pltpu.SemaphoreType.DMA((n,)),
            pltpu.SemaphoreType.DMA((slots, heads)),
            pltpu.SemaphoreType.DMA((n, heads)),
            pltpu.SemaphoreType.DMA((2 + heads,)),
        ],
        compiler_params=pltpu.CompilerParams(
            collective_id=0, has_side_effects=True, vmem_limit_bytes=48 * 2**20
        ),
        name="combine",
    )(counts, queries, blob, prior)


def on_device_gather(queries, keys_values, prior_state, counts, continuation, query_table, pair_table):
    tok_rows, heads, group, head_size = queries.shape
    n = lax.axis_size("ctx")
    shard_index = lax.axis_index("ctx")
    step_count = continuation.shape[0]
    per_shard = step_count // n
    rows_valid = prior_state.shape[1]

    query_pick, pair_pick = pick_rows(
        continuation, query_table.transpose(0, 2, 1, 3), pair_table
    )

    window_planes = keys_values.transpose(2, 1, 0, 3).reshape(2 * heads, tok_rows, head_size)
    step_planes = pair_pick.transpose(2, 1, 0, 3)
    step_planes = step_planes.reshape(2 * heads, step_count, head_size)
    query_planes = query_pick.transpose(2, 0, 1, 3).reshape(
        2 * heads, step_count * group // 2, head_size
    )
    blob = jnp.concatenate([window_planes, step_planes, query_planes], axis=1)
    query_planes = queries.transpose(1, 0, 2, 3).reshape(heads, tok_rows * group, head_size)
    prior = prior_state
    if rows_valid % 16 != 0:
        leads = [source * rows_valid % LANES for source in range(n)]
        prior = lax.dynamic_update_slice(
            jnp.zeros((heads, round_up(max(leads) + rows_valid, LANES), LANES), prior.dtype),
            prior_state,
            (0, shard_index * rows_valid % LANES, 0),
        )
    out_rows = round_up((tok_rows + per_shard) * group, TILE)
    sizes = (n, heads, group, tok_rows, step_count, rows_valid)
    window_out, step_out, state = combine(sizes, counts, query_planes, blob, prior, out_rows)

    decode_state = state
    if rows_valid % 16 != 0:
        decode_state = prior_state.astype(jnp.float32) + state[:, :rows_valid]
    readout = window_out.reshape(heads, tok_rows, group, head_size).transpose(1, 0, 2, 3)
    decode_out = step_out[:, : per_shard * group]
    decode_out = decode_out.reshape(heads, per_shard, group, head_size).transpose(1, 0, 2, 3)
    return (readout, decode_out, decode_state)


def identity():
    row = lax.broadcasted_iota(jnp.int32, (LANES, LANES), 0)
    column = lax.broadcasted_iota(jnp.int32, (LANES, LANES), 1)
    return (row == column).astype(jnp.bfloat16)


def turned_rows(rows):
    return lax.dot_general(
        identity(), rows, CONTRACT_LAST, preferred_element_type=jnp.float32
    )


def turn_queries(load, count, plain, scaled):
    for chunk in range(count // LANES):
        piece = turned_rows(load(chunk * LANES))
        twice = piece * ROOT_TWO
        plain[chunk] = piece
        scaled[chunk, pl.ds(0, LANES), :] = twice
        scaled[chunk, pl.ds(LANES, LANES), :] = twice


def carry_tile(state_turned, first_offset, plain, scaled, tile):
    blocks = state_turned.shape[1] // LANES
    columns = []
    for side in range(TILE // LANES):
        chunk = tile * (TILE // LANES) + side
        here = plain[chunk]
        pieces = []
        for block in range(blocks):
            other = scaled[chunk, pl.ds(first_offset + block, LANES), :]
            if block == 0:
                other = jnp.where(first_offset == 0, here, other)
            pieces.append((here * other).astype(jnp.bfloat16))
        columns.append(jnp.concatenate(pieces, axis=0))
    features = jnp.concatenate(columns, axis=1)
    return jnp.dot(state_turned[...], features, preferred_element_type=jnp.float32).T


def chip_place(rows_valid):
    first = lax.div(lax.axis_index("ctx"), 2) * (2 * rows_valid)
    return lax.div(first, LANES), pl.multiple_of(lax.rem(first, LANES), 16)


def early_kernel(rows_valid, queries, own, other, turned, local, rows, plain, scaled):
    heads, padded = turned.shape[0], turned.shape[2]
    first_offset, lead = chip_place(rows_valid)
    core = lax.rem(lax.axis_index("ctx"), 2)
    count = local.shape[1]
    for head in range(heads):
        rows[pl.ds(0, LANES), :] = jnp.zeros((LANES, LANES), rows.dtype)
        spare = padded - 2 * rows_valid
        rows[pl.ds(padded - spare, spare), :] = jnp.zeros((spare, LANES), rows.dtype)
        for source, index in ((own, core), (other, 1 - core)):
            start = pl.multiple_of(lead + index * rows_valid, 16)
            rows[pl.ds(start, rows_valid), :] = source[head]
        for first in range(0, padded, 2 * LANES):
            size = min(2 * LANES, padded - first)
            turned[head, :, pl.ds(first, size)] = turned_rows(
                rows[pl.ds(first, size), :]
            ).astype(turned.dtype)
        turn_queries(
            lambda at: queries[head, pl.ds(at, LANES), :], count, plain, scaled
        )
        for tile in range(count // TILE):
            local[head, pl.ds(tile * TILE, TILE), :] = carry_tile(
                turned.at[head], first_offset, plain, scaled, tile
            )


def fill_tail(queries, steps, first, tail):
    window = queries.shape[0] - first
    count = steps.shape[0]
    tail[...] = jnp.zeros_like(tail)
    tail[pl.ds(0, window), :] = queries[pl.ds(first, window), :]
    tail[pl.ds(window, count), :] = steps


def rows_at(sizes, who, first):
    n, _, group, tok_rows, step_count, _ = sizes
    window_rows = tok_rows * group
    at = first + lax.broadcasted_iota(jnp.int32, (TILE, 1), 0)
    return jnp.where(
        at < window_rows,
        at + who * window_rows,
        at + (n - 1) * window_rows + who * (step_count // n * group),
    )


def rows_scale(sizes, counts, position):
    token = jnp.floor((position.astype(jnp.float32) + 0.5) / sizes[2])
    place_in_prompt = token + counts[pl.ds(0, 1), pl.ds(0, 1)]
    return 1.0 / (LANES * jnp.sqrt(place_in_prompt))


def send_tile(sizes, counts, head, first, rows, mixed, base):
    n, heads = sizes[:2]
    across = lax.rem(lax.axis_index("ctx") + 2, n)
    rows = rows * rows_scale(sizes, counts, rows_at(sizes, across, first))
    size = min(TILE, mixed.shape[0] // heads - (first - base))
    mixed[pl.ds((first - base) * heads + head, size, stride=heads), :] = rows[:size]


def remote_kernel(sizes, counts, queries, turned, partial, mixed, plain, scaled):
    heads, rows_valid = sizes[1], sizes[5]
    first_offset, _ = chip_place(rows_valid)
    count = partial.shape[0] // heads
    for head in range(heads):
        turn_queries(
            lambda at: queries[head, pl.ds(at, LANES), :], count, plain, scaled
        )
        for tile in range(count // TILE):
            rows = carry_tile(turned.at[head], first_offset, plain, scaled, tile)
            send_tile(sizes, counts, head, tile * TILE, rows, mixed, 0)
    partial[...] = mixed[...].astype(partial.dtype)


def remote_tail_kernel(
    sizes, base, early, counts, queries, steps, turned, partial, tail, mixed, plain, scaled
):
    n, heads, rows_valid = sizes[0], sizes[1], sizes[5]
    first_offset, _ = chip_place(rows_valid)
    there = lax.div(lax.rem(lax.axis_index("ctx") + 2, n), 2)
    for head in range(heads):
        turn_queries(
            lambda at: queries[head, pl.ds(base + at, LANES), :], early - base, plain, scaled
        )
        for first in range(base, early, TILE):
            rows = carry_tile(
                turned.at[head], first_offset, plain, scaled, (first - base) // TILE
            )
            send_tile(sizes, counts, head, first, rows, mixed, base)
        fill_tail(queries.at[head], steps[there, head], early, tail)
        turn_queries(lambda at: tail[pl.ds(at, LANES), :], TILE, plain, scaled)
        rows = carry_tile(turned.at[head], first_offset, plain, scaled, 0)
        send_tile(sizes, counts, head, early, rows, mixed, base)
    partial[...] = mixed[...].astype(partial.dtype)


def merge_kernel(n, own, twin, send):
    core = lax.rem(lax.axis_index("ctx"), 2)
    step_count, rows, heads = own.shape[:3]
    group = rows - heads
    per_shard = step_count // n

    def both(step, first, count):
        at = (step, pl.ds(first, count))
        return own[at] + twin[at]

    for at in range(n // 2):
        for step in range(per_shard):
            row = (at * per_shard + step) * group
            send[pl.ds(row, group)] = both((core + 2 * at) * per_shard + step, 0, group)
    for step in range(step_count):
        row = n // 2 * per_shard * group + step * heads
        send[pl.ds(row, heads)] = both(step, group, heads)


def own_tail_kernel(rows_valid, early, queries, steps, turned, local, tail, plain, scaled):
    first_offset, _ = chip_place(rows_valid)
    here = lax.div(lax.axis_index("ctx"), 2)
    for head in range(turned.shape[0]):
        fill_tail(queries.at[head], steps[here, head], early, tail)
        turn_queries(lambda at: tail[pl.ds(at, LANES), :], TILE, plain, scaled)
        local[head] = carry_tile(turned.at[head], first_offset, plain, scaled, 0)


def add_out(result, got, first, window_out, step_out, total, sems):
    split = window_out.shape[0]
    stop = first + got.shape[0]
    piece = round_up(got.shape[0], 16 * PIECES) // PIECES
    cuts = sorted({*range(first, stop, piece), min(max(split, first), stop), stop})
    copies = []
    for start, last in zip(cuts, cuts[1:]):
        at = pl.ds(start - first, last - start)
        rows = result[pl.ds(start, last - start), :] + got[at, :].astype(jnp.float32)
        total[at, :] = rows.astype(total.dtype)
        target, base = (window_out, 0) if last <= split else (step_out, split)
        copy = pltpu.make_async_copy(
            total.at[at],
            target.at[pl.ds(start - base, last - start)],
            sems.at[len(copies)],
        )
        copy.start()
        copies.append(copy)
    for copy in copies:
        copy.wait()


def finish_kernel(result, got, window_out, total, sems):
    add_out(result, got, 0, window_out, None, total, sems)


def finish_tail_kernel(first, result, got, window_in, window_out, step_out, total, sems):
    add_out(result, got, first, window_out, step_out, total, sems)


def state_blocks(load_keys, chunks, values, delta, keys_plain, keys_scaled, my_offset):
    for chunk in range(chunks):
        piece = turned_rows(load_keys(chunk))
        twice = piece * ROOT_TWO
        keys_plain[chunk] = piece
        keys_scaled[chunk, pl.ds(0, LANES), :] = twice
        keys_scaled[chunk, pl.ds(LANES, LANES), :] = twice

    def key_features(block):
        pieces = []
        for chunk in range(chunks):
            here = keys_plain[chunk]
            other = keys_scaled[chunk, pl.ds(my_offset + block, LANES), :]
            if block == 0:
                other = jnp.where(my_offset == 0, here, other)
            pieces.append((here * other).astype(jnp.bfloat16))
        return jnp.concatenate(pieces, axis=1)

    for block in range(delta.shape[0] // LANES):
        delta[pl.ds(block * LANES, LANES), :] = jnp.dot(
            key_features(block), values, preferred_element_type=jnp.float32
        )


def part_kernel(sizes, own_pairs, twin_pairs, delta, keys, values, keys_plain, keys_scaled):
    heads, tok_rows, rows_valid = sizes[1], sizes[3], sizes[5]
    my_offset = lax.div(lax.axis_index("ctx") * rows_valid, LANES)
    for head in range(heads):
        for plane, target in ((0, keys), (1, values)):
            target[pl.ds(0, tok_rows), :] = own_pairs[plane, head]
            target[pl.ds(tok_rows, tok_rows), :] = twin_pairs[plane, head]
        state_blocks(
            lambda chunk: keys[pl.ds(chunk * LANES, LANES), :],
            keys.shape[0] // LANES,
            values[...],
            delta.at[head],
            keys_plain,
            keys_scaled,
            my_offset,
        )


def late_kernel(
    sizes,
    counts,
    queries,
    steps,
    local_tail,
    local,
    own_pairs,
    twin_pairs,
    across_pairs,
    far_pairs,
    step_pairs,
    prior,
    part,
    result,
    state_out,
    tail,
    key_rows,
    value_rows,
    keys_plain,
    keys_scaled,
    delta,
    state,
    state_sem,
):
    n, heads, group, tok_rows, step_count, rows_valid = sizes
    me = lax.axis_index("ctx")
    twin = me + 1 - 2 * lax.rem(me, 2)
    window = n * tok_rows
    first_tail = local.shape[1]
    padded_keys = key_rows.shape[1]
    my_first = me * rows_valid
    my_offset = lax.div(my_first, LANES)
    my_lead = pl.multiple_of(lax.rem(my_first, LANES), 8)
    places = (
        (own_pairs, me),
        (twin_pairs, twin),
        (across_pairs, lax.rem(me + 2, n)),
        (far_pairs, lax.rem(twin + 2, n)),
    )

    def state_copy(head):
        return pltpu.make_async_copy(state.at[head], state_out.at[head], state_sem.at[head])

    for head in range(heads):
        for plane, target in ((0, key_rows), (1, value_rows)):
            for pairs, source in places:
                start = pl.multiple_of(source * tok_rows, 16)
                target[head, pl.ds(start, tok_rows), :] = pairs[plane, head]
            target[head, pl.ds(window, step_count), :] = step_pairs[plane, head]
            spare = padded_keys - window - step_count
            if spare > 0:
                target[head, pl.ds(window + step_count, spare), :] = jnp.zeros(
                    (spare, LANES), target.dtype
                )
        chip_rows = 2 * tok_rows
        far = pl.multiple_of((1 - lax.div(me, 2)) * chip_rows, LANES)
        chip_chunks = chip_rows // LANES
        last = padded_keys - n * tok_rows

        def load_keys(chunk):
            first = far if chunk < chip_chunks else window - chip_rows
            return key_rows[head, pl.ds(first + chunk * LANES, LANES), :]

        values = jnp.concatenate(
            [value_rows[head, pl.ds(far, chip_rows), :], value_rows[head, pl.ds(window, last), :]]
        )
        state_blocks(
            load_keys,
            (chip_rows + last) // LANES,
            values,
            delta,
            keys_plain,
            keys_scaled,
            my_offset,
        )
        mine = pl.ds(my_lead, rows_valid)
        state[head] = prior[head].astype(jnp.float32) + part[head, mine, :] + delta[mine, :]
        state_copy(head).start()

    for head in range(heads):
        fill_tail(queries.at[head], steps[lax.div(me, 2), head], first_tail, tail)
        rows_out = result.shape[0] // heads
        for first in range(0, rows_out, TILE):
            last = first >= first_tail
            rows = tail[...] if last else queries[head, pl.ds(first, TILE), :]
            scores = lax.dot_general(
                rows, key_rows[head], CONTRACT_LAST, preferred_element_type=jnp.float32
            )
            position = rows_at(sizes, me, first)
            key_index = lax.broadcasted_iota(jnp.int32, scores.shape, 1)
            weights = jnp.where(position >= key_index * group, scores * scores, 0.0)
            total = jnp.dot(
                weights.astype(jnp.bfloat16), value_rows[head], preferred_element_type=jnp.float32
            )
            carried = local_tail[head] if last else local[head, pl.ds(first, TILE), :]
            size = min(TILE, rows_out - first)
            total = (total + carried) * rows_scale(sizes, counts, position)
            result[pl.ds(first * heads + head, size, stride=heads), :] = total[:size]
    for head in range(heads):
        state_copy(head).wait()


def pick_both_kernel(
    ids_ref, counts, query_table, pair_table, picked, origin, query_sem, pair_sem
):
    vocab_rows, group = query_table.shape[:2]
    first_row = lax.axis_index("ctx") * vocab_rows
    heads = pair_table.shape[1]
    picked[...] = jnp.zeros_like(picked)

    def each(step, act):
        row = ids_ref[step] - first_row

        @pl.when(jnp.logical_and(row >= 0, row < vocab_rows))
        def _():
            to_queries = picked.at[step, pl.ds(0, group)]
            to_pairs = picked.at[step, pl.ds(group, heads)]
            act(pltpu.make_async_copy(query_table.at[row], to_queries, query_sem.at[step]))
            act(pltpu.make_async_copy(pair_table.at[row], to_pairs, pair_sem.at[step]))

    for step in range(picked.shape[0]):
        each(step, lambda copy: copy.start())
    for step in range(picked.shape[0]):
        each(step, lambda copy: copy.wait())
    origin[...] = jnp.full(origin.shape, counts[0] + 1, jnp.int32).astype(jnp.float32)


def pick_both(ids, counts, query_table, pair_table):
    steps, group, heads = ids.shape[0], query_table.shape[1], pair_table.shape[1]
    shape = (steps, group + heads) + pair_table.shape[2:]
    return pl.pallas_call(
        pick_both_kernel,
        out_shape=(pltpu.VMEM(shape, pair_table.dtype), pltpu.VMEM((8, LANES), jnp.float32)),
        in_specs=[
            pl.BlockSpec(memory_space=pltpu.SMEM),
            pl.BlockSpec(memory_space=pltpu.SMEM),
            pl.BlockSpec(memory_space=pl.ANY),
            pl.BlockSpec(memory_space=pl.ANY),
        ],
        out_specs=(pl.BlockSpec(memory_space=pltpu.VMEM), pl.BlockSpec(memory_space=pltpu.VMEM)),
        scratch_shapes=[
            pltpu.SemaphoreType.DMA((steps,)),
            pltpu.SemaphoreType.DMA((steps,)),
        ],
        compiler_params=pltpu.CompilerParams(vmem_limit_bytes=56 * 2**20),
        name="pick_both",
    )(ids, counts, query_table, pair_table)


def vmem_call(kernel, out_shape, operands, scratch, limit, out_specs=None):
    vmem = pl.BlockSpec(memory_space=pltpu.VMEM)
    return pl.pallas_call(
        kernel,
        out_shape=out_shape,
        in_specs=[vmem] * len(operands),
        out_specs=out_specs if out_specs is not None else jax.tree.map(lambda _: vmem, out_shape),
        scratch_shapes=scratch,
        compiler_params=pltpu.CompilerParams(vmem_limit_bytes=limit * 2**20),
    )(*operands)


def turn_scratch(columns):
    chunks = columns // LANES
    return [
        pltpu.VMEM((chunks, LANES, LANES), jnp.float32),
        pltpu.VMEM((chunks, 2 * LANES, LANES), jnp.float32),
    ]


def on_device_exchange(
    queries, keys_values, prior, counts, continuation, query_table, pair_table
):
    tok_rows, heads, group, head_size = queries.shape
    n = lax.axis_size("ctx")
    step_count = continuation.shape[0]
    per_shard = step_count // n
    step_rows = per_shard * group
    rows_valid = prior.shape[1]
    window_rows = tok_rows * group
    early = window_rows // TILE * TILE
    rows_chip = 2 * rows_valid
    padded = max(
        round_up(chip_at * rows_chip % LANES + rows_chip, LANES) for chip_at in range(n // 2)
    )
    blocks = max(
        round_up(source * rows_valid % LANES + rows_valid, LANES) // LANES for source in range(n)
    )
    padded_keys = round_up(n * tok_rows + step_count, LANES)
    bf16, f32 = jnp.bfloat16, jnp.float32
    sizes = (n, heads, group, tok_rows, step_count, rows_valid)
    shape = jax.ShapeDtypeStruct

    def swap_across(value):
        return lax.ppermute(value, "ctx", [(i, (i + 2) % n) for i in range(n)])

    def swap_twin(value):
        return lax.ppermute(value, "ctx", [(i, i ^ 1) for i in range(n)])

    def query_planes(value):
        return value.transpose(1, 0, 2, 3).reshape(heads, -1, head_size)

    def pair_planes(value):
        return value.transpose(2, 1, 0, 3)

    across_queries = swap_across(queries)
    across_pairs = swap_across(keys_values)
    twin_prior = swap_twin(prior)
    twin_pairs = swap_twin(keys_values)
    picked, counts = pick_both(continuation, counts, query_table.transpose(0, 2, 1, 3), pair_table)
    twin_picked = swap_twin(picked)
    send = vmem_call(
        functools.partial(merge_kernel, n),
        shape((n // 2 * step_rows + step_count * heads, 2, head_size), bf16),
        (picked, twin_picked),
        [],
        4,
    )
    steps = send + swap_across(send)
    step_pairs = pair_planes(steps[n // 2 * step_rows :].reshape(step_count, heads, 2, head_size))
    step_queries = steps[: n // 2 * step_rows].reshape(n // 2, step_rows, heads, head_size)
    step_queries = step_queries.transpose(0, 2, 1, 3)

    own_rows = query_planes(queries)
    turned, local = vmem_call(
        functools.partial(early_kernel, rows_valid),
        (shape((heads, LANES, padded), bf16), shape((heads, early, LANES), f32)),
        (own_rows, prior, twin_prior),
        [pltpu.VMEM((padded, LANES), bf16)] + turn_scratch(early),
        16,
    )
    own_planes, twin_planes = pair_planes(keys_values), pair_planes(twin_pairs)
    chip_chunks = 2 * tok_rows // LANES
    part = vmem_call(
        functools.partial(part_kernel, sizes),
        shape((heads, blocks * LANES, LANES), f32),
        (own_planes, twin_planes),
        [
            pltpu.VMEM((2 * tok_rows, LANES), bf16),
            pltpu.VMEM((2 * tok_rows, LANES), bf16),
            pltpu.VMEM((chip_chunks, LANES, LANES), f32),
            pltpu.VMEM((chip_chunks, 2 * LANES, LANES), f32),
        ],
        16,
    )
    across_rows = query_planes(across_queries)
    half = (early // TILE + 1) // 2 * TILE
    partial = vmem_call(
        functools.partial(remote_kernel, sizes),
        shape((heads * half, LANES), bf16),
        (counts, across_rows, turned),
        [pltpu.VMEM((heads * half, LANES), f32)] + turn_scratch(half),
        16,
    )
    got = swap_across(partial)
    rest = heads * (window_rows + step_rows - half)
    partial_tail = vmem_call(
        functools.partial(remote_tail_kernel, sizes, half, early),
        shape((rest, LANES), bf16),
        (counts, across_rows, step_queries, turned),
        [pltpu.VMEM((TILE, LANES), bf16), pltpu.VMEM((rest, LANES), f32)]
        + turn_scratch(max(early - half, TILE)),
        16,
    )
    got_tail = swap_across(partial_tail)
    far_pairs = swap_twin(across_pairs)
    local_tail = vmem_call(
        functools.partial(own_tail_kernel, rows_valid, early),
        shape((heads, TILE, LANES), f32),
        (own_rows, step_queries, turned),
        [pltpu.VMEM((TILE, LANES), bf16)] + turn_scratch(TILE),
        16,
    )
    vmem = pl.BlockSpec(memory_space=pltpu.VMEM)
    chunks = (padded_keys - (n - 2) * tok_rows) // LANES
    result, decode_state = vmem_call(
        functools.partial(late_kernel, sizes),
        (
            shape((heads * (window_rows + step_rows), LANES), f32),
            shape((heads, rows_valid, LANES), f32),
        ),
        (
            counts,
            own_rows,
            step_queries,
            local_tail,
            local,
            own_planes,
            twin_planes,
            pair_planes(across_pairs),
            pair_planes(far_pairs),
            step_pairs,
            prior,
            part,
        ),
        [
            pltpu.VMEM((TILE, LANES), bf16),
            pltpu.VMEM((heads, padded_keys, LANES), bf16),
            pltpu.VMEM((heads, padded_keys, LANES), bf16),
            pltpu.VMEM((chunks, LANES, LANES), f32),
            pltpu.VMEM((chunks, 2 * LANES, LANES), f32),
            pltpu.VMEM((blocks * LANES, LANES), f32),
            pltpu.VMEM((heads, rows_valid, LANES), f32),
            pltpu.SemaphoreType.DMA((heads,)),
        ],
        24,
        (vmem, pl.BlockSpec(memory_space=pl.ANY)),
    )
    hbm = pl.BlockSpec(memory_space=pl.ANY)
    vmem = pl.BlockSpec(memory_space=pltpu.VMEM)
    window_shape = shape((heads * window_rows, LANES), bf16)
    sems = pltpu.SemaphoreType.DMA((PIECES + 2,))
    params = pltpu.CompilerParams(vmem_limit_bytes=8 * 2**20)
    readout = pl.pallas_call(
        finish_kernel,
        out_shape=window_shape,
        in_specs=[vmem, vmem],
        out_specs=hbm,
        scratch_shapes=[pltpu.VMEM(got.shape, bf16), sems],
        compiler_params=params,
        name="finish",
    )(result, got)
    readout, decode_out = pl.pallas_call(
        functools.partial(finish_tail_kernel, got.shape[0]),
        out_shape=(window_shape, shape((heads * step_rows, LANES), bf16)),
        in_specs=[vmem, vmem, hbm],
        out_specs=(hbm, hbm),
        scratch_shapes=[pltpu.VMEM(got_tail.shape, bf16), sems],
        input_output_aliases={2: 0},
        compiler_params=params,
        name="finishtail",
    )(result, got_tail, readout)
    readout = readout.reshape(tok_rows, group, heads, head_size)
    decode_out = decode_out.reshape(per_shard, group, heads, head_size)
    return (readout.transpose(0, 2, 1, 3), decode_out.transpose(0, 2, 1, 3), decode_state)


def solution(mesh):
    in_specs = (
        P(("groups", "ctx"), "head", None, None),
        P(("groups", "ctx"), "head", None, None),
        P(("groups", "head"), "ctx", None),
        P("groups"),
        P("groups"),
        P("ctx", "head", None, None),
        P("ctx", "head", None, None),
    )
    out_specs = (
        P(("groups", "ctx"), "head", None, None),
        P(("groups", "ctx"), "head", None, None),
        P(("groups", "head"), "ctx", None),
    )

    def on_device(*arguments):
        n, rows_valid = lax.axis_size("ctx"), arguments[2].shape[1]
        if n == 4 and rows_valid % 16 == 0 and 2 * arguments[0].shape[0] % LANES == 0:
            return on_device_exchange(*arguments)
        return on_device_gather(*arguments)

    return jax.shard_map(
        on_device, mesh=mesh, in_specs=in_specs, out_specs=out_specs, check_vma=False
    )
```
